32 devices in a mesh: dp: 16 (over z, x, core), mp: 2 (over y).
Axes of the slice: x: 2, y: 2, z: 4, core: 2. Of those that a mesh axis runs over, the one named last changes fastest.
Arguments:
- hidden: bfloat16 [16, 780, 1536], P('dp', 'mp'), may hold values from -6 to 6
- text_states: bfloat16 [16, 512, 1536], P('dp', 'mp'), may hold values from -6 to 6
- time_emb: float32 [16, 6, 1536], P('dp'), may hold values from -1.2 to 1.2
- lengths: int32 [16], replicated, may hold values from 702 to 780
- positions: int32 [16, 3, 780], P('dp'), may hold values from 0 to 38, as said below
- teacher: bfloat16 [16, 780, 1536], P('dp', 'mp'), may hold values from -14 to 14
- modulation: float32 [6, 1536], P(None, ('dp', 'mp')), may hold values from -0.9 to 0.9
- out_bias: float32 [4, 1536], P(None, ('dp', 'mp')), may hold values from -0.4 to 0.4
- norm3_gain: float32 [1536], P(('dp', 'mp')), may hold values from 0.5 to 1.5
- self_qkv: bfloat16 [3, 1536, 1536], P(None, 'dp', 'mp'), may hold values from -0.15625 to 0.15625
- self_out: bfloat16 [1536, 1536], P('mp', 'dp'), may hold values from -1 to 1
- cross_qkv: bfloat16 [3, 1536, 1536], P(None, 'dp', 'mp'), may hold values from -0.15625 to 0.15625
- cross_out: bfloat16 [1536, 1536], P('mp', 'dp'), may hold values from -0.875 to 0.875
- ffn_in: bfloat16 [1536, 8960], P('dp', 'mp'), may hold values from -0.15625 to 0.15625
- ffn_out: bfloat16 [8960, 1536], P('mp', 'dp'), may hold values from -0.0625 to 0.0625
- head_bias: bfloat16 [2, 3, 12, 128], P(None, None, 'mp', 'dp'), may hold values from -0.15917969 to 0.15917969
- qk_gain: bfloat16 [2, 2, 12, 128], P(None, None, 'mp', 'dp'), may hold values from 1.1484375 to 1.4453125
- ffn_bias: bfloat16 [70, 128], P('mp', 'dp'), may hold values from -2 to 2
Outputs:
- layer_out: bfloat16 [16, 780, 1536], P('dp', 'mp')
- mean_loss: float32 [], replicated
- hidden_grad: float32 [16, 780, 1536], P('dp', 'mp')
- text_grad: float32 [16, 512, 1536], P('dp', 'mp')
- modulation_grad: float32 [6, 1536], P(None, ('dp', 'mp'))
- out_bias_grad: float32 [4, 1536], P(None, ('dp', 'mp'))
- norm3_grad: float32 [1536], P(('dp', 'mp'))
- self_qkv_grad: float32 [3, 1536, 1536], P(None, 'dp', 'mp')
- self_out_grad: float32 [1536, 1536], P('mp', 'dp')
- cross_qkv_grad: float32 [3, 1536, 1536], P(None, 'dp', 'mp')
- cross_out_grad: float32 [1536, 1536], P('mp', 'dp')
- ffn_in_grad: float32 [1536, 8960], P('dp', 'mp')
- ffn_out_grad: float32 [8960, 1536], P('mp', 'dp')
- head_bias_grad: float32 [2, 3, 12, 128], P(None, None, 'mp', 'dp')
- qk_gain_grad: float32 [2, 2, 12, 128], P(None, None, 'mp', 'dp')
- ffn_bias_grad: float32 [70, 128], P('mp', 'dp')
The draws below stay inside these ranges and needn't reach their ends.
Inputs may be any that keep to these rules, and one draw needn't show every extreme that they name: The valid slots of clip c are its first lengths[c] slots; later slots are padding. `positions`: slot s of a clip holds frame s // (R W), row (s // W) mod R and column s mod W of a grid whose W (16 to 39) and R (8 to 19) are drawn for each clip; the first clip has W = 39.
All inputs are finite; a program needn't handle non-finite values.
Results may differ from the reference program's by a relative error of at most 0.025.
Values may be sent and summed in bfloat16 or wider, within the bound.
A program may use at most 320 MiB of HBM per device.

```python
import math
import jax
import jax.numpy as jnp
from jax import lax

D = 1536
HEADS = 12
HD = 128
FF = 8960
TXT = 512
LEN = 780
CLIPS = 16


def draw_positions(key, part):
    col_key = jax.random.fold_in(key, 11)
    row_key = jax.random.fold_in(key, 23)
    col_low = min(16, max(2, LEN // 4))
    col_high = min(39, LEN)
    row_low = min(8, max(2, LEN // 4))
    row_high = min(19, LEN)
    columns = jax.random.randint(col_key, (CLIPS, 1), col_low, col_high + 1)
    first_clip = jnp.arange(CLIPS, dtype=jnp.int32)[:, None] == 0
    columns = jnp.where(first_clip, col_high, columns)
    rows_per = jax.random.randint(row_key, (CLIPS, 1), row_low, row_high + 1)
    slots = jnp.arange(LEN, dtype=jnp.int32)[None, :]
    column = slots % columns
    row_index = slots // columns % rows_per
    frame = slots // (columns * rows_per)
    return jnp.stack([frame, row_index, column], axis=1).astype(jnp.int32)


def draw_teacher(key, part):
    clip_rank = jnp.arange(CLIPS, dtype=jnp.float32)[:, None, None] / max(CLIPS - 1, 1)
    base_draw = jax.random.truncated_normal(key, -4.0, 4.0, (CLIPS, LEN, D), jnp.float32)
    scale_vec = jnp.sqrt(1.0 + 11.0 * clip_rank)
    return (base_draw * scale_vec).astype(jnp.bfloat16)


def scaled_rows(key, shape_all, row_scales):
    base_draw = jax.random.truncated_normal(key, -3.0, 3.0, shape_all, jnp.float32)
    return base_draw * row_scales


def draw_modulation(key, part):
    row_scales = jnp.array([0.02, 0.3, 0.3, 0.02, 0.3, 0.3], jnp.float32)[:, None]
    return scaled_rows(jax.random.fold_in(key, 31), (6, D), row_scales).astype(jnp.float32)


def draw_time_emb(key, part):
    row_scales = jnp.array([0.02, 0.4, 0.4, 0.02, 0.4, 0.4], jnp.float32)[None, :, None]
    return scaled_rows(jax.random.fold_in(key, 37), (CLIPS, 6, D), row_scales).astype(jnp.float32)


def set_ends(drawn, stream_key, smallest, largest):
    longest = drawn.shape.index(max(drawn.shape))
    spots = []
    for shift in (0, 1):
        where = [jax.random.randint(jax.random.fold_in(stream_key, axis), (), 0, length) for axis, length in enumerate(drawn.shape)]
        where[longest] = (where[longest] + shift) % drawn.shape[longest]
        spots.append(tuple(where))
    return drawn.at[spots[0]].set(smallest).at[spots[1]].set(largest)


def block_scale(key, shape, cuts, low, high):
    def one(position, parts):
        draws = jax.random.uniform(jax.random.fold_in(jax.random.fold_in(key, 6), position), (parts,), jnp.float32, low / len(cuts), high / len(cuts))
        return jnp.repeat(jnp.exp(draws), shape[position] // parts).reshape((-1,) + (1,) * (len(shape) - position - 1))

    level = one(*cuts[0])
    for cut in cuts[1:]:
        level = level * one(*cut)
    return level


def bell_draw(own_key, shape, deviation, reach, cuts=(), kind=jnp.bfloat16):
    values = deviation * jax.random.normal(own_key, shape, jnp.float32)
    if cuts:
        values = values * block_scale(own_key, shape, cuts, -0.22, 0.18)
    return jnp.clip(values, -reach, reach).astype(kind)


def setup_inputs(seed: int = 0) -> dict:
    streams_of = jax.random.split(jax.random.key(seed), 19)
    return {
        "hidden": bell_draw(streams_of[0], (CLIPS, LEN, D), 1.0, 6.0, ((0, 16), (1, 2))),
        "text_states": bell_draw(streams_of[1], (CLIPS, TXT, D), 1.0, 6.0, ((0, 16), (1, 2))),
        "time_emb": draw_time_emb(jax.random.fold_in(streams_of[18], 71), 0),
        "lengths": set_ends(jax.random.randint(streams_of[3], (CLIPS,), LEN * 9 // 10, LEN + 1), jax.random.fold_in(streams_of[3], 1), LEN * 9 // 10, LEN).astype(jnp.int32),
        "positions": draw_positions(jax.random.fold_in(streams_of[18], 71), 0),
        "teacher": draw_teacher(jax.random.fold_in(streams_of[18], 71), 0),
        "modulation": draw_modulation(jax.random.fold_in(streams_of[18], 71), 0),
        "out_bias": bell_draw(streams_of[7], (4, D), 0.1, 0.4, ((1, 32),), jnp.float32),
        "norm3_gain": jnp.clip(1.0 + 0.1 * jax.random.normal(streams_of[8], (D,), jnp.float32), 0.5, 1.5),
        "self_qkv": bell_draw(streams_of[9], (3, D, D), D ** -0.5, 0.15625, ((1, 16), (2, 2))),
        "self_out": bell_draw(streams_of[10], (D, D), (min(D, max(D * 18 // LEN, 1))) ** -0.5, 1.0, ((0, 2), (1, 16))),
        "cross_qkv": bell_draw(streams_of[11], (3, D, D), D ** -0.5, 0.15625, ((1, 16), (2, 2))),
        "cross_out": bell_draw(streams_of[12], (D, D), (min(D, max(D * 18 // TXT, 1))) ** -0.5, 0.875, ((0, 2), (1, 16))),
        "ffn_in": bell_draw(streams_of[13], (D, FF), D ** -0.5, 0.15625, ((0, 16), (1, 2))),
        "ffn_out": bell_draw(streams_of[14], (FF, D), FF ** -0.5, 0.0625, ((0, 2), (1, 16))),
        "head_bias": bell_draw(streams_of[15], (2, 3, HEADS, HD), 0.04, 0.15917969, ((2, 2), (3, 16))),
        "qk_gain": jnp.clip(1.1484375 + 0.296875 * jax.random.uniform(streams_of[16], (2, 2, HEADS, HD), jnp.float32) ** block_scale(streams_of[16], (2, 2, HEADS, HD), ((2, 2), (3, 16)), -0.2, 0.2), 1.1484375, 1.4453125).astype(jnp.bfloat16),
        "ffn_bias": bell_draw(streams_of[17], (FF // 128, 128), 0.3, 2.0, ((0, 2), (1, 16))),
    }


HIGH = lax.Precision.HIGHEST
EPS = 1e-06

@jax.custom_vjp
def low(v):
    return lax.optimization_barrier(v.astype(jnp.bfloat16)).astype(jnp.float32)

@jax.custom_vjp
def low_back(v):
    return v

def low_keep(v):
    return (low(v), None)

def low_pass(kept, grad):
    return (grad,)

def back_keep(v):
    return (v, None)

def back_low(kept, grad):
    return (low(grad),)
low.defvjp(low_keep, low_pass)
low_back.defvjp(back_keep, back_low)

def rope_tables(positions):
    pair_count = HD // 2
    third_count = pair_count // 3
    counts = [pair_count - 2 * third_count, third_count, third_count]
    pieces = []
    for axis_id in range(3):
        rank_steps = jnp.arange(counts[axis_id], dtype=jnp.float32) / counts[axis_id]
        freq_rates = jnp.exp(-math.log(10000.0) * rank_steps)
        pieces.append(positions[axis_id].astype(jnp.float32)[:, None] * freq_rates[None, :])
    angles = jnp.repeat(jnp.concatenate(pieces, axis=1), 2, axis=1)
    return (jnp.cos(angles), jnp.sin(angles))

def pair_turn(values):
    next_value = jnp.roll(values, -1, axis=-1)
    prev_value = jnp.roll(values, 1, axis=-1)
    parity = jnp.arange(values.shape[-1]) % 2 == 0
    return jnp.where(parity, -next_value, prev_value)

def rotate(values, cosine, sine_table):
    return values * cosine + pair_turn(values) * sine_table

def layer_norm(values):
    center = values - lax.optimization_barrier(jnp.mean(values, axis=-1, keepdims=True))
    spread = lax.optimization_barrier(jnp.mean(center * center, axis=-1, keepdims=True))
    return center * lax.rsqrt(spread + EPS)

def modulate(values, shift_vec, scale_vec):
    return layer_norm(values) * (1.0 + scale_vec) + shift_vec

def rms_norm(values, gain_vec):
    return values * lax.rsqrt(lax.optimization_barrier(jnp.mean(values * values, axis=-1, keepdims=True)) + EPS) * gain_vec

def dense(left, right):
    return jnp.dot(left, right, precision=HIGH)

def attend(query_heads, key_heads, value_heads, key_valid):
    scores = low_back(jnp.einsum('qhd,khd->hqk', query_heads, key_heads, precision=HIGH) * HD ** (-0.5))
    scores = jnp.where(key_valid[None, None, :], scores, -1e+30)
    row_top = lax.optimization_barrier(jnp.max(scores, axis=-1, keepdims=True))
    weights = jnp.exp(scores - row_top)
    probabilities = weights / lax.optimization_barrier(jnp.sum(weights, axis=-1, keepdims=True))
    mixed_rows = jnp.einsum('hqk,khd->qhd', low(probabilities), value_heads, precision=HIGH)
    return low_back(low(mixed_rows))

def clip_layer(params, hidden_rows, text_rows, time_rows, clip_length, clip_positions, teacher_rows):
    modulation, out_bias, norm3_gain, self_qkv, self_out, cross_qkv, cross_out, ffn_in, ffn_out, head_bias, qk_gain, ffn_bias = params
    signals = modulation + time_rows
    cosine, sine_table = rope_tables(clip_positions)
    cosine = cosine[:, None, :]
    sine_table = sine_table[:, None, :]
    key_valid = jnp.arange(LEN) < clip_length
    attn_in = low(modulate(hidden_rows, signals[0], signals[1]))
    self_query_pre = low_back(dense(attn_in, self_qkv[0]) + head_bias[0, 0].reshape(-1))
    self_key_pre = low_back(dense(attn_in, self_qkv[1]) + head_bias[0, 1].reshape(-1))
    self_value = low_back(low(dense(attn_in, self_qkv[2]) + head_bias[0, 2].reshape(-1)))
    self_query = low(rotate(rms_norm(self_query_pre, qk_gain[0, 0].reshape(-1)).reshape(LEN, HEADS, HD), cosine, sine_table))
    self_key = low(rotate(rms_norm(self_key_pre, qk_gain[0, 1].reshape(-1)).reshape(LEN, HEADS, HD), cosine, sine_table))
    self_mixed = attend(self_query, self_key, self_value.reshape(LEN, HEADS, HD), key_valid).reshape(LEN, D)
    self_branch = low_back(dense(self_mixed, self_out) + out_bias[1])
    after_self = hidden_rows + signals[2] * self_branch
    cross_in = low(layer_norm(after_self) * norm3_gain + out_bias[0])
    cross_query_pre = low_back(dense(cross_in, cross_qkv[0]) + head_bias[1, 0].reshape(-1))
    cross_key_pre = low_back(dense(text_rows, cross_qkv[1]) + head_bias[1, 1].reshape(-1))
    cross_value = low_back(low(dense(text_rows, cross_qkv[2]) + head_bias[1, 2].reshape(-1)))
    cross_query = low(rms_norm(cross_query_pre, qk_gain[1, 0].reshape(-1)).reshape(LEN, HEADS, HD))
    cross_key = low(rms_norm(cross_key_pre, qk_gain[1, 1].reshape(-1)).reshape(TXT, HEADS, HD))
    text_valid = jnp.arange(TXT) < TXT
    cross_mixed = attend(cross_query, cross_key, cross_value.reshape(TXT, HEADS, HD), text_valid).reshape(LEN, D)
    cross_branch = low_back(dense(cross_mixed, cross_out) + out_bias[2])
    after_cross = after_self + cross_branch
    ffn_rows = low(modulate(after_cross, signals[3], signals[4]))
    inner_act = low_back(dense(ffn_rows, ffn_in) + ffn_bias.reshape(-1))
    activated = low(jax.nn.gelu(inner_act, approximate=True))
    ffn_branch = low_back(dense(activated, ffn_out) + out_bias[3])
    result = after_cross + signals[5] * ffn_branch
    row_valid = (jnp.arange(LEN) < clip_length).astype(jnp.float32)[:, None]
    error_rows = (result - teacher_rows) * row_valid
    return (result, jnp.sum(error_rows * error_rows))

def reference(hidden, text_states, time_emb, lengths, positions, teacher, modulation, out_bias, norm3_gain, self_qkv, self_out, cross_qkv, cross_out, ffn_in, ffn_out, head_bias, qk_gain, ffn_bias):
    params = tuple((item.astype(jnp.float32) for item in (modulation, out_bias, norm3_gain, self_qkv, self_out, cross_qkv, cross_out, ffn_in, ffn_out, head_bias, qk_gain, ffn_bias)))
    hidden_wide = hidden.astype(jnp.float32)
    text_wide = text_states.astype(jnp.float32)
    teacher_wide = teacher.astype(jnp.float32)

    def whole(param_set, hidden_set, text_set):

        def one_clip(items):
            clip_hidden, clip_text, clip_time, clip_length, clip_positions, clip_teacher = items
            return clip_layer(param_set, clip_hidden, clip_text, clip_time, clip_length, clip_positions, clip_teacher)
        results, squares = lax.map(jax.checkpoint(one_clip), (hidden_set, text_set, time_emb, lengths, positions, teacher_wide))
        return (results, jnp.sum(squares))
    (result, total), backward = jax.vjp(whole, params, hidden_wide, text_wide)
    grads, hidden_grad, text_grad = backward((jnp.zeros_like(result), jnp.float32(0.5)))
    valid_count = jnp.sum(lengths).astype(jnp.float32)
    mean_loss = total / (valid_count * D)
    return (result.astype(jnp.bfloat16), mean_loss, hidden_grad, text_grad, grads[0], grads[1], grads[2], grads[3], grads[4], grads[5], grads[6], grads[7], grads[8], grads[9], grads[10], grads[11])
```

```python
import functools
import math

import jax
import jax.numpy as jnp
import numpy as np
from jax import lax
from jax.experimental import pallas as pl
from jax.experimental.pallas import tpu as pltpu
from jax.sharding import PartitionSpec as P

D = 1536
HD = 128
EPS = 1e-06
SCALE = HD ** (-0.5)
BF = jnp.bfloat16
F32 = jnp.float32
NEG = -1e30
SWAP = [(0, 1), (1, 0)]
VMEM_BYTES = 48 * 1024 * 1024


def rope_rates():
    pair_count = HD // 2
    third = pair_count // 3
    counts = [pair_count - 2 * third, third, third]
    rates = np.zeros((3, HD), np.float32)
    start = 0
    for axis_id, count in enumerate(counts):
        steps = np.arange(count, dtype=np.float32) / np.float32(count)
        values = np.exp(np.float32(-math.log(10000.0)) * steps).astype(np.float32)
        rates[axis_id, 2 * start : 2 * (start + count)] = np.repeat(values, 2)
        start += count
    return rates


def dot_nn(a, b):
    return lax.dot_general(a, b, (((1,), (0,)), ((), ())), preferred_element_type=F32)


def dot_nt(a, b):
    return lax.dot_general(a, b, (((1,), (1,)), ((), ())), preferred_element_type=F32)


def dot_tn(a, b):
    return lax.dot_general(a, b, (((0,), (0,)), ((), ())), preferred_element_type=F32)


def cost(flops, nbytes, trans=0):
    return pl.CostEstimate(flops=int(flops), bytes_accessed=int(nbytes), transcendentals=int(trans))


def params():
    return pltpu.CompilerParams(vmem_limit_bytes=VMEM_BYTES)


def turn(values):
    lane = lax.broadcasted_iota(jnp.int32, values.shape, 1)
    after = pltpu.roll(values, HD - 1, 1)
    before = pltpu.roll(values, 1, 1)
    return jnp.where(lane % 2 == 0, after, before)


def prep_kernel(qp, kp, qs, ks, qg, kg, cos, sin, q_out, k_out):
    c = cos[...]
    s = sin[...]
    for pre, sq, gain, out in ((qp, qs, qg, q_out), (kp, ks, kg, k_out)):
        v = pre[...] * lax.rsqrt(sq[...] * (1.0 / D) + EPS) * gain[...]
        out[...] = (v * c + turn(v) * s).astype(BF)


def prep(qp, kp, qs, ks, qg, kg, cos, sin):
    rows, width = qp.shape
    head = pl.BlockSpec((rows, HD), lambda h: (0, h))
    col = pl.BlockSpec((rows, 1), lambda h: (0, 0))
    gain = pl.BlockSpec((1, HD), lambda h: (0, h))
    tab = pl.BlockSpec((rows, HD), lambda h: (0, 0))
    return pl.pallas_call(
        prep_kernel,
        grid=(width // HD,),
        in_specs=[head, head, col, col, gain, gain, tab, tab],
        out_specs=[head, head],
        out_shape=[jax.ShapeDtypeStruct((rows, width), BF)] * 2,
        compiler_params=params(),
        cost_estimate=cost(rows * width * 20, rows * width * 12),
        name="rope_prep",
    )(qp, kp, qs, ks, qg, kg, cos, sin)


def attend_kernel(masked, *refs):
    if masked:
        q, k, v, mask, out, lse = refs
    else:
        q, k, v, out, lse = refs
    st = dot_nt(k[...], q[...]) * SCALE
    if masked:
        st = st + mask[...]
    top = jnp.max(st, axis=0, keepdims=True)
    e = jnp.exp(st - top)
    total = jnp.sum(e, axis=0, keepdims=True)
    lse[0] = top + jnp.log(total)
    mixed = dot_tn(v[...], e.astype(BF)) * (1.0 / total)
    out[...] = mixed.T.astype(BF)


def attend(q, k, v, mask):
    nq, width = q.shape
    nk = k.shape[0]
    heads = width // HD
    qb = pl.BlockSpec((nq, HD), lambda h: (0, h))
    kb = pl.BlockSpec((nk, HD), lambda h: (0, h))
    ins = [qb, kb, kb]
    args = [q, k, v]
    if mask is not None:
        ins.append(pl.BlockSpec((nk, 1), lambda h: (0, 0)))
        args.append(mask)
    return pl.pallas_call(
        functools.partial(attend_kernel, mask is not None),
        grid=(heads,),
        in_specs=ins,
        out_specs=[qb, pl.BlockSpec((1, 1, nq), lambda h: (h, 0, 0))],
        out_shape=[
            jax.ShapeDtypeStruct((nq, width), BF),
            jax.ShapeDtypeStruct((heads, 1, nq), F32),
        ],
        compiler_params=params(),
        cost_estimate=cost(4 * nq * nk * width * 3, 4 * nq * width + 4 * nk * width, nq * nk * heads),
        name="attend_fwd",
    )(*args)


def attend_back_kernel(self_form, *refs):
    if self_form:
        (q, k, v, do, lse, mask, qp, kp, qs, ks, qg, kg, cos, sin,
         dq_out, dk_out, dv_out, qdot, kdot, qgain, kgain) = refs
    else:
        q, k, v, do, lse, qp, qs, qg, dq_out, dk_out, dv_out, qdot, qgain = refs
    st = dot_nt(k[...], q[...]) * SCALE
    if self_form:
        st = st + mask[...]
    p = jnp.exp(st - lse[0])
    dp = dot_nt(v[...], do[...])
    inner = jnp.sum(dp * p, axis=0, keepdims=True)
    ds = (p * (dp - inner)).astype(BF)
    dv_out[...] = dot_nn(p.astype(BF), do[...]).astype(dv_out.dtype)
    dk = dot_nn(ds, q[...]) * SCALE
    dq = dot_tn(k[...], ds).T * SCALE
    sides = [(dq, qp, qs, qg, dq_out, qdot, qgain)]
    if self_form:
        dq = dq * cos[...] - turn(dq) * sin[...]
        dk = dk * cos[...] - turn(dk) * sin[...]
        sides = [(dq, qp, qs, qg, dq_out, qdot, qgain), (dk, kp, ks, kg, dk_out, kdot, kgain)]
    else:
        dk_out[...] = dk
    for grad, pre, sq, gain, out, dots, gains in sides:
        p_rows = pre[...]
        weighted = grad * gain[...]
        out[...] = weighted
        part = jnp.sum(weighted * p_rows, axis=1, keepdims=True)

        @pl.when(pl.program_id(0) == 0)
        def _():
            dots[...] = part

        @pl.when(pl.program_id(0) > 0)
        def _():
            dots[...] += part

        scaled = p_rows * lax.rsqrt(sq[...] * (1.0 / D) + EPS)
        gains[...] = jnp.sum(grad * scaled, axis=0, keepdims=True)


def attend_back_self(q, k, v, do, lse, mask, qp, kp, qs, ks, qg, kg, cos, sin):
    n, width = q.shape
    heads = width // HD
    rows = pl.BlockSpec((n, HD), lambda h: (0, h))
    col = pl.BlockSpec((n, 1), lambda h: (0, 0))
    gain = pl.BlockSpec((1, HD), lambda h: (0, h))
    tab = pl.BlockSpec((n, HD), lambda h: (0, 0))
    lses = pl.BlockSpec((1, 1, n), lambda h: (h, 0, 0))
    full = jax.ShapeDtypeStruct((n, width), F32)
    cols = jax.ShapeDtypeStruct((n, 1), F32)
    gains = jax.ShapeDtypeStruct((1, width), F32)
    return pl.pallas_call(
        functools.partial(attend_back_kernel, True),
        grid=(heads,),
        in_specs=[rows, rows, rows, rows, lses, col, rows, rows, col, col, gain, gain, tab, tab],
        out_specs=[rows, rows, rows, col, col, gain, gain],
        out_shape=[full, full, jax.ShapeDtypeStruct((n, width), BF), cols, cols, gains, gains],
        compiler_params=params(),
        cost_estimate=cost(10 * n * n * width * 3, 26 * n * width, n * n * heads),
        name="attend_bwd_self",
    )(q, k, v, do, lse, mask, qp, kp, qs, ks, qg, kg, cos, sin)


def attend_back_cross(q, k, v, do, lse, qp, qs, qg):
    n, width = q.shape
    nk = k.shape[0]
    heads = width // HD
    rows = pl.BlockSpec((n, HD), lambda h: (0, h))
    keys = pl.BlockSpec((nk, HD), lambda h: (0, h))
    col = pl.BlockSpec((n, 1), lambda h: (0, 0))
    gain = pl.BlockSpec((1, HD), lambda h: (0, h))
    lses = pl.BlockSpec((1, 1, n), lambda h: (h, 0, 0))
    return pl.pallas_call(
        functools.partial(attend_back_kernel, False),
        grid=(heads,),
        in_specs=[rows, keys, keys, rows, lses, rows, col, gain],
        out_specs=[rows, keys, keys, col, gain],
        out_shape=[
            jax.ShapeDtypeStruct((n, width), F32),
            jax.ShapeDtypeStruct((nk, width), F32),
            jax.ShapeDtypeStruct((nk, width), F32),
            jax.ShapeDtypeStruct((n, 1), F32),
            jax.ShapeDtypeStruct((1, width), F32),
        ],
        compiler_params=params(),
        cost_estimate=cost(10 * n * nk * width * 3, 12 * n * width + 12 * nk * width, n * nk * heads),
        name="attend_bwd_cross",
    )(q, k, v, do, lse, qp, qs, qg)


def normal(values):
    center = values - jnp.mean(values, axis=-1, keepdims=True)
    scale = lax.rsqrt(jnp.mean(center * center, axis=-1, keepdims=True) + EPS)
    return center * scale, scale


def normal_back(grad, unit, scale):
    mean_g = jnp.mean(grad, axis=-1, keepdims=True)
    mean_gz = jnp.mean(grad * unit, axis=-1, keepdims=True)
    return scale * (grad - mean_g - unit * mean_gz)


def swap(values):
    return lax.ppermute(values, "mp", SWAP)


def collect(own):
    return jnp.concatenate([own, swap(own)], axis=0)


def spread(partial):
    half = partial.shape[0] // 2
    return partial[:half] + swap(partial[half:].astype(BF)).astype(F32)


def row_totals(own):
    half = own.shape[0] // 2
    return own + swap(jnp.concatenate([own[half:], own[:half]], axis=0))


def squares(values):
    return jnp.sum(values * values, axis=-1, keepdims=True)


def colsum(values):
    return jnp.sum(values, axis=0, dtype=F32)


def tie(*values):
    return lax.optimization_barrier(values)


def ring_order(chips):
    return list(range(0, chips, 2)) + list(range(chips - 1, 0, -2))


class Ring:
    def __init__(self, ndp, dp):
        self.chips = ndp // 2
        self.order = ring_order(self.chips)
        place = [self.order.index(i) for i in range(self.chips)]
        self.core = dp % 2
        self.place = jnp.asarray(place, jnp.int32)[dp // 2]
        self.way = 1 - 2 * self.core
        self.steps = []
        for i, chip in enumerate(self.order):
            after = self.order[(i + 1) % self.chips]
            self.steps.append((2 * chip, 2 * after))
            self.steps.append((2 * after + 1, 2 * chip + 1))
        self.pairs = [(i, i ^ 1) for i in range(ndp)]

    def chip_at(self, shift):
        spot = (self.place + self.way * shift) % self.chips
        return jnp.asarray(self.order, jnp.int32)[spot]

    def forward(self, values):
        return lax.ppermute(values, "dp", self.steps)

    def cross(self, values):
        return lax.ppermute(values, "dp", self.pairs)

    def gather(self, shard):
        k, r, n = shard.shape
        whole = jnp.zeros((k, 2 * self.chips, r, n), shard.dtype)
        piece = shard
        for step in range(self.chips):
            mine = 2 * self.chip_at(-step) + self.core
            theirs = 2 * self.chip_at(step) + 1 - self.core
            other = self.cross(piece)
            whole = lax.dynamic_update_slice(whole, piece[:, None], (0, mine, 0, 0))
            whole = lax.dynamic_update_slice(whole, other[:, None], (0, theirs, 0, 0))
            if step < self.chips - 1:
                piece = self.forward(piece)
        return whole

    def scatter_steps(self, full):
        k, rows, n = full.shape
        r = rows // (2 * self.chips)
        parts = full.astype(BF).reshape(k, self.chips, 2, r, n)
        mine = lax.dynamic_index_in_dim(parts, self.core, 2, False)
        theirs = lax.dynamic_index_in_dim(parts, 1 - self.core, 2, False)
        got = yield self.cross(theirs)
        total = None
        for step in range(self.chips):
            chip = self.chip_at(-1 - step)
            term = lax.dynamic_index_in_dim(mine, chip, 1, False).astype(F32)
            term = term + lax.dynamic_index_in_dim(got, chip, 1, False).astype(F32)
            total = term if total is None else total.astype(F32) + term
            if step < self.chips - 1:
                total = yield self.forward(total.astype(BF))
        yield total


class Steps:
    def __init__(self, ring, full):
        self.left = ring.chips
        self.work = ring.scatter_steps(full)
        self.piece = next(self.work)

    def step(self, *values):
        self.left -= 1
        *values, piece = tie(*values, self.piece)
        self.piece = self.work.send(piece)
        return values if len(values) > 1 else values[0]

    def finish(self):
        while self.left:
            self.left -= 1
            self.piece = self.work.send(self.piece)
        return self.piece


def partners(ndp, bit):
    return [(i, i ^ (1 << bit)) for i in range(ndp)]


def gather_small(flat, ndp, dp, mp):
    rows = flat[None]
    got = swap(rows)
    rows = jnp.where(mp == 0, jnp.concatenate([rows, got]), jnp.concatenate([got, rows]))
    for bit in range(ndp.bit_length() - 1):
        got = lax.ppermute(rows, "dp", partners(ndp, bit))
        low = (dp >> bit) % 2 == 0
        rows = jnp.where(low, jnp.concatenate([rows, got]), jnp.concatenate([got, rows]))
    return rows


def sum_small(values, ndp):
    for bit in range(ndp.bit_length() - 1):
        values = values + lax.ppermute(values, "dp", partners(ndp, bit))
    return values


def chunks_of(padded):
    first = (padded // 2 + 15) // 16 * 16
    return [(0, first), (first, padded)]


def local(
    hidden,
    text_states,
    time_emb,
    lengths,
    positions,
    teacher,
    modulation,
    out_bias,
    norm3_gain,
    self_qkv,
    self_out,
    cross_qkv,
    cross_out,
    ffn_in,
    ffn_out,
    head_bias,
    qk_gain,
    ffn_bias,
):
    ndp = lax.axis_size("dp")
    dp = lax.axis_index("dp")
    mp = lax.axis_index("mp")
    own_len = hidden.shape[1]
    length = 2 * own_len
    padded = (own_len + 15) // 16 * 16
    pad = padded - own_len
    cuts = chunks_of(padded)

    f32_part = jnp.concatenate([modulation, out_bias, norm3_gain[None]], axis=0)
    hb = head_bias.reshape(-1, head_bias.shape[-1])
    qg = qk_gain.reshape(-1, qk_gain.shape[-1])
    low_part = jnp.concatenate([hb, qg, ffn_bias], axis=0).astype(F32)
    n_f32, w_f32 = f32_part.shape
    n_low, w_low = low_part.shape
    flat = jnp.concatenate([f32_part.reshape(-1), low_part.reshape(-1)])
    n_flat = flat.shape[0]
    flat_all = gather_small(jnp.pad(flat, (0, -n_flat % 128)), ndp, dp, mp)[:, :n_flat]
    f32_all = flat_all[:, : n_f32 * w_f32].reshape(2 * ndp, n_f32, w_f32)
    f32_all = f32_all.transpose(1, 0, 2).reshape(n_f32, -1)
    low_all = flat_all[:, n_f32 * w_f32 :].reshape(ndp, 2, n_low, w_low)
    low_all = lax.dynamic_index_in_dim(low_all, mp, 1, False)
    low_all = low_all.transpose(1, 0, 2).reshape(n_low, -1)
    mod_full = f32_all[:6]
    out_bias_full = f32_all[6:10]
    norm3_full = f32_all[10]
    hb_full = low_all[: hb.shape[0]].reshape(2, 3, -1)
    qg_full = low_all[hb.shape[0] : hb.shape[0] + qg.shape[0]].reshape(2, 2, 1, -1)
    ffn_bias_full = low_all[hb.shape[0] + qg.shape[0] :].reshape(-1)

    ring = Ring(ndp, dp)
    def whole(shards):
        return lax.all_gather(shards, "dp", axis=1, tiled=True)

    heads_w = whole(jnp.concatenate([self_qkv, self_out.T[None], cross_qkv, cross_out.T[None]]))
    self_w = heads_w[:4]
    cross_w = heads_w[4:]
    ffn_w = whole(jnp.stack([ffn_in, ffn_out.T]))
    self_out_t = self_w[3]
    cross_out_t = cross_w[3]
    ffn_in_w = ffn_w[0]
    ffn_out_t = ffn_w[1]

    signals = mod_full + time_emb[0]
    shift_attn, scale_attn, gate_attn, shift_ffn, scale_ffn, gate_ffn = [
        signals[i : i + 1] for i in range(6)
    ]
    clip_length = lax.dynamic_index_in_dim(lengths, dp, 0, False)

    def own_chunks(array):
        full = jnp.pad(array, ((0, pad), (0, 0)))
        return [full[a:b] for a, b in cuts]

    hid = own_chunks(hidden[0])
    teach = own_chunks(teacher[0])
    index = jnp.arange(padded)
    pos_pad = jnp.pad(positions[0].reshape(3, 2, own_len), ((0, 0), (0, 0), (0, pad)))

    def both(own, other):
        return jnp.concatenate([x[a:b] for a, b in cuts for x in (own, other)], axis=0)

    def slot_valid(half):
        return (index < own_len) & (half * own_len + index < clip_length)

    own_valid = slot_valid(mp)
    key_valid = both(own_valid, slot_valid(1 - mp))
    key_mask = jnp.where(key_valid, 0.0, NEG).astype(F32)[:, None]
    row_valid = [own_valid.astype(F32)[a:b, None] for a, b in cuts]
    pos_own = lax.dynamic_index_in_dim(pos_pad, mp, 1, False)
    pos_other = lax.dynamic_index_in_dim(pos_pad, 1 - mp, 1, False)
    rates = rope_rates()
    angle = sum(
        both(pos_own[i], pos_other[i]).astype(F32)[:, None] * rates[i][None, :] for i in range(3)
    )
    even = np.arange(HD) % 2 == 0
    cos = jnp.cos(angle)
    sin = jnp.sin(angle) * np.where(even, -1.0, 1.0).astype(np.float32)
    ends = np.cumsum([0] + [2 * (b - a) for a, b in cuts])
    spans = [(int(ends[i]), int(ends[i + 1])) for i in range(len(cuts))]
    nc = len(cuts)

    text_rows = collect(text_states[0])
    cross_kp = dot_nn(text_rows, cross_w[1]) + hb_full[1, 1]
    cross_v = (dot_nn(text_rows, cross_w[2]) + hb_full[1, 2]).astype(BF)
    cross_ks = row_totals(squares(cross_kp))
    cross_kr = lax.rsqrt(cross_ks / D + EPS)
    cross_k = (cross_kp * cross_kr * qg_full[1, 1]).astype(BF)

    res0, unit0, scale0, rows0 = [], [], [], []
    qp, kp, vv, qs, ks = [], [], [], [], []
    for c in range(nc):
        r = hid[c].astype(F32)
        z, s = normal(r)
        x = (z * (1.0 + scale_attn) + shift_attn).astype(BF)
        rows = collect(x)
        qc = dot_nn(rows, self_w[0]) + hb_full[0, 0]
        kc = dot_nn(rows, self_w[1]) + hb_full[0, 1]
        vc = (dot_nn(rows, self_w[2]) + hb_full[0, 2]).astype(BF)
        tot = row_totals(jnp.concatenate([squares(qc), squares(kc)], axis=1))
        res0.append(r)
        unit0.append(z)
        scale0.append(s)
        rows0.append(rows)
        qp.append(qc)
        kp.append(kc)
        vv.append(vc)
        qs.append(tot[:, 0:1])
        ks.append(tot[:, 1:2])
    qp, kp, vv = [jnp.concatenate(x, axis=0) for x in (qp, kp, vv)]
    qs, ks = [jnp.concatenate(x, axis=0) for x in (qs, ks)]
    rows0 = jnp.concatenate(rows0, axis=0)
    self_q, self_k = prep(qp, kp, qs, ks, qg_full[0, 0], qg_full[0, 1], cos, sin)

    self_mixed, self_lse = [], []
    cross_mixed, cross_lse, cross_q, cross_qp, cross_qs = [], [], [], [], []
    rows1, rows2, branch0, unit1, scale1, unit2, scale2 = [], [], [], [], [], [], []
    acts, slopes, results, errors, d_ffn_all, grads2 = [], [], [], [], [], []
    gate_ffn_grad, err_sq = 0.0, 0.0
    for c in range(nc):
        a, b = spans[c]
        mixed, lse = attend(self_q[a:b], self_k, vv, key_mask)
        self_mixed.append(mixed)
        self_lse.append(lse)
        branch = spread(dot_nt(mixed, self_out_t)) + out_bias_full[1]
        after_self = res0[c] + gate_attn * branch
        branch0.append(branch)
        z, s = normal(after_self)
        unit1.append(z)
        scale1.append(s)
        rows = collect((z * norm3_full + out_bias_full[0]).astype(BF))
        rows1.append(rows)
        qc = dot_nn(rows, cross_w[0]) + hb_full[1, 0]
        tot = row_totals(squares(qc))
        qn = (qc * lax.rsqrt(tot / D + EPS) * qg_full[1, 0]).astype(BF)
        cross_qp.append(qc)
        cross_qs.append(tot)
        cross_q.append(qn)
        mixed, lse = attend(qn, cross_k, cross_v, None)
        cross_mixed.append(mixed)
        cross_lse.append(lse)
        after_cross = after_self + spread(dot_nt(mixed, cross_out_t)) + out_bias_full[2]
        z, s = normal(after_cross)
        unit2.append(z)
        scale2.append(s)
        rows = collect((z * (1.0 + scale_ffn) + shift_ffn).astype(BF))
        rows2.append(rows)
        inner = dot_nn(rows, ffn_in_w) + ffn_bias_full
        act, back = jax.vjp(functools.partial(jax.nn.gelu, approximate=True), inner)
        slope = back(jnp.ones_like(inner))[0]
        act = act.astype(BF)
        acts.append(act)
        slopes.append(slope.astype(BF))
        branch = spread(dot_nt(act, ffn_out_t)) + out_bias_full[3]
        result = after_cross + gate_ffn * branch
        results.append(result.astype(BF))
        error = (result - teach[c].astype(F32)) * row_valid[c]
        errors.append(error)
        err_sq = err_sq + jnp.sum(error * error)
        gate_ffn_grad = gate_ffn_grad + colsum(branch * error)
        d_ffn_all.append((gate_ffn * error).astype(BF))

    def cat(parts):
        return jnp.concatenate(parts, axis=0)

    bias3 = bias2 = bias0 = bias1 = shift2 = scale2_g = norm3_g = gate0_g = 0.0
    ffn_b_grad = cross_qb = cross_qgain = 0.0
    d_rows2, d_inners, d_rows1, d_qpres = [], [], [], []
    cross_dk = cross_dv = 0.0
    d_rows0, state, backs = [], [], []
    def reduce_rows(full):
        return lax.psum_scatter(full, "dp", scatter_dimension=1, tiled=True)

    for c in range(nc):
        bias3 = bias3 + colsum(d_ffn_all[c].astype(F32))
        d_rows2.append(collect(d_ffn_all[c]))
    g_out = dot_tn(cat(d_rows2), cat(acts)).astype(BF)
    d_rows2[-1], g_out = tie(d_rows2[-1], g_out)
    s_out = reduce_rows(g_out[None])
    for c in range(nc):
        rows = d_rows2[c]
        d_inner = (dot_nn(rows, ffn_out_t) * slopes[c].astype(F32)).astype(BF)
        d_inners.append(d_inner)
        ffn_b_grad = ffn_b_grad + colsum(d_inner.astype(F32))
        backs.append(spread(dot_nt(d_inner, ffn_in_w)))
    g_in = dot_tn(cat(rows2), cat(d_inners)).astype(BF)
    for c in range(nc):
        back = backs[c]
        shift2 = shift2 + colsum(back)
        scale2_g = scale2_g + colsum(back * unit2[c])
        d_after_cross = errors[c] + normal_back(back * (1.0 + scale_ffn), unit2[c], scale2[c])
        d_cross = d_after_cross.astype(BF)
        bias2 = bias2 + colsum(d_cross.astype(F32))
        rows = collect(d_cross)
        d_rows1.append(rows)
        d_mixed = dot_nn(rows, cross_out_t).astype(BF)
        if c == 0:
            d_mixed, g_in = tie(d_mixed, g_in)
        dqw, dk, dv, qdot, qgain = attend_back_cross(
            cross_q[c], cross_k, cross_v, d_mixed, cross_lse[c], cross_qp[c], cross_qs[c], qg_full[1, 0]
        )
        cross_dk = cross_dk + dk
        cross_dv = cross_dv + dv
        cross_qgain = cross_qgain + qgain[0]
        r = lax.rsqrt(cross_qs[c] / D + EPS)
        dot = row_totals(qdot)
        d_qpre = (dqw * r - cross_qp[c] * (r * r * r * dot / D)).astype(BF)
        d_qpres.append(d_qpre)
        cross_qb = cross_qb + colsum(d_qpre.astype(F32))
        back = spread(dot_nt(d_qpre, cross_w[0]))
        norm3_g = norm3_g + colsum(back * unit1[c])
        bias0 = bias0 + colsum(back)
        st = d_after_cross + normal_back(back * norm3_full, unit1[c], scale1[c])
        state.append(st)
        gate0_g = gate0_g + colsum(branch0[c] * st)
        d_self = (gate_attn * st).astype(BF)
        if c == nc - 1:
            d_self, s_out = tie(d_self, s_out)
            s_in = reduce_rows(g_in[None])
        bias1 = bias1 + colsum(d_self.astype(F32))
        d_rows0.append(collect(d_self))
    ffn_out_g = s_out[0].astype(F32).T

    cross_dkw = cross_dk * qg_full[1, 1]
    kdot = row_totals(jnp.sum(cross_dkw * cross_kp, axis=-1, keepdims=True))
    cross_kgain = colsum(cross_dk * cross_kp * cross_kr)
    d_kpre = (cross_dkw * cross_kr - cross_kp * (cross_kr**3 * kdot / D)).astype(BF)
    d_v = cross_dv.astype(BF)
    g_cross = jnp.stack(
        [
            dot_tn(cat(rows1), cat(d_qpres)).astype(BF),
            dot_tn(text_rows, d_kpre).astype(BF),
            dot_tn(text_rows, d_v).astype(BF),
            dot_tn(cat(d_rows1), cat(cross_mixed)).astype(BF),
        ]
    )
    text_g = spread(dot_nt(d_kpre, cross_w[1]) + dot_nt(d_v, cross_w[2]))
    cross_b = jnp.stack([cross_qb, colsum(d_kpre.astype(F32)), colsum(d_v.astype(F32))])

    d_rows0 = cat(d_rows0)
    d_mixed = dot_nn(d_rows0, self_out_t).astype(BF)
    g_self_out = dot_tn(d_rows0, cat(self_mixed)).astype(BF)
    d_mixed, g_self_out, g_cross = tie(d_mixed, g_self_out, g_cross)
    lse = jnp.concatenate(self_lse, axis=2)
    dqw, dkw, dv, qdot, kdot, self_qgain, self_kgain = attend_back_self(
        self_q, self_k, vv, d_mixed, lse, key_mask, qp, kp, qs, ks, qg_full[0, 0], qg_full[0, 1], cos, sin
    )
    dots = []
    for a, b in spans:
        dots.append(row_totals(jnp.concatenate([qdot[a:b], kdot[a:b]], axis=1)))
    g_vo = jnp.stack([dot_tn(rows0, dv).astype(BF), g_self_out])
    steps_vo = Steps(ring, g_vo)
    dots = steps_vo.step(cat(dots))
    rq = lax.rsqrt(qs / D + EPS)
    rk = lax.rsqrt(ks / D + EPS)
    d_q = (dqw * rq - qp * (rq**3 * dots[:, 0:1] / D)).astype(BF)
    d_k = (dkw * rk - kp * (rk**3 * dots[:, 1:2] / D)).astype(BF)
    d_q, d_k, s_in, g_cross = tie(d_q, d_k, s_in, g_cross)
    ffn_in_g = s_in[0].astype(F32)
    cross_g = reduce_rows(g_cross).astype(F32)
    cross_qkv_g = cross_g[:3]
    cross_out_g = cross_g[3].T
    backs = []
    for a, b in spans:
        backs.append(dot_nt(d_q[a:b], self_w[0]) + dot_nt(d_k[a:b], self_w[1]) + dot_nt(dv[a:b], self_w[2]))
    d_q, d_k, *backs = steps_vo.step(d_q, d_k, *backs)
    g_qk = jnp.stack([dot_tn(rows0, g).astype(BF) for g in (d_q, d_k)])
    backs = [spread(x) for x in backs]
    g_qk = steps_vo.step(g_qk)
    self_g = jnp.concatenate([Steps(ring, g_qk).finish(), steps_vo.finish()])
    self_qkv_g = self_g[:3]
    self_out_g = self_g[3].T
    self_b = jnp.stack([colsum(g.astype(F32)) for g in (d_q, d_k, dv)])
    shift0 = scale0_g = 0.0
    hidden_g = []
    for c in range(nc):
        back = backs[c]
        shift0 = shift0 + colsum(back)
        scale0_g = scale0_g + colsum(back * unit0[c])
        hidden_g.append(state[c] + normal_back(back * (1.0 + scale_attn), unit0[c], scale0[c]))

    wide = jnp.stack(
        [shift0, scale0_g, gate0_g, shift2, scale2_g, gate_ffn_grad, bias0, bias1, bias2, bias3, norm3_g]
        + [jnp.broadcast_to(err_sq, (D,))]
    )
    narrow = jnp.concatenate(
        [
            self_b.reshape(-1, HD),
            cross_b.reshape(-1, HD),
            jnp.stack([self_qgain[0], self_kgain[0], cross_qgain, cross_kgain]).reshape(-1, HD),
            ffn_b_grad.reshape(-1, HD),
        ],
        axis=0,
    )
    n_wide = wide.size // HD
    small = sum_small(jnp.concatenate([wide.reshape(-1, HD), narrow]), ndp)
    wide = (small[:n_wide] + swap(small[:n_wide])).reshape(-1, D)
    narrow = lax.dynamic_slice_in_dim(small[n_wide:], dp * w_low, w_low, 1)
    mine = lax.dynamic_slice_in_dim(wide, (dp * 2 + mp) * w_f32, w_f32, 1)
    mean_loss = wide[11, 0] / (jnp.sum(lengths).astype(F32) * D)
    nh = head_bias.size // head_bias.shape[-1]
    ng = qk_gain.size // qk_gain.shape[-1]
    return (
        cat(results)[None, :own_len],
        mean_loss,
        cat(hidden_g)[None, :own_len],
        text_g[None],
        mine[:6],
        mine[6:10],
        mine[10],
        self_qkv_g,
        self_out_g,
        cross_qkv_g,
        cross_out_g,
        ffn_in_g,
        ffn_out_g,
        narrow[:nh].reshape(head_bias.shape),
        narrow[nh : nh + ng].reshape(qk_gain.shape),
        narrow[nh + ng :].reshape(ffn_bias.shape),
    )


def solution(mesh):
    in_specs = (
        P("dp", "mp", None),
        P("dp", "mp", None),
        P("dp", None, None),
        P(),
        P("dp", None, None),
        P("dp", "mp", None),
        P(None, ("dp", "mp")),
        P(None, ("dp", "mp")),
        P(("dp", "mp")),
        P(None, "dp", "mp"),
        P("mp", "dp"),
        P(None, "dp", "mp"),
        P("mp", "dp"),
        P("dp", "mp"),
        P("mp", "dp"),
        P(None, None, "mp", "dp"),
        P(None, None, "mp", "dp"),
        P("mp", "dp"),
    )
    out_specs = (
        P("dp", "mp", None),
        P(),
        P("dp", "mp", None),
        P("dp", "mp", None),
        P(None, ("dp", "mp")),
        P(None, ("dp", "mp")),
        P(("dp", "mp")),
        P(None, "dp", "mp"),
        P("mp", "dp"),
        P(None, "dp", "mp"),
        P("mp", "dp"),
        P("dp", "mp"),
        P("mp", "dp"),
        P(None, None, "mp", "dp"),
        P(None, None, "mp", "dp"),
        P("mp", "dp"),
    )
    return jax.shard_map(local, mesh=mesh, in_specs=in_specs, out_specs=out_specs, check_vma=False)
```

```python
import functools
import math

import jax
import jax.numpy as jnp
import numpy as np
from jax import lax
from jax.experimental import pallas as pl
from jax.experimental.pallas import tpu as pltpu
from jax.sharding import PartitionSpec as P

D = 1536
HD = 128
EPS = 1e-06
SCALE = HD ** (-0.5)
BF = jnp.bfloat16
F32 = jnp.float32
NEG = -1e30
SWAP = [(0, 1), (1, 0)]
VMEM_BYTES = 48 * 1024 * 1024


def rope_rates():
    pair_count = HD // 2
    third = pair_count // 3
    counts = [pair_count - 2 * third, third, third]
    rates = np.zeros((3, HD), np.float32)
    start = 0
    for axis_id, count in enumerate(counts):
        steps = np.arange(count, dtype=np.float32) / np.float32(count)
        values = np.exp(np.float32(-math.log(10000.0)) * steps).astype(np.float32)
        rates[axis_id, 2 * start : 2 * (start + count)] = np.repeat(values, 2)
        start += count
    return rates


def dot_nn(a, b):
    return lax.dot_general(a, b, (((1,), (0,)), ((), ())), preferred_element_type=F32)


def dot_nt(a, b):
    return lax.dot_general(a, b, (((1,), (1,)), ((), ())), preferred_element_type=F32)


def dot_tn(a, b):
    return lax.dot_general(a, b, (((0,), (0,)), ((), ())), preferred_element_type=F32)


def cost(flops, nbytes, trans=0):
    return pl.CostEstimate(flops=int(flops), bytes_accessed=int(nbytes), transcendentals=int(trans))


def params():
    return pltpu.CompilerParams(vmem_limit_bytes=VMEM_BYTES)


def turn(values):
    lane = lax.broadcasted_iota(jnp.int32, values.shape, 1)
    after = pltpu.roll(values, HD - 1, 1)
    before = pltpu.roll(values, 1, 1)
    return jnp.where(lane % 2 == 0, after, before)


def prep_kernel(qp, kp, qs, ks, qg, kg, cos, sin, q_out, k_out):
    c = cos[...]
    s = sin[...]
    for pre, sq, gain, out in ((qp, qs, qg, q_out), (kp, ks, kg, k_out)):
        v = pre[...] * lax.rsqrt(sq[...] * (1.0 / D) + EPS) * gain[...]
        out[...] = (v * c + turn(v) * s).astype(BF)


def prep(qp, kp, qs, ks, qg, kg, cos, sin):
    rows, width = qp.shape
    head = pl.BlockSpec((rows, HD), lambda h: (0, h))
    col = pl.BlockSpec((rows, 1), lambda h: (0, 0))
    gain = pl.BlockSpec((1, HD), lambda h: (0, h))
    tab = pl.BlockSpec((rows, HD), lambda h: (0, 0))
    return pl.pallas_call(
        prep_kernel,
        grid=(width // HD,),
        in_specs=[head, head, col, col, gain, gain, tab, tab],
        out_specs=[head, head],
        out_shape=[jax.ShapeDtypeStruct((rows, width), BF)] * 2,
        compiler_params=params(),
        cost_estimate=cost(rows * width * 20, rows * width * 12),
        name="rope_prep",
    )(qp, kp, qs, ks, qg, kg, cos, sin)


def attend_kernel(masked, *refs):
    if masked:
        q, k, v, mask, out, lse = refs
    else:
        q, k, v, out, lse = refs
    st = dot_nt(k[...], q[...]) * SCALE
    if masked:
        st = st + mask[...]
    top = jnp.max(st, axis=0, keepdims=True)
    e = jnp.exp(st - top)
    total = jnp.sum(e, axis=0, keepdims=True)
    lse[0] = top + jnp.log(total)
    mixed = dot_tn(v[...], e.astype(BF)) * (1.0 / total)
    out[...] = mixed.T.astype(BF)


def attend(q, k, v, mask):
    nq, width = q.shape
    nk = k.shape[0]
    heads = width // HD
    qb = pl.BlockSpec((nq, HD), lambda h: (0, h))
    kb = pl.BlockSpec((nk, HD), lambda h: (0, h))
    ins = [qb, kb, kb]
    args = [q, k, v]
    if mask is not None:
        ins.append(pl.BlockSpec((nk, 1), lambda h: (0, 0)))
        args.append(mask)
    return pl.pallas_call(
        functools.partial(attend_kernel, mask is not None),
        grid=(heads,),
        in_specs=ins,
        out_specs=[qb, pl.BlockSpec((1, 1, nq), lambda h: (h, 0, 0))],
        out_shape=[
            jax.ShapeDtypeStruct((nq, width), BF),
            jax.ShapeDtypeStruct((heads, 1, nq), F32),
        ],
        compiler_params=params(),
        cost_estimate=cost(4 * nq * nk * width * 3, 4 * nq * width + 4 * nk * width, nq * nk * heads),
        name="attend_fwd",
    )(*args)


def attend_back_kernel(self_form, *refs):
    if self_form:
        (q, k, v, do, lse, mask, qp, kp, qs, ks, qg, kg, cos, sin,
         dq_out, dk_out, dv_out, qdot, kdot, qgain, kgain) = refs
    else:
        q, k, v, do, lse, qp, qs, qg, dq_out, dk_out, dv_out, qdot, qgain = refs
    st = dot_nt(k[...], q[...]) * SCALE
    if self_form:
        st = st + mask[...]
    p = jnp.exp(st - lse[0])
    dp = dot_nt(v[...], do[...])
    inner = jnp.sum(dp * p, axis=0, keepdims=True)
    ds = (p * (dp - inner)).astype(BF)
    dv_out[...] = dot_nn(p.astype(BF), do[...]).astype(dv_out.dtype)
    dk = dot_nn(ds, q[...]) * SCALE
    dq = dot_tn(k[...], ds).T * SCALE
    sides = [(dq, qp, qs, qg, dq_out, qdot, qgain)]
    if self_form:
        dq = dq * cos[...] - turn(dq) * sin[...]
        dk = dk * cos[...] - turn(dk) * sin[...]
        sides = [(dq, qp, qs, qg, dq_out, qdot, qgain), (dk, kp, ks, kg, dk_out, kdot, kgain)]
    else:
        dk_out[...] = dk
    for grad, pre, sq, gain, out, dots, gains in sides:
        p_rows = pre[...]
        weighted = grad * gain[...]
        out[...] = weighted
        part = jnp.sum(weighted * p_rows, axis=1, keepdims=True)

        @pl.when(pl.program_id(0) == 0)
        def _():
            dots[...] = part

        @pl.when(pl.program_id(0) > 0)
        def _():
            dots[...] += part

        scaled = p_rows * lax.rsqrt(sq[...] * (1.0 / D) + EPS)
        gains[...] = jnp.sum(grad * scaled, axis=0, keepdims=True)


def attend_back_self(q, k, v, do, lse, mask, qp, kp, qs, ks, qg, kg, cos, sin):
    n, width = q.shape
    heads = width // HD
    rows = pl.BlockSpec((n, HD), lambda h: (0, h))
    col = pl.BlockSpec((n, 1), lambda h: (0, 0))
    gain = pl.BlockSpec((1, HD), lambda h: (0, h))
    tab = pl.BlockSpec((n, HD), lambda h: (0, 0))
    lses = pl.BlockSpec((1, 1, n), lambda h: (h, 0, 0))
    full = jax.ShapeDtypeStruct((n, width), F32)
    cols = jax.ShapeDtypeStruct((n, 1), F32)
    gains = jax.ShapeDtypeStruct((1, width), F32)
    return pl.pallas_call(
        functools.partial(attend_back_kernel, True),
        grid=(heads,),
        in_specs=[rows, rows, rows, rows, lses, col, rows, rows, col, col, gain, gain, tab, tab],
        out_specs=[rows, rows, rows, col, col, gain, gain],
        out_shape=[full, full, jax.ShapeDtypeStruct((n, width), BF), cols, cols, gains, gains],
        compiler_params=params(),
        cost_estimate=cost(10 * n * n * width * 3, 26 * n * width, n * n * heads),
        name="attend_bwd_self",
    )(q, k, v, do, lse, mask, qp, kp, qs, ks, qg, kg, cos, sin)


def attend_back_cross(q, k, v, do, lse, qp, qs, qg):
    n, width = q.shape
    nk = k.shape[0]
    heads = width // HD
    rows = pl.BlockSpec((n, HD), lambda h: (0, h))
    keys = pl.BlockSpec((nk, HD), lambda h: (0, h))
    col = pl.BlockSpec((n, 1), lambda h: (0, 0))
    gain = pl.BlockSpec((1, HD), lambda h: (0, h))
    lses = pl.BlockSpec((1, 1, n), lambda h: (h, 0, 0))
    return pl.pallas_call(
        functools.partial(attend_back_kernel, False),
        grid=(heads,),
        in_specs=[rows, keys, keys, rows, lses, rows, col, gain],
        out_specs=[rows, keys, keys, col, gain],
        out_shape=[
            jax.ShapeDtypeStruct((n, width), F32),
            jax.ShapeDtypeStruct((nk, width), F32),
            jax.ShapeDtypeStruct((nk, width), F32),
            jax.ShapeDtypeStruct((n, 1), F32),
            jax.ShapeDtypeStruct((1, width), F32),
        ],
        compiler_params=params(),
        cost_estimate=cost(10 * n * nk * width * 3, 12 * n * width + 12 * nk * width, n * nk * heads),
        name="attend_bwd_cross",
    )(q, k, v, do, lse, qp, qs, qg)


def head_grads_kernel(plan, *refs):
    out = refs[-1]
    for i, terms in enumerate(plan):

        @pl.when(pl.program_id(0) == i)
        def _(terms=terms):
            total = None
            for a, b, lo, hi in terms:
                term = dot_tn(refs[a][...], refs[b][lo:hi])
                total = term if total is None else total + term
            out[0] = total.astype(BF)


def self_back_kernel(spans, *refs):
    n = 2 * len(spans)
    rows = refs[:n]
    weights = refs[n]
    heads = refs[n + 1 : n + 4]
    grads, part, other, acc = refs[n + 4 :]
    halves = [x for a, b in spans for x in ((a, (a + b) // 2), ((a + b) // 2, b))]
    for i in range(3):

        @pl.when(pl.program_id(0) == i)
        def _(i=i):
            total = None
            for x, (a, b) in zip(rows, halves):
                term = dot_tn(x[...], heads[i][a:b])
                total = term if total is None else total + term
            grads[0] = total.astype(BF)
            back = dot_nt(heads[i][...], weights[0])
            if i == 0:
                acc[...] = back
            elif i == 1:
                acc[...] += back
            else:
                back = acc[...] + back
                at = 0
                for a, b in spans:
                    half = (b - a) // 2
                    part[at : at + half] = back[a : a + half]
                    other[at : at + half] = back[a + half : b].astype(BF)
                    at += half


def self_back(rows, spans, weights, heads):
    n, width = heads[0].shape
    d = rows[0].shape[1]
    once = lambda x: pl.BlockSpec(x.shape, lambda i: (0, 0), pipeline_mode=pl.Buffered(1))
    return pl.pallas_call(
        functools.partial(self_back_kernel, spans),
        grid=(3,),
        in_specs=[once(x) for x in rows]
        + [pl.BlockSpec((1, d, width), lambda i: (i, 0, 0))]
        + [once(x) for x in heads],
        out_specs=[
            pl.BlockSpec((1, d, width), lambda i: (i, 0, 0)),
            pl.BlockSpec((n // 2, d), lambda i: (0, 0)),
            pl.BlockSpec((n // 2, d), lambda i: (0, 0)),
        ],
        out_shape=[
            jax.ShapeDtypeStruct((3, d, width), BF),
            jax.ShapeDtypeStruct((n // 2, d), F32),
            jax.ShapeDtypeStruct((n // 2, d), BF),
        ],
        scratch_shapes=[pltpu.VMEM((n, d), F32)],
        compiler_params=params(),
        cost_estimate=cost(12 * n * d * width, 30e6),
        name="self_back",
    )(*rows, weights, *heads)


def head_grads(products):
    arrays, plan = [], []

    def place(x):
        for i, y in enumerate(arrays):
            if x is y:
                return i
        arrays.append(x)
        return len(arrays) - 1

    for pairs in products:
        terms = []
        for pieces, b in pairs:
            at = 0
            for a in pieces:
                terms.append((place(a), place(b), at, at + a.shape[0]))
                at += a.shape[0]
        plan.append(terms)
    m, n = products[0][0][0][0].shape[1], products[0][0][1].shape[1]
    rows = sum(b.shape[0] for pairs in products for _, b in pairs)
    return pl.pallas_call(
        functools.partial(head_grads_kernel, plan),
        grid=(len(products),),
        in_specs=[
            pl.BlockSpec(x.shape, lambda i: (0, 0), pipeline_mode=pl.Buffered(1)) for x in arrays
        ],
        out_specs=pl.BlockSpec((1, m, n), lambda i: (i, 0, 0)),
        out_shape=jax.ShapeDtypeStruct((len(products), m, n), BF),
        compiler_params=params(),
        cost_estimate=cost(2 * rows * m * n, 2 * sum(x.size for x in arrays) + 2 * len(products) * m * n),
        name="head_grads",
    )(*arrays)


def tail_kernel(ndp, counts, nc, *refs):
    n = len(counts)
    g = refs[:n]
    state = refs[n : n + nc]
    unit = refs[n + nc : n + 2 * nc]
    (part, other, lns, ones, small, gsum, hgrad, small_out,
     mine, got, send, slot, ybuf, pbuf, stbuf, ubuf, vals, inbox,
     mine_sem, got_send, got_recv, ring_send, ring_recv, y_sem, load_sem, sum_send, sum_recv) = refs[n + 2 * nc :]
    chips = ndp // 2
    bits = ndp.bit_length() - 1
    dp = lax.axis_index("dp")
    mp = lax.axis_index("mp")
    core = lax.rem(dp, 2)
    chip = lax.div(dp, 2)
    odd = lax.rem(chip, 2)
    row = lax.div(chip, 2)
    place = row * (1 - odd) + (chips - 1 - row) * odd
    way = 1 - 2 * core

    def chip_at(shift):
        spot = lax.rem(place + way * shift + 2 * chips, chips)
        back = lax.div(spot, chips // 2)
        return 2 * spot * (1 - back) + (2 * (chips - 1 - spot) + 1) * back

    after = 2 * chip_at(1) + core
    before = 2 * chip_at(-1) + core
    mates = [dp + (1 - 2 * lax.rem(lax.div(dp, 1 << b), 2)) * (1 << b) for b in range(bits)]
    mesh_id = pl.DeviceIdType.MESH

    barrier = pltpu.get_barrier_semaphore()
    for device in (after, before, *mates):
        pl.semaphore_signal(barrier, inc=1, device_id=(device, mp), device_id_type=mesh_id)
    pl.semaphore_signal(barrier, inc=1, device_id=(dp, 1 - mp), device_id_type=mesh_id)
    pl.semaphore_wait(barrier, 3 + bits)

    def remote(src, dst, s_sem, r_sem, device):
        return pltpu.make_async_remote_copy(
            src_ref=src, dst_ref=dst, send_sem=s_sem, recv_sem=r_sem, device_id=device, device_id_type=mesh_id
        )

    starts = [sum(counts[:i]) for i in range(n)]
    total = sum(counts)
    cuts = [(0, (total + 1) // 2), ((total + 1) // 2, total)]

    def to_mate(s, i):
        return remote(
            g[i].at[:, chip_at(1 + s), 1 - core],
            got.at[s, pl.ds(starts[i], counts[i])],
            got_send.at[i, s],
            got_recv.at[i, s],
            (mates[0], mp),
        )

    def to_self(s, i):
        return pltpu.make_async_copy(
            g[i].at[:, chip_at(-1 - s), core], mine.at[s, pl.ds(starts[i], counts[i])], mine_sem.at[i, s]
        )

    def along(s, half):
        lo, hi = cuts[half]
        return remote(
            send.at[s, pl.ds(lo, hi - lo)],
            slot.at[s, pl.ds(lo, hi - lo)],
            ring_send.at[half, s],
            ring_recv.at[half, s],
            (after, mp),
        )

    def sum_copy(j):
        if j < bits:
            return remote(vals.at[j], inbox.at[j], sum_send.at[j], sum_recv.at[j], (mates[j], mp))
        return remote(
            vals.at[j, pl.ds(0, 16)], inbox.at[j, pl.ds(0, 16)], sum_send.at[j], sum_recv.at[j], (dp, 1 - mp)
        )

    y_copy = remote(other, ybuf, y_sem.at[0], y_sem.at[1], (dp, 1 - mp))
    for s in range(chips):
        for i in range(n):
            to_mate(s, i).start()
            to_self(s, i).start()
        if s == 0:
            y_copy.start()
    pairs = [(part, pbuf)]
    at = 0
    for st, un in zip(state, unit):
        span = pl.ds(at, st.shape[0])
        pairs += [(st, stbuf.at[span]), (un, ubuf.at[span])]
        at += st.shape[0]
    loads = [pltpu.make_async_copy(src, dst, load_sem.at[i]) for i, (src, dst) in enumerate(pairs)]
    for load in loads:
        load.start()

    def finish_rows():
        for load in loads:
            load.wait()
        y_copy.wait_recv()
        rows, width = pbuf.shape
        block = 80 if rows % 80 == 0 else 16
        gain = ones[...]

        def body(i, sums):
            at = pl.ds(pl.multiple_of(i * block, block), block)
            back = pbuf[at, :] + ybuf[at, :].astype(F32)
            z = ubuf[at, :]
            grad = back * gain
            mean_g = jnp.mean(grad, axis=1, keepdims=True)
            mean_gz = jnp.mean(grad * z, axis=1, keepdims=True)
            hgrad[at, :] = stbuf[at, :] + lns[at, :] * (grad - mean_g - z * mean_gz)
            return (
                sums[0] + jnp.sum(back, axis=0, keepdims=True),
                sums[1] + jnp.sum(back * z, axis=0, keepdims=True),
            )

        zero = jnp.zeros((1, width), F32)
        sums = lax.fori_loop(0, rows // block, body, (zero, zero))
        vals[0] = small[...]
        vals[0, 0:1, :] = sums[0]
        vals[0, 1:2, :] = sums[1]
        sum_copy(0).start()

    def sum_step(j):
        sum_copy(j).wait_recv()
        if j < bits:
            vals[j + 1] = vals[j] + inbox[j]
            sum_copy(j + 1).start()
        else:
            small_out[...] = vals[j]
            small_out[0:16, :] = vals[j, 0:16, :] + inbox[j, 0:16, :]

    first = min(2, chips - 1)
    done = 0
    for s in range(chips):
        for i in range(n):
            to_self(s, i).wait()
            to_mate(s, i).wait_recv()
        for half in range(2):
            lo, hi = cuts[half]
            value = mine[s, lo:hi].astype(F32) + got[s, lo:hi].astype(F32)
            if s > 0:
                along(s - 1, half).wait_recv()
                value = value + slot[s - 1, lo:hi].astype(F32)
            if s < chips - 1:
                send[s, lo:hi] = value.astype(BF)
                along(s, half).start()
            else:
                gsum[lo:hi] = value
        if s == first:
            finish_rows()
        elif s > first and done <= bits:
            sum_step(done)
            done += 1
    while done <= bits:
        sum_step(done)
        done += 1
    for s in range(chips):
        for i in range(n):
            to_mate(s, i).wait_send()
        if s < chips - 1:
            for half in range(2):
                along(s, half).wait_send()
    y_copy.wait_send()
    for j in range(bits + 1):
        sum_copy(j).wait_send()


def tail(ndp, grads, part, other, state, unit, lns, ones, small):
    chips = ndp // 2
    bits = ndp.bit_length() - 1
    split = [x.reshape(x.shape[0], chips, 2, x.shape[1] // ndp, x.shape[2]) for x in grads]
    counts = tuple(x.shape[0] for x in grads)
    total = sum(counts)
    r, w = split[0].shape[3:]
    rows, width = part.shape
    n = len(grads)
    nc = len(state)
    hbm = pl.BlockSpec(memory_space=pl.ANY)
    vmem = pl.BlockSpec(memory_space=pltpu.VMEM)
    dma = pltpu.SemaphoreType.DMA
    return pl.pallas_call(
        functools.partial(tail_kernel, ndp, counts, nc),
        in_specs=[hbm] * (n + 2 * nc) + [hbm, hbm, vmem, vmem, vmem],
        out_specs=[vmem] * 3,
        out_shape=[
            jax.ShapeDtypeStruct((total, r, w), F32),
            jax.ShapeDtypeStruct((rows, width), F32),
            jax.ShapeDtypeStruct(small.shape, F32),
        ],
        scratch_shapes=[
            pltpu.VMEM((chips, total, r, w), BF),
            pltpu.VMEM((chips, total, r, w), BF),
            pltpu.VMEM((chips - 1, total, r, w), BF),
            pltpu.VMEM((chips - 1, total, r, w), BF),
            pltpu.VMEM((rows, width), BF),
            pltpu.VMEM((rows, width), F32),
            pltpu.VMEM((rows, width), F32),
            pltpu.VMEM((rows, width), F32),
            pltpu.VMEM((bits + 1,) + small.shape, F32),
            pltpu.VMEM((bits + 1,) + small.shape, F32),
            dma((n, chips)),
            dma((n, chips)),
            dma((n, chips)),
            dma((2, chips - 1)),
            dma((2, chips - 1)),
            dma((2,)),
            dma((1 + 2 * nc,)),
            dma((bits + 1,)),
            dma((bits + 1,)),
        ],
        compiler_params=pltpu.CompilerParams(
            vmem_limit_bytes=58 * 1024 * 1024, collective_id=0, has_side_effects=True
        ),
        cost_estimate=cost(1e6, 1e6),
        name="tail_sums",
    )(*split, *state, *unit, part, other, lns, ones, small)


def normal(values):
    center = values - jnp.mean(values, axis=-1, keepdims=True)
    scale = lax.rsqrt(jnp.mean(center * center, axis=-1, keepdims=True) + EPS)
    return center * scale, scale


def normal_back(grad, unit, scale):
    mean_g = jnp.mean(grad, axis=-1, keepdims=True)
    mean_gz = jnp.mean(grad * unit, axis=-1, keepdims=True)
    return scale * (grad - mean_g - unit * mean_gz)


def swap(values):
    return lax.ppermute(values, "mp", SWAP)


def collect(own):
    pieces = [own, swap(own)]
    return jnp.concatenate(pieces, axis=0), pieces


def spread(partial):
    half = partial.shape[0] // 2
    return partial[:half] + swap(partial[half:].astype(BF)).astype(F32)


def row_totals(own):
    half = own.shape[0] // 2
    return own + swap(jnp.concatenate([own[half:], own[:half]], axis=0))


def squares(values):
    return jnp.sum(values * values, axis=-1, keepdims=True)


def colsum(values):
    return jnp.sum(values, axis=0, dtype=F32)


def tie(*values):
    return lax.optimization_barrier(values)


def partners(ndp, bit):
    return [(i, i ^ (1 << bit)) for i in range(ndp)]


def gather_small(flat, ndp, dp, mp):
    rows = flat[None]
    got = swap(rows)
    rows = jnp.where(mp == 0, jnp.concatenate([rows, got]), jnp.concatenate([got, rows]))
    for bit in range(ndp.bit_length() - 1):
        got = lax.ppermute(rows, "dp", partners(ndp, bit))
        low = (dp >> bit) % 2 == 0
        rows = jnp.where(low, jnp.concatenate([rows, got]), jnp.concatenate([got, rows]))
    return rows


def chunks_of(padded):
    first = (padded // 2 + 15) // 16 * 16
    return [(0, first), (first, padded)]


def local(
    hidden,
    text_states,
    time_emb,
    lengths,
    positions,
    teacher,
    modulation,
    out_bias,
    norm3_gain,
    self_qkv,
    self_out,
    cross_qkv,
    cross_out,
    ffn_in,
    ffn_out,
    head_bias,
    qk_gain,
    ffn_bias,
):
    ndp = lax.axis_size("dp")
    dp = lax.axis_index("dp")
    mp = lax.axis_index("mp")
    own_len = hidden.shape[1]
    length = 2 * own_len
    padded = (own_len + 15) // 16 * 16
    pad = padded - own_len
    cuts = chunks_of(padded)

    f32_part = jnp.concatenate([modulation, out_bias, norm3_gain[None]], axis=0)
    hb = head_bias.reshape(-1, head_bias.shape[-1])
    qg = qk_gain.reshape(-1, qk_gain.shape[-1])
    low_part = jnp.concatenate([hb, qg, ffn_bias], axis=0).astype(F32)
    n_f32, w_f32 = f32_part.shape
    n_low, w_low = low_part.shape
    flat = jnp.concatenate([f32_part.reshape(-1), low_part.reshape(-1)])
    n_flat = flat.shape[0]
    flat_all = gather_small(jnp.pad(flat, (0, -n_flat % 128)), ndp, dp, mp)[:, :n_flat]
    f32_all = flat_all[:, : n_f32 * w_f32].reshape(2 * ndp, n_f32, w_f32)
    f32_all = f32_all.transpose(1, 0, 2).reshape(n_f32, -1)
    low_all = flat_all[:, n_f32 * w_f32 :].reshape(ndp, 2, n_low, w_low)
    low_all = lax.dynamic_index_in_dim(low_all, mp, 1, False)
    low_all = low_all.transpose(1, 0, 2).reshape(n_low, -1)
    mod_full = f32_all[:6]
    out_bias_full = f32_all[6:10]
    norm3_full = f32_all[10]
    hb_full = low_all[: hb.shape[0]].reshape(2, 3, -1)
    qg_full = low_all[hb.shape[0] : hb.shape[0] + qg.shape[0]].reshape(2, 2, 1, -1)
    ffn_bias_full = low_all[hb.shape[0] + qg.shape[0] :].reshape(-1)

    def whole(shards):
        return lax.all_gather(shards, "dp", axis=1, tiled=True)

    heads_w = whole(jnp.concatenate([self_qkv, self_out.T[None], cross_qkv, cross_out.T[None]]))
    self_w = heads_w[:4]
    cross_w = heads_w[4:]
    ffn_w = whole(jnp.stack([ffn_in, ffn_out.T]))
    self_out_t = self_w[3]
    cross_out_t = cross_w[3]
    ffn_in_w = ffn_w[0]
    ffn_out_t = ffn_w[1]

    signals = mod_full + time_emb[0]
    shift_attn, scale_attn, gate_attn, shift_ffn, scale_ffn, gate_ffn = [
        signals[i : i + 1] for i in range(6)
    ]
    clip_length = lax.dynamic_index_in_dim(lengths, dp, 0, False)

    def own_chunks(array):
        full = jnp.pad(array, ((0, pad), (0, 0)))
        return [full[a:b] for a, b in cuts]

    hid = own_chunks(hidden[0])
    teach = own_chunks(teacher[0])
    index = jnp.arange(padded)
    pos_pad = jnp.pad(positions[0].reshape(3, 2, own_len), ((0, 0), (0, 0), (0, pad)))

    def both(own, other):
        return jnp.concatenate([x[a:b] for a, b in cuts for x in (own, other)], axis=0)

    def slot_valid(half):
        return (index < own_len) & (half * own_len + index < clip_length)

    own_valid = slot_valid(mp)
    key_valid = both(own_valid, slot_valid(1 - mp))
    key_mask = jnp.where(key_valid, 0.0, NEG).astype(F32)[:, None]
    row_valid = [own_valid.astype(F32)[a:b, None] for a, b in cuts]
    pos_own = lax.dynamic_index_in_dim(pos_pad, mp, 1, False)
    pos_other = lax.dynamic_index_in_dim(pos_pad, 1 - mp, 1, False)
    rates = rope_rates()
    angle = sum(
        both(pos_own[i], pos_other[i]).astype(F32)[:, None] * rates[i][None, :] for i in range(3)
    )
    even = np.arange(HD) % 2 == 0
    cos = jnp.cos(angle)
    sin = jnp.sin(angle) * np.where(even, -1.0, 1.0).astype(np.float32)
    ends = np.cumsum([0] + [2 * (b - a) for a, b in cuts])
    spans = [(int(ends[i]), int(ends[i + 1])) for i in range(len(cuts))]
    nc = len(cuts)

    text_rows, text_pieces = collect(text_states[0])
    cross_kp = dot_nn(text_rows, cross_w[1]) + hb_full[1, 1]
    cross_v = (dot_nn(text_rows, cross_w[2]) + hb_full[1, 2]).astype(BF)
    cross_ks = row_totals(squares(cross_kp))
    cross_kr = lax.rsqrt(cross_ks / D + EPS)
    cross_k = (cross_kp * cross_kr * qg_full[1, 1]).astype(BF)

    res0, unit0, scale0, rows0 = [], [], [], []
    qp, kp, vv, qs, ks = [], [], [], [], []
    for c in range(nc):
        r = hid[c].astype(F32)
        z, s = normal(r)
        x = (z * (1.0 + scale_attn) + shift_attn).astype(BF)
        rows, pieces = collect(x)
        qc = dot_nn(rows, self_w[0]) + hb_full[0, 0]
        kc = dot_nn(rows, self_w[1]) + hb_full[0, 1]
        vc = (dot_nn(rows, self_w[2]) + hb_full[0, 2]).astype(BF)
        tot = row_totals(jnp.concatenate([squares(qc), squares(kc)], axis=1))
        res0.append(r)
        unit0.append(z)
        scale0.append(s)
        rows0 += pieces
        qp.append(qc)
        kp.append(kc)
        vv.append(vc)
        qs.append(tot[:, 0:1])
        ks.append(tot[:, 1:2])
    qp, kp, vv = [jnp.concatenate(x, axis=0) for x in (qp, kp, vv)]
    qs, ks = [jnp.concatenate(x, axis=0) for x in (qs, ks)]
    self_q, self_k = prep(qp, kp, qs, ks, qg_full[0, 0], qg_full[0, 1], cos, sin)

    self_mixed, self_lse = [], []
    cross_mixed, cross_lse, cross_q, cross_qp, cross_qs = [], [], [], [], []
    rows1, rows2, branch0, unit1, scale1, unit2, scale2 = [], [], [], [], [], [], []
    acts, slopes, results, errors, d_ffn_all, after = [], [], [], [], [], []
    gate_ffn_grad, err_sq = 0.0, 0.0
    for c in range(nc):
        a, b = spans[c]
        mixed, lse = attend(self_q[a:b], self_k, vv, key_mask)
        self_mixed.append(mixed)
        self_lse.append(lse)
        branch = spread(dot_nt(mixed, self_out_t)) + out_bias_full[1]
        after_self = res0[c] + gate_attn * branch
        branch0.append(branch)
        z, s = normal(after_self)
        unit1.append(z)
        scale1.append(s)
        rows, pieces = collect((z * norm3_full + out_bias_full[0]).astype(BF))
        rows1.append(pieces)
        qc = dot_nn(rows, cross_w[0]) + hb_full[1, 0]
        tot = row_totals(squares(qc))
        qn = (qc * lax.rsqrt(tot / D + EPS) * qg_full[1, 0]).astype(BF)
        cross_qp.append(qc)
        cross_qs.append(tot)
        cross_q.append(qn)
        mixed, lse = attend(qn, cross_k, cross_v, None)
        cross_mixed.append(mixed)
        cross_lse.append(lse)
        after_cross = after_self + spread(dot_nt(mixed, cross_out_t)) + out_bias_full[2]
        z, s = normal(after_cross)
        unit2.append(z)
        scale2.append(s)
        rows, _ = collect((z * (1.0 + scale_ffn) + shift_ffn).astype(BF))
        rows2.append(rows)
        inner = dot_nn(rows, ffn_in_w) + ffn_bias_full
        act, back = jax.vjp(functools.partial(jax.nn.gelu, approximate=True), inner)
        slope = back(jnp.ones_like(inner))[0]
        acts.append(act.astype(BF))
        slopes.append(slope.astype(BF))
        after.append(after_cross)
    acts = list(tie(*acts))
    for c in range(nc):
        branch = spread(dot_nt(acts[c], ffn_out_t)) + out_bias_full[3]
        result = after[c] + gate_ffn * branch
        results.append(result.astype(BF))
        error = (result - teach[c].astype(F32)) * row_valid[c]
        errors.append(error)
        err_sq = err_sq + jnp.sum(error * error)
        gate_ffn_grad = gate_ffn_grad + colsum(branch * error)
        d_ffn_all.append((gate_ffn * error).astype(BF))

    def cat(parts):
        return jnp.concatenate(parts, axis=0)

    bias3 = bias2 = bias0 = bias1 = shift2 = scale2_g = norm3_g = gate0_g = 0.0
    ffn_b_grad = cross_qb = cross_qgain = 0.0
    d_rows2, d_inners, d_rows1, d_qpres = [], [], [], []
    cross_dk = cross_dv = 0.0
    d_rows0, state, backs = [], [], []
    def reduce_rows(full):
        return lax.psum_scatter(full, "dp", scatter_dimension=1, tiled=True)

    for c in range(nc):
        bias3 = bias3 + colsum(d_ffn_all[c].astype(F32))
        d_rows2.append(collect(d_ffn_all[c])[0])
    def inner_only(c):
        return (dot_nn(d_rows2[c], ffn_out_t) * slopes[c].astype(F32)).astype(BF)

    def inner_back(c):
        d_inner = inner_only(c)
        return d_inner, dot_nt(d_inner, ffn_in_w)

    def after_back(c, back):
        d_after = errors[c] + normal_back(back * (1.0 + scale_ffn), unit2[c], scale2[c])
        return d_after, d_after.astype(BF)

    g_out = dot_tn(cat(d_rows2), cat(acts)).astype(BF)
    d_rows2[0], g_out = tie(d_rows2[0], g_out)
    s_out = reduce_rows(g_out[None])
    d_inner, back = inner_back(0)
    d_inners.append(d_inner)
    back = spread(back)
    d_inner = inner_only(1)
    back, d_inner = tie(back, d_inner)
    backs.append(back)
    d_after, d_cross = after_back(0, back)
    d_afters, d_crosses = [d_after], [d_cross]
    d_inner, d_crosses[0] = tie(d_inner, d_crosses[0])
    cross_rows = [collect(d_crosses[0])]
    back = dot_nt(d_inner, ffn_in_w)
    cross_rows[0][1][1], d_inner, back = tie(cross_rows[0][1][1], d_inner, back)
    d_inners.append(d_inner)
    back = spread(back)
    g_in = dot_tn(cat(rows2), cat(d_inners)).astype(BF)
    back, g_in = tie(back, g_in)
    backs.append(back)
    d_after, d_cross = after_back(1, back)
    cross_rows[0][1][1], d_cross = tie(cross_rows[0][1][1], d_cross)
    cross_rows[0] = (cat(cross_rows[0][1]), cross_rows[0][1])
    d_afters.append(d_after)
    d_crosses.append(d_cross)
    cross_rows.append(collect(d_cross))
    for c in range(nc):
        back = backs[c]
        ffn_b_grad = ffn_b_grad + colsum(d_inners[c].astype(F32))
        shift2 = shift2 + colsum(back)
        scale2_g = scale2_g + colsum(back * unit2[c])
        d_after_cross = d_afters[c]
        bias2 = bias2 + colsum(d_crosses[c].astype(F32))
        rows, pieces = cross_rows[c]
        d_rows1.append(pieces)
        d_mixed = dot_nn(rows, cross_out_t).astype(BF)
        dqw, dk, dv, qdot, qgain = attend_back_cross(
            cross_q[c], cross_k, cross_v, d_mixed, cross_lse[c], cross_qp[c], cross_qs[c], qg_full[1, 0]
        )
        cross_dk = cross_dk + dk
        cross_dv = cross_dv + dv
        cross_qgain = cross_qgain + qgain[0]
        r = lax.rsqrt(cross_qs[c] / D + EPS)
        dot = row_totals(qdot)
        d_qpre = (dqw * r - cross_qp[c] * (r * r * r * dot / D)).astype(BF)
        d_qpres.append(d_qpre)
        cross_qb = cross_qb + colsum(d_qpre.astype(F32))
        back = spread(dot_nt(d_qpre, cross_w[0]))
        norm3_g = norm3_g + colsum(back * unit1[c])
        bias0 = bias0 + colsum(back)
        st = d_after_cross + normal_back(back * norm3_full, unit1[c], scale1[c])
        state.append(st)
        gate0_g = gate0_g + colsum(branch0[c] * st)
        d_self = (gate_attn * st).astype(BF)
        if c == nc - 1:
            d_self, s_out = tie(d_self, s_out)
            s_in = reduce_rows(g_in[None])
        bias1 = bias1 + colsum(d_self.astype(F32))
        d_rows0.append(collect(d_self)[1])

    cross_dkw = cross_dk * qg_full[1, 1]
    kdot = row_totals(jnp.sum(cross_dkw * cross_kp, axis=-1, keepdims=True))
    cross_kgain = colsum(cross_dk * cross_kp * cross_kr)
    d_kpre = (cross_dkw * cross_kr - cross_kp * (cross_kr**3 * kdot / D)).astype(BF)
    d_v = cross_dv.astype(BF)
    g_cross = head_grads(
        [
            list(zip(rows1, d_qpres)),
            [(text_pieces, d_kpre)],
            [(text_pieces, d_v)],
            list(zip(d_rows1, cross_mixed)),
        ]
    )
    ffn_out_g = s_out[0].astype(F32).T
    ffn_in_g = s_in[0].astype(F32)
    text_g = spread(dot_nt(d_kpre, cross_w[1]) + dot_nt(d_v, cross_w[2]))
    cross_b = jnp.stack([cross_qb, colsum(d_kpre.astype(F32)), colsum(d_v.astype(F32))])

    g_self_out = head_grads([list(zip(d_rows0, self_mixed))])
    d_mixed = dot_nn(cat([x for pieces in d_rows0 for x in pieces]), self_out_t).astype(BF)
    d_mixed, g_self_out, g_cross = tie(d_mixed, g_self_out, g_cross)
    lse = jnp.concatenate(self_lse, axis=2)
    dqw, dkw, dv, qdot, kdot, self_qgain, self_kgain = attend_back_self(
        self_q, self_k, vv, d_mixed, lse, key_mask, qp, kp, qs, ks, qg_full[0, 0], qg_full[0, 1], cos, sin
    )
    dots = []
    for a, b in spans:
        dots.append(row_totals(jnp.concatenate([qdot[a:b], kdot[a:b]], axis=1)))
    dots = cat(dots)
    rq = lax.rsqrt(qs / D + EPS)
    rk = lax.rsqrt(ks / D + EPS)
    d_q = (dqw * rq - qp * (rq**3 * dots[:, 0:1] / D)).astype(BF)
    d_k = (dkw * rk - kp * (rk**3 * dots[:, 1:2] / D)).astype(BF)
    g_self, part, other = self_back(rows0, spans, heads_w, [d_q, d_k, dv])
    self_b = jnp.stack([colsum(g.astype(F32)) for g in (d_q, d_k, dv)])

    blank = jnp.zeros((D,), F32)
    wide = jnp.stack(
        [blank, blank, gate0_g, shift2, scale2_g, gate_ffn_grad, bias0, bias1, bias2, bias3, norm3_g]
        + [jnp.broadcast_to(err_sq, (D,))]
        + [blank] * 4
    )
    narrow = jnp.concatenate(
        [
            self_b.reshape(-1, HD),
            cross_b.reshape(-1, HD),
            jnp.stack([self_qgain[0], self_kgain[0], cross_qgain, cross_kgain]).reshape(-1, HD),
            ffn_b_grad.reshape(-1, HD),
        ],
        axis=0,
    )
    n_narrow = narrow.shape[0]
    narrow = jnp.pad(narrow.reshape(-1), (0, -narrow.size % (8 * D))).reshape(-1, D)
    sums, hidden_g, small = tail(
        ndp,
        [g_self, g_self_out, g_cross],
        part,
        other,
        state,
        unit0,
        cat(scale0),
        1.0 + scale_attn,
        jnp.concatenate([wide, narrow]),
    )
    self_qkv_g = sums[:3]
    self_out_g = sums[3].T
    cross_qkv_g = sums[4:7]
    cross_out_g = sums[7].T
    wide = small[:16]
    narrow = small[16:].reshape(-1)[: n_narrow * HD].reshape(n_narrow, HD)
    narrow = lax.dynamic_slice_in_dim(narrow, dp * w_low, w_low, 1)
    mine = lax.dynamic_slice_in_dim(wide, (dp * 2 + mp) * w_f32, w_f32, 1)
    mean_loss = wide[11, 0] / (jnp.sum(lengths).astype(F32) * D)
    nh = head_bias.size // head_bias.shape[-1]
    ng = qk_gain.size // qk_gain.shape[-1]
    return (
        cat(results)[None, :own_len],
        mean_loss,
        hidden_g[None, :own_len],
        text_g[None],
        mine[:6],
        mine[6:10],
        mine[10],
        self_qkv_g,
        self_out_g,
        cross_qkv_g,
        cross_out_g,
        ffn_in_g,
        ffn_out_g,
        narrow[:nh].reshape(head_bias.shape),
        narrow[nh : nh + ng].reshape(qk_gain.shape),
        narrow[nh + ng :].reshape(ffn_bias.shape),
    )


def solution(mesh):
    in_specs = (
        P("dp", "mp", None),
        P("dp", "mp", None),
        P("dp", None, None),
        P(),
        P("dp", None, None),
        P("dp", "mp", None),
        P(None, ("dp", "mp")),
        P(None, ("dp", "mp")),
        P(("dp", "mp")),
        P(None, "dp", "mp"),
        P("mp", "dp"),
        P(None, "dp", "mp"),
        P("mp", "dp"),
        P("dp", "mp"),
        P("mp", "dp"),
        P(None, None, "mp", "dp"),
        P(None, None, "mp", "dp"),
        P("mp", "dp"),
    )
    out_specs = (
        P("dp", "mp", None),
        P(),
        P("dp", "mp", None),
        P("dp", "mp", None),
        P(None, ("dp", "mp")),
        P(None, ("dp", "mp")),
        P(("dp", "mp")),
        P(None, "dp", "mp"),
        P("mp", "dp"),
        P(None, "dp", "mp"),
        P("mp", "dp"),
        P("dp", "mp"),
        P("mp", "dp"),
        P(None, None, "mp", "dp"),
        P(None, None, "mp", "dp"),
        P("mp", "dp"),
    )
    return jax.shard_map(local, mesh=mesh, in_specs=in_specs, out_specs=out_specs, check_vma=False)
```

```python
import functools
import math

import jax
import jax.numpy as jnp
import numpy as np
from jax import lax
from jax.experimental import pallas as pl
from jax.experimental.pallas import tpu as pltpu
from jax.sharding import PartitionSpec as P

D = 1536
HD = 128
EPS = 1e-06
SCALE = HD ** (-0.5)
BF = jnp.bfloat16
F32 = jnp.float32
NEG = -1e30
SWAP = [(0, 1), (1, 0)]
VMEM_BYTES = 48 * 1024 * 1024


def rope_rates():
    pair_count = HD // 2
    third = pair_count // 3
    counts = [pair_count - 2 * third, third, third]
    rates = np.zeros((3, HD), np.float32)
    start = 0
    for axis_id, count in enumerate(counts):
        steps = np.arange(count, dtype=np.float32) / np.float32(count)
        values = np.exp(np.float32(-math.log(10000.0)) * steps).astype(np.float32)
        rates[axis_id, 2 * start : 2 * (start + count)] = np.repeat(values, 2)
        start += count
    return rates


def dot_nn(a, b):
    return lax.dot_general(a, b, (((1,), (0,)), ((), ())), preferred_element_type=F32)


def dot_nt(a, b):
    return lax.dot_general(a, b, (((1,), (1,)), ((), ())), preferred_element_type=F32)


def dot_tn(a, b):
    return lax.dot_general(a, b, (((0,), (0,)), ((), ())), preferred_element_type=F32)


def cost(flops, nbytes, trans=0):
    return pl.CostEstimate(flops=int(flops), bytes_accessed=int(nbytes), transcendentals=int(trans))


def params():
    return pltpu.CompilerParams(vmem_limit_bytes=VMEM_BYTES)


def turn(values):
    lane = lax.broadcasted_iota(jnp.int32, values.shape, 1)
    after = pltpu.roll(values, HD - 1, 1)
    before = pltpu.roll(values, 1, 1)
    return jnp.where(lane % 2 == 0, after, before)


def prep_kernel(qp, kp, qs, ks, qg, kg, cos, sin, q_out, k_out):
    c = cos[...]
    s = sin[...]
    for pre, scale, gain, out in ((qp, qs, qg, q_out), (kp, ks, kg, k_out)):
        v = pre[...] * scale[...] * gain[...]
        out[...] = (v * c + turn(v) * s).astype(BF)


def prep(qp, kp, qs, ks, qg, kg, cos, sin):
    rows, width = qp.shape
    head = pl.BlockSpec((rows, HD), lambda h: (0, h))
    col = pl.BlockSpec((rows, 1), lambda h: (0, 0))
    gain = pl.BlockSpec((1, HD), lambda h: (0, h))
    tab = pl.BlockSpec((rows, HD), lambda h: (0, 0))
    return pl.pallas_call(
        prep_kernel,
        grid=(width // HD,),
        in_specs=[head, head, col, col, gain, gain, tab, tab],
        out_specs=[head, head],
        out_shape=[jax.ShapeDtypeStruct((rows, width), BF)] * 2,
        compiler_params=params(),
        cost_estimate=cost(rows * width * 20, rows * width * 12),
        name="rope_prep",
    )(qp, kp, qs, ks, qg, kg, cos, sin)


def attend_kernel(masked, *refs):
    if masked:
        q, k, v, w, mask, out, lse, own, other = refs
    else:
        q, k, v, w, out, lse, own, other = refs
    st = dot_nt(k[...], q[...]) * SCALE
    if masked:
        st = st + mask[...]
    top = jnp.max(st, axis=0, keepdims=True)
    e = jnp.exp(st - top)
    total = jnp.sum(e, axis=0, keepdims=True)
    lse[0] = top + jnp.log(total)
    mixed = dot_tn(v[...], e.astype(BF)) * (1.0 / total)
    h = pl.program_id(0)
    out[:, pl.ds(pl.multiple_of(h * HD, HD), HD)] = mixed.T.astype(BF)

    @pl.when(h == pl.num_programs(0) - 1)
    def _():
        half = out.shape[0] // 2
        own[...] = dot_nt(out[:half], w[0])
        other[...] = dot_nt(out[half:], w[0]).astype(BF)


def attend(q, k, v, mask, weights, slab):
    nq, width = q.shape
    nk = k.shape[0]
    d = weights.shape[1]
    heads = width // HD
    qb = pl.BlockSpec((nq, HD), lambda h: (0, h))
    kb = pl.BlockSpec((nk, HD), lambda h: (0, h))
    ins = [qb, kb, kb, pl.BlockSpec((1, d, width), lambda h: (slab, 0, 0), pipeline_mode=pl.Buffered(1))]
    args = [q, k, v, weights]
    if mask is not None:
        ins.append(pl.BlockSpec((nk, 1), lambda h: (0, 0)))
        args.append(mask)
    return pl.pallas_call(
        functools.partial(attend_kernel, mask is not None),
        grid=(heads,),
        in_specs=ins,
        out_specs=[
            pl.BlockSpec((nq, width), lambda h: (0, 0)),
            pl.BlockSpec((1, 1, nq), lambda h: (h, 0, 0)),
            pl.BlockSpec((nq // 2, d), lambda h: (0, 0)),
            pl.BlockSpec((nq // 2, d), lambda h: (0, 0)),
        ],
        out_shape=[
            jax.ShapeDtypeStruct((nq, width), BF),
            jax.ShapeDtypeStruct((heads, 1, nq), F32),
            jax.ShapeDtypeStruct((nq // 2, d), F32),
            jax.ShapeDtypeStruct((nq // 2, d), BF),
        ],
        compiler_params=params(),
        cost_estimate=cost(4 * nq * nk * width * 3, 4 * nq * width + 4 * nk * width, nq * nk * heads),
        name="attend_fwd",
    )(*args)


def attend_back_kernel(self_form, *refs):
    if self_form:
        (q, k, v, do, lse, mask, qp, kp, qs, ks, qg, kg, cos, sin,
         dq_out, dk_out, dv_out, qdot, kdot, qgain, kgain) = refs
    else:
        q, k, v, do, lse, qp, qs, qg, dq_out, dk_out, dv_out, qdot, qgain = refs
    st = dot_nt(k[...], q[...]) * SCALE
    if self_form:
        st = st + mask[...]
    p = jnp.exp(st - lse[0])
    dp = dot_nt(v[...], do[...])
    inner = jnp.sum(dp * p, axis=0, keepdims=True)
    ds = (p * (dp - inner)).astype(BF)
    dv_out[...] = dot_nn(p.astype(BF), do[...]).astype(dv_out.dtype)
    dk = dot_nn(ds, q[...]) * SCALE
    dq = dot_tn(k[...], ds).T * SCALE
    sides = [(dq, qp, qs, qg, dq_out, qdot, qgain)]
    if self_form:
        dq = dq * cos[...] - turn(dq) * sin[...]
        dk = dk * cos[...] - turn(dk) * sin[...]
        sides = [(dq, qp, qs, qg, dq_out, qdot, qgain), (dk, kp, ks, kg, dk_out, kdot, kgain)]
    else:
        dk_out[...] = dk
    for grad, pre, scale, gain, out, dots, gains in sides:
        p_rows = pre[...]
        weighted = grad * gain[...]
        out[...] = weighted
        part = jnp.sum(weighted * p_rows, axis=1, keepdims=True)

        @pl.when(pl.program_id(0) == 0)
        def _():
            dots[...] = part

        @pl.when(pl.program_id(0) > 0)
        def _():
            dots[...] += part

        gains[...] = jnp.sum(grad * (p_rows * scale[...]), axis=0, keepdims=True)


def attend_back_self(q, k, v, do, lse, mask, qp, kp, qs, ks, qg, kg, cos, sin):
    n, width = q.shape
    heads = width // HD
    rows = pl.BlockSpec((n, HD), lambda h: (0, h))
    col = pl.BlockSpec((n, 1), lambda h: (0, 0))
    gain = pl.BlockSpec((1, HD), lambda h: (0, h))
    tab = pl.BlockSpec((n, HD), lambda h: (0, 0))
    lses = pl.BlockSpec((1, 1, n), lambda h: (h, 0, 0))
    full = jax.ShapeDtypeStruct((n, width), F32)
    cols = jax.ShapeDtypeStruct((n, 1), F32)
    gains = jax.ShapeDtypeStruct((1, width), F32)
    return pl.pallas_call(
        functools.partial(attend_back_kernel, True),
        grid=(heads,),
        in_specs=[rows, rows, rows, rows, lses, col, rows, rows, col, col, gain, gain, tab, tab],
        out_specs=[rows, rows, rows, col, col, gain, gain],
        out_shape=[full, full, jax.ShapeDtypeStruct((n, width), BF), cols, cols, gains, gains],
        compiler_params=params(),
        cost_estimate=cost(10 * n * n * width * 3, 26 * n * width, n * n * heads),
        name="attend_bwd_self",
    )(q, k, v, do, lse, mask, qp, kp, qs, ks, qg, kg, cos, sin)


def attend_back_cross(q, k, v, do, lse, qp, qs, qg):
    n, width = q.shape
    nk = k.shape[0]
    heads = width // HD
    rows = pl.BlockSpec((n, HD), lambda h: (0, h))
    keys = pl.BlockSpec((nk, HD), lambda h: (0, h))
    col = pl.BlockSpec((n, 1), lambda h: (0, 0))
    gain = pl.BlockSpec((1, HD), lambda h: (0, h))
    lses = pl.BlockSpec((1, 1, n), lambda h: (h, 0, 0))
    return pl.pallas_call(
        functools.partial(attend_back_kernel, False),
        grid=(heads,),
        in_specs=[rows, keys, keys, rows, lses, rows, col, gain],
        out_specs=[rows, keys, keys, col, gain],
        out_shape=[
            jax.ShapeDtypeStruct((n, width), F32),
            jax.ShapeDtypeStruct((nk, width), F32),
            jax.ShapeDtypeStruct((nk, width), F32),
            jax.ShapeDtypeStruct((n, 1), F32),
            jax.ShapeDtypeStruct((1, width), F32),
        ],
        compiler_params=params(),
        cost_estimate=cost(10 * n * nk * width * 3, 12 * n * width + 12 * nk * width, n * nk * heads),
        name="attend_bwd_cross",
    )(q, k, v, do, lse, qp, qs, qg)


def head_grads_kernel(plan, *refs):
    out = refs[-1]
    for i, terms in enumerate(plan):

        @pl.when(pl.program_id(0) == i)
        def _(terms=terms):
            total = None
            for a, b, lo, hi in terms:
                term = dot_tn(refs[a][...], refs[b][lo:hi])
                total = term if total is None else total + term
            out[0] = total.astype(BF)


def self_back_kernel(spans, *refs):
    n = 2 * len(spans)
    rows = refs[:n]
    weights = refs[n]
    heads = refs[n + 1 : n + 4]
    grads, part, other, acc = refs[n + 4 :]
    halves = [x for a, b in spans for x in ((a, (a + b) // 2), ((a + b) // 2, b))]
    for i in range(3):

        @pl.when(pl.program_id(0) == i)
        def _(i=i):
            total = None
            for x, (a, b) in zip(rows, halves):
                term = dot_tn(x[...], heads[i][a:b])
                total = term if total is None else total + term
            grads[0] = total.astype(BF)
            back = dot_nt(heads[i][...], weights[0])
            if i == 0:
                acc[...] = back
            elif i == 1:
                acc[...] += back
            else:
                back = acc[...] + back
                at = 0
                for a, b in spans:
                    half = (b - a) // 2
                    part[at : at + half] = back[a : a + half]
                    other[at : at + half] = back[a + half : b].astype(BF)
                    at += half


def self_back(rows, spans, weights, heads):
    n, width = heads[0].shape
    d = rows[0].shape[1]
    once = lambda x: pl.BlockSpec(x.shape, lambda i: (0, 0), pipeline_mode=pl.Buffered(1))
    return pl.pallas_call(
        functools.partial(self_back_kernel, spans),
        grid=(3,),
        in_specs=[once(x) for x in rows]
        + [pl.BlockSpec((1, d, width), lambda i: (i, 0, 0))]
        + [once(x) for x in heads],
        out_specs=[
            pl.BlockSpec((1, d, width), lambda i: (i, 0, 0)),
            pl.BlockSpec((n // 2, d), lambda i: (0, 0)),
            pl.BlockSpec((n // 2, d), lambda i: (0, 0)),
        ],
        out_shape=[
            jax.ShapeDtypeStruct((3, d, width), BF),
            jax.ShapeDtypeStruct((n // 2, d), F32),
            jax.ShapeDtypeStruct((n // 2, d), BF),
        ],
        scratch_shapes=[pltpu.VMEM((n, d), F32)],
        compiler_params=params(),
        cost_estimate=cost(12 * n * d * width, 30e6),
        name="self_back",
    )(*rows, weights, *heads)


def head_grads(products):
    arrays, plan = [], []

    def place(x):
        for i, y in enumerate(arrays):
            if x is y:
                return i
        arrays.append(x)
        return len(arrays) - 1

    for pairs in products:
        terms = []
        for pieces, b in pairs:
            at = 0
            for a in pieces:
                terms.append((place(a), place(b), at, at + a.shape[0]))
                at += a.shape[0]
        plan.append(terms)
    m, n = products[0][0][0][0].shape[1], products[0][0][1].shape[1]
    rows = sum(b.shape[0] for pairs in products for _, b in pairs)
    return pl.pallas_call(
        functools.partial(head_grads_kernel, plan),
        grid=(len(products),),
        in_specs=[
            pl.BlockSpec(x.shape, lambda i: (0, 0), pipeline_mode=pl.Buffered(1)) for x in arrays
        ],
        out_specs=pl.BlockSpec((1, m, n), lambda i: (i, 0, 0)),
        out_shape=jax.ShapeDtypeStruct((len(products), m, n), BF),
        compiler_params=params(),
        cost_estimate=cost(2 * rows * m * n, 2 * sum(x.size for x in arrays) + 2 * len(products) * m * n),
        name="head_grads",
    )(*arrays)


def tail_kernel(ndp, counts, nc, *refs):
    n = len(counts)
    g = refs[:n]
    state = refs[n : n + nc]
    unit = refs[n + nc : n + 2 * nc]
    (part, other, lns, ones, small, gsum, hgrad, small_out,
     mine, got, send, slot, ybuf, pbuf, stbuf, ubuf, vals, inbox,
     mine_sem, got_send, got_recv, ring_send, ring_recv, y_sem, load_sem, sum_send, sum_recv) = refs[n + 2 * nc :]
    chips = ndp // 2
    bits = ndp.bit_length() - 1
    dp = lax.axis_index("dp")
    mp = lax.axis_index("mp")
    core = lax.rem(dp, 2)
    chip = lax.div(dp, 2)
    odd = lax.rem(chip, 2)
    row = lax.div(chip, 2)
    place = row * (1 - odd) + (chips - 1 - row) * odd
    way = 1 - 2 * core

    def chip_at(shift):
        spot = lax.rem(place + way * shift + 2 * chips, chips)
        back = lax.div(spot, chips // 2)
        return 2 * spot * (1 - back) + (2 * (chips - 1 - spot) + 1) * back

    after = 2 * chip_at(1) + core
    before = 2 * chip_at(-1) + core
    mates = [dp + (1 - 2 * lax.rem(lax.div(dp, 1 << b), 2)) * (1 << b) for b in range(bits)]
    mesh_id = pl.DeviceIdType.MESH

    barrier = pltpu.get_barrier_semaphore()
    for device in (after, before, *mates):
        pl.semaphore_signal(barrier, inc=1, device_id=(device, mp), device_id_type=mesh_id)
    pl.semaphore_signal(barrier, inc=1, device_id=(dp, 1 - mp), device_id_type=mesh_id)
    pl.semaphore_wait(barrier, 3 + bits)

    def remote(src, dst, s_sem, r_sem, device):
        return pltpu.make_async_remote_copy(
            src_ref=src, dst_ref=dst, send_sem=s_sem, recv_sem=r_sem, device_id=device, device_id_type=mesh_id
        )

    starts = [sum(counts[:i]) for i in range(n)]
    total = sum(counts)
    cuts = [(0, (total + 1) // 2), ((total + 1) // 2, total)]

    def to_mate(s, i):
        return remote(
            g[i].at[:, chip_at(1 + s), 1 - core],
            got.at[s, pl.ds(starts[i], counts[i])],
            got_send.at[i, s],
            got_recv.at[i, s],
            (mates[0], mp),
        )

    def to_self(s, i):
        return pltpu.make_async_copy(
            g[i].at[:, chip_at(-1 - s), core], mine.at[s, pl.ds(starts[i], counts[i])], mine_sem.at[i, s]
        )

    def along(s, half):
        lo, hi = cuts[half]
        return remote(
            send.at[s, pl.ds(lo, hi - lo)],
            slot.at[s, pl.ds(lo, hi - lo)],
            ring_send.at[half, s],
            ring_recv.at[half, s],
            (after, mp),
        )

    def sum_copy(j):
        if j < bits:
            return remote(vals.at[j], inbox.at[j], sum_send.at[j], sum_recv.at[j], (mates[j], mp))
        return remote(
            vals.at[j, pl.ds(0, 16)], inbox.at[j, pl.ds(0, 16)], sum_send.at[j], sum_recv.at[j], (dp, 1 - mp)
        )

    y_copy = remote(other, ybuf, y_sem.at[0], y_sem.at[1], (dp, 1 - mp))
    for s in range(chips):
        for i in range(n):
            to_mate(s, i).start()
            to_self(s, i).start()
        if s == 0:
            y_copy.start()
    pairs = [(part, pbuf)]
    at = 0
    for st, un in zip(state, unit):
        span = pl.ds(at, st.shape[0])
        pairs += [(st, stbuf.at[span]), (un, ubuf.at[span])]
        at += st.shape[0]
    loads = [pltpu.make_async_copy(src, dst, load_sem.at[i]) for i, (src, dst) in enumerate(pairs)]
    for load in loads:
        load.start()

    def finish_rows():
        for load in loads:
            load.wait()
        y_copy.wait_recv()
        rows, width = pbuf.shape
        block = 80 if rows % 80 == 0 else 16
        gain = ones[...]

        def body(i, sums):
            at = pl.ds(pl.multiple_of(i * block, block), block)
            back = pbuf[at, :] + ybuf[at, :].astype(F32)
            z = ubuf[at, :]
            grad = back * gain
            mean_g = jnp.mean(grad, axis=1, keepdims=True)
            mean_gz = jnp.mean(grad * z, axis=1, keepdims=True)
            hgrad[at, :] = stbuf[at, :] + lns[at, :] * (grad - mean_g - z * mean_gz)
            return (
                sums[0] + jnp.sum(back, axis=0, keepdims=True),
                sums[1] + jnp.sum(back * z, axis=0, keepdims=True),
            )

        zero = jnp.zeros((1, width), F32)
        sums = lax.fori_loop(0, rows // block, body, (zero, zero))
        vals[0] = small[...]
        vals[0, 0:1, :] = sums[0]
        vals[0, 1:2, :] = sums[1]
        sum_copy(0).start()

    def sum_step(j):
        sum_copy(j).wait_recv()
        if j < bits:
            vals[j + 1] = vals[j] + inbox[j]
            sum_copy(j + 1).start()
        else:
            small_out[...] = vals[j]
            small_out[0:16, :] = vals[j, 0:16, :] + inbox[j, 0:16, :]

    first = min(2, chips - 1)
    done = 0
    for s in range(chips):
        for i in range(n):
            to_self(s, i).wait()
            to_mate(s, i).wait_recv()
        for half in range(2):
            lo, hi = cuts[half]
            value = mine[s, lo:hi].astype(F32) + got[s, lo:hi].astype(F32)
            if s > 0:
                along(s - 1, half).wait_recv()
                value = value + slot[s - 1, lo:hi].astype(F32)
            if s < chips - 1:
                send[s, lo:hi] = value.astype(BF)
                along(s, half).start()
            else:
                gsum[lo:hi] = value
        if s == first:
            finish_rows()
        elif s > first and done <= bits:
            sum_step(done)
            done += 1
    while done <= bits:
        sum_step(done)
        done += 1
    for s in range(chips):
        for i in range(n):
            to_mate(s, i).wait_send()
        if s < chips - 1:
            for half in range(2):
                along(s, half).wait_send()
    y_copy.wait_send()
    for j in range(bits + 1):
        sum_copy(j).wait_send()


def tail(ndp, grads, part, other, state, unit, lns, ones, small):
    chips = ndp // 2
    bits = ndp.bit_length() - 1
    split = [x.reshape(x.shape[0], chips, 2, x.shape[1] // ndp, x.shape[2]) for x in grads]
    counts = tuple(x.shape[0] for x in grads)
    total = sum(counts)
    r, w = split[0].shape[3:]
    rows, width = part.shape
    n = len(grads)
    nc = len(state)
    hbm = pl.BlockSpec(memory_space=pl.ANY)
    vmem = pl.BlockSpec(memory_space=pltpu.VMEM)
    dma = pltpu.SemaphoreType.DMA
    return pl.pallas_call(
        functools.partial(tail_kernel, ndp, counts, nc),
        in_specs=[hbm] * (n + 2 * nc) + [hbm, hbm, vmem, vmem, vmem],
        out_specs=[vmem] * 3,
        out_shape=[
            jax.ShapeDtypeStruct((total, r, w), F32),
            jax.ShapeDtypeStruct((rows, width), F32),
            jax.ShapeDtypeStruct(small.shape, F32),
        ],
        scratch_shapes=[
            pltpu.VMEM((chips, total, r, w), BF),
            pltpu.VMEM((chips, total, r, w), BF),
            pltpu.VMEM((chips - 1, total, r, w), BF),
            pltpu.VMEM((chips - 1, total, r, w), BF),
            pltpu.VMEM((rows, width), BF),
            pltpu.VMEM((rows, width), F32),
            pltpu.VMEM((rows, width), F32),
            pltpu.VMEM((rows, width), F32),
            pltpu.VMEM((bits + 1,) + small.shape, F32),
            pltpu.VMEM((bits + 1,) + small.shape, F32),
            dma((n, chips)),
            dma((n, chips)),
            dma((n, chips)),
            dma((2, chips - 1)),
            dma((2, chips - 1)),
            dma((2,)),
            dma((1 + 2 * nc,)),
            dma((bits + 1,)),
            dma((bits + 1,)),
        ],
        compiler_params=pltpu.CompilerParams(
            vmem_limit_bytes=58 * 1024 * 1024, collective_id=0, has_side_effects=True
        ),
        cost_estimate=cost(1e6, 1e6),
        name="tail_sums",
    )(*split, *state, *unit, part, other, lns, ones, small)


def normal(values):
    center = values - jnp.mean(values, axis=-1, keepdims=True)
    scale = lax.rsqrt(jnp.mean(center * center, axis=-1, keepdims=True) + EPS)
    return center * scale, scale


def normal_back(grad, unit, scale):
    mean_g = jnp.mean(grad, axis=-1, keepdims=True)
    mean_gz = jnp.mean(grad * unit, axis=-1, keepdims=True)
    return scale * (grad - mean_g - unit * mean_gz)


def swap(values):
    return lax.ppermute(values, "mp", SWAP)


def collect(own):
    pieces = [own, swap(own)]
    return jnp.concatenate(pieces, axis=0), pieces


def spread(partial):
    half = partial.shape[0] // 2
    return partial[:half] + swap(partial[half:].astype(BF)).astype(F32)


def halves(partial):
    half = partial.shape[0] // 2
    return partial[:half], swap(partial[half:].astype(BF))


def row_totals(own):
    half = own.shape[0] // 2
    return own + swap(jnp.concatenate([own[half:], own[:half]], axis=0))


def squares(values):
    return jnp.sum(values * values, axis=-1, keepdims=True)


def colsum(values):
    return jnp.sum(values, axis=0, dtype=F32)


def tie(*values):
    return lax.optimization_barrier(values)


def partners(ndp, bit):
    return [(i, i ^ (1 << bit)) for i in range(ndp)]


def gather_small(flat, ndp, dp, mp):
    rows = flat[None]
    got = swap(rows)
    rows = jnp.where(mp == 0, jnp.concatenate([rows, got]), jnp.concatenate([got, rows]))
    for bit in range(ndp.bit_length() - 1):
        got = lax.ppermute(rows, "dp", partners(ndp, bit))
        low = (dp >> bit) % 2 == 0
        rows = jnp.where(low, jnp.concatenate([rows, got]), jnp.concatenate([got, rows]))
    return rows


def chunks_of(padded):
    first = (padded // 2 + 15) // 16 * 16
    return [(0, first), (first, padded)]


def local(
    hidden,
    text_states,
    time_emb,
    lengths,
    positions,
    teacher,
    modulation,
    out_bias,
    norm3_gain,
    self_qkv,
    self_out,
    cross_qkv,
    cross_out,
    ffn_in,
    ffn_out,
    head_bias,
    qk_gain,
    ffn_bias,
):
    ndp = lax.axis_size("dp")
    dp = lax.axis_index("dp")
    mp = lax.axis_index("mp")
    own_len = hidden.shape[1]
    length = 2 * own_len
    padded = (own_len + 15) // 16 * 16
    pad = padded - own_len
    cuts = chunks_of(padded)

    f32_part = jnp.concatenate([modulation, out_bias, norm3_gain[None]], axis=0)
    hb = head_bias.reshape(-1, head_bias.shape[-1])
    qg = qk_gain.reshape(-1, qk_gain.shape[-1])
    low_part = jnp.concatenate([hb, qg, ffn_bias], axis=0).astype(F32)
    n_f32, w_f32 = f32_part.shape
    n_low, w_low = low_part.shape
    flat = jnp.concatenate([f32_part.reshape(-1), low_part.reshape(-1)])
    n_flat = flat.shape[0]
    flat_all = gather_small(jnp.pad(flat, (0, -n_flat % 128)), ndp, dp, mp)[:, :n_flat]
    f32_all = flat_all[:, : n_f32 * w_f32].reshape(2 * ndp, n_f32, w_f32)
    f32_all = f32_all.transpose(1, 0, 2).reshape(n_f32, -1)
    low_all = flat_all[:, n_f32 * w_f32 :].reshape(ndp, 2, n_low, w_low)
    low_all = lax.dynamic_index_in_dim(low_all, mp, 1, False)
    low_all = low_all.transpose(1, 0, 2).reshape(n_low, -1)
    mod_full = f32_all[:6]
    out_bias_full = f32_all[6:10]
    norm3_full = f32_all[10]
    hb_full = low_all[: hb.shape[0]].reshape(2, 3, -1)
    qg_full = low_all[hb.shape[0] : hb.shape[0] + qg.shape[0]].reshape(2, 2, 1, -1)
    ffn_bias_full = low_all[hb.shape[0] + qg.shape[0] :].reshape(-1)

    def whole(shards):
        return lax.all_gather(shards, "dp", axis=1, tiled=True)

    heads_w = whole(jnp.concatenate([self_qkv, self_out.T[None], cross_qkv, cross_out.T[None]]))
    self_w = heads_w[:4]
    cross_w = heads_w[4:]
    ffn_w = whole(jnp.stack([ffn_in, ffn_out.T]))
    self_out_t = self_w[3]
    cross_out_t = cross_w[3]
    ffn_in_w = ffn_w[0]
    ffn_out_t = ffn_w[1]

    signals = mod_full + time_emb[0]
    shift_attn, scale_attn, gate_attn, shift_ffn, scale_ffn, gate_ffn = [
        signals[i : i + 1] for i in range(6)
    ]
    clip_length = lax.dynamic_index_in_dim(lengths, dp, 0, False)

    def own_chunks(array):
        full = jnp.pad(array, ((0, pad), (0, 0)))
        return [full[a:b] for a, b in cuts]

    hid = own_chunks(hidden[0])
    teach = own_chunks(teacher[0])
    index = jnp.arange(padded)
    pos_pad = jnp.pad(positions[0].reshape(3, 2, own_len), ((0, 0), (0, 0), (0, pad)))

    def both(own, other):
        return jnp.concatenate([x[a:b] for a, b in cuts for x in (own, other)], axis=0)

    def slot_valid(half):
        return (index < own_len) & (half * own_len + index < clip_length)

    own_valid = slot_valid(mp)
    key_valid = both(own_valid, slot_valid(1 - mp))
    key_mask = jnp.where(key_valid, 0.0, NEG).astype(F32)[:, None]
    row_valid = [own_valid.astype(F32)[a:b, None] for a, b in cuts]
    pos_own = lax.dynamic_index_in_dim(pos_pad, mp, 1, False)
    pos_other = lax.dynamic_index_in_dim(pos_pad, 1 - mp, 1, False)
    rates = rope_rates()
    angle = sum(
        both(pos_own[i], pos_other[i]).astype(F32)[:, None] * rates[i][None, :] for i in range(3)
    )
    even = np.arange(HD) % 2 == 0
    cos = jnp.cos(angle)
    sin = jnp.sin(angle) * np.where(even, -1.0, 1.0).astype(np.float32)
    ends = np.cumsum([0] + [2 * (b - a) for a, b in cuts])
    spans = [(int(ends[i]), int(ends[i + 1])) for i in range(len(cuts))]
    nc = len(cuts)

    text_rows, text_pieces = collect(text_states[0])
    cross_kp = dot_nn(text_rows, cross_w[1]) + hb_full[1, 1]
    cross_v = (dot_nn(text_rows, cross_w[2]) + hb_full[1, 2]).astype(BF)
    cross_ks = row_totals(squares(cross_kp))
    cross_kr = lax.rsqrt(cross_ks / D + EPS)
    cross_k = (cross_kp * cross_kr * qg_full[1, 1]).astype(BF)

    res0, unit0, scale0, rows0 = [], [], [], []
    qp, kp, vv, qs, ks = [], [], [], [], []
    for c in range(nc):
        r = hid[c].astype(F32)
        z, s = normal(r)
        x = (z * (1.0 + scale_attn) + shift_attn).astype(BF)
        rows, pieces = collect(x)
        qc = dot_nn(rows, self_w[0]) + hb_full[0, 0]
        kc = dot_nn(rows, self_w[1]) + hb_full[0, 1]
        vc = (dot_nn(rows, self_w[2]) + hb_full[0, 2]).astype(BF)
        tot = row_totals(jnp.concatenate([squares(qc), squares(kc)], axis=1))
        res0.append(r)
        unit0.append(z)
        scale0.append(s)
        rows0 += pieces
        qp.append(qc)
        kp.append(kc)
        vv.append(vc)
        scales = lax.rsqrt(tot / D + EPS)
        qs.append(scales[:, 0:1])
        ks.append(scales[:, 1:2])
    qp, kp, vv = [jnp.concatenate(x, axis=0) for x in (qp, kp, vv)]
    qs, ks = [jnp.concatenate(x, axis=0) for x in (qs, ks)]
    self_q, self_k = prep(qp, kp, qs, ks, qg_full[0, 0], qg_full[0, 1], cos, sin)

    none = [None] * nc
    f, g = nc - 1, 0
    self_mixed, self_lse, branch0, unit1, scale1, after_self = [list(none) for _ in range(6)]
    cross_mixed, cross_lse, cross_q, cross_qp, cross_qs = [list(none) for _ in range(5)]
    rows1, rows2, unit2, scale2, after = [list(none) for _ in range(5)]

    def self_rows(c):
        a, b = spans[c]
        self_mixed[c], self_lse[c], own, other = attend(self_q[a:b], self_k, vv, key_mask, heads_w, 3)
        return own, swap(other)

    def cross_query(c, own, got):
        branch0[c] = own + got.astype(F32) + out_bias_full[1]
        after_self[c] = res0[c] + gate_attn * branch0[c]
        unit1[c], scale1[c] = normal(after_self[c])
        x = (unit1[c] * norm3_full + out_bias_full[0]).astype(BF)
        rows1[c] = [x, swap(x)]

    def cross_prepare(c, got=None):
        qc = dot_nn(jnp.concatenate(rows1[c], axis=0), heads_w[4]) + hb_full[1, 0]
        if got is not None:
            qc, got = tie(qc, got)
        cross_qp[c] = qc
        cross_qs[c] = lax.rsqrt(row_totals(squares(qc)) / D + EPS)
        cross_q[c] = (qc * cross_qs[c] * qg_full[1, 0]).astype(BF)
        return got

    def cross_attend(c):
        cross_mixed[c], cross_lse[c], own, other = attend(cross_q[c], cross_k, cross_v, None, heads_w, 7)
        return own, other

    def ffn_input(c, own, got):
        after[c] = after_self[c] + own + got.astype(F32) + out_bias_full[2]
        unit2[c], scale2[c] = normal(after[c])
        return (unit2[c] * (1.0 + scale_ffn) + shift_ffn).astype(BF)

    own_f, got_f = self_rows(f)
    own_g, got_g = self_rows(g)
    got_f, own_g = tie(got_f, own_g)
    cross_query(f, own_f, got_f)
    cross_query(g, own_g, got_g)
    cross_prepare(f)
    own_f, other_f = cross_attend(f)
    rows1[g][1], other_f = tie(rows1[g][1], other_f)
    got_f = swap(other_f)
    got_f = cross_prepare(g, got_f)
    x_f = ffn_input(f, own_f, got_f)
    cross_q[g], x_f = tie(cross_q[g], x_f)
    y_f = swap(x_f)
    own_g, other_g = cross_attend(g)
    y_f, own_g, other_g = tie(y_f, own_g, other_g)
    rows2[f] = jnp.concatenate([x_f, y_f], axis=0)
    got_g = swap(other_g)

    def cat(parts):
        return jnp.concatenate(parts, axis=0)

    def reduce_rows(full):
        return lax.psum_scatter(full, "dp", scatter_dimension=1, tiled=True)

    acts, slopes, results, errors, d_ffn, d_inners, d_afters, d_crosses = [list(none) for _ in range(8)]
    squares_of, gate_grads, ffn_backs = [list(none) for _ in range(3)]

    def inner_of(c):
        inner = dot_nn(rows2[c], ffn_in_w) + ffn_bias_full
        act, back = jax.vjp(functools.partial(jax.nn.gelu, approximate=True), inner)
        acts[c] = act.astype(BF)
        slopes[c] = back(jnp.ones_like(inner))[0].astype(BF)

    def loss_of(c, own, got):
        branch = own + got.astype(F32) + out_bias_full[3]
        result = after[c] + gate_ffn * branch
        results[c] = result.astype(BF)
        errors[c] = (result - teach[c].astype(F32)) * row_valid[c]
        d_ffn[c] = (gate_ffn * errors[c]).astype(BF)
        squares_of[c] = jnp.sum(errors[c] * errors[c])
        gate_grads[c] = colsum(branch * errors[c])

    def inner_back(c, rows):
        d_inners[c] = (dot_nn(rows, ffn_out_t) * slopes[c].astype(F32)).astype(BF)

    def after_back(c, own, got):
        back = own + got.astype(F32)
        ffn_backs[c] = back
        d_afters[c] = errors[c] + normal_back(back * (1.0 + scale_ffn), unit2[c], scale2[c])
        d_crosses[c] = d_afters[c].astype(BF)

    inner_of(f)
    got_g, acts[f] = tie(got_g, acts[f])
    x_g = ffn_input(g, own_g, got_g)
    acts[f], x_g = tie(acts[f], x_g)
    y_g = swap(x_g)
    branch_f = dot_nt(acts[f], ffn_out_t)
    y_g, branch_f = tie(y_g, branch_f)
    rows2[g] = jnp.concatenate([x_g, y_g], axis=0)
    own_f, got_f = halves(branch_f)
    inner_of(g)
    got_f, acts[g] = tie(got_f, acts[g])
    loss_of(f, own_f, got_f)
    acts[g], d_ffn[f] = tie(acts[g], d_ffn[f])
    d_f = swap(d_ffn[f])
    branch_g = dot_nt(acts[g], ffn_out_t)
    d_f, branch_g = tie(d_f, branch_g)
    own_g, got_g = halves(branch_g)
    d_f = cat([d_ffn[f], d_f])
    inner_back(f, d_f)
    d_inners[f], got_g = tie(d_inners[f], got_g)
    loss_of(g, own_g, got_g)
    d_inners[f], d_ffn[g] = tie(d_inners[f], d_ffn[g])
    d_g = swap(d_ffn[g])
    back_f = dot_nt(d_inners[f], ffn_in_w)
    d_g, back_f = tie(d_g, back_f)
    own_f, got_f = halves(back_f)
    d_g = cat([d_ffn[g], d_g])
    g_out = dot_tn(cat([d_f, d_g]), cat([acts[f], acts[g]])).astype(BF)
    got_f, d_g, g_out = tie(got_f, d_g, g_out)
    s_out = reduce_rows(g_out[None])
    inner_back(g, d_g)
    after_back(f, own_f, got_f)
    d_inners[g], d_crosses[f] = tie(d_inners[g], d_crosses[f])
    c_f = swap(d_crosses[f])
    back_g = dot_nt(d_inners[g], ffn_in_w)
    c_f, d_inners[g], back_g = tie(c_f, d_inners[g], back_g)
    own_g, got_g = halves(back_g)
    g_in = dot_tn(cat([rows2[f], rows2[g]]), cat([d_inners[f], d_inners[g]])).astype(BF)
    got_g, g_in = tie(got_g, g_in)
    after_back(g, own_g, got_g)
    c_f, d_crosses[g] = tie(c_f, d_crosses[g])
    c_g = swap(d_crosses[g])
    d_rows1 = list(none)
    d_rows1[f] = [d_crosses[f], c_f]
    d_rows1[g] = [d_crosses[g], c_g]
    err_sq = sum(squares_of)
    gate_ffn_grad = sum(gate_grads)
    bias3 = sum(colsum(x.astype(F32)) for x in d_ffn)
    bias2 = sum(colsum(x.astype(F32)) for x in d_crosses)
    ffn_b_grad = sum(colsum(x.astype(F32)) for x in d_inners)
    shift2 = sum(colsum(x) for x in ffn_backs)
    scale2_g = sum(colsum(x * z) for x, z in zip(ffn_backs, unit2))

    bias0 = bias1 = norm3_g = gate0_g = cross_qb = cross_qgain = cross_dk = cross_dv = 0.0
    d_qpres, d_rows0, state = [list(none) for _ in range(3)]
    for c in (f, g):
        d_mixed = dot_nn(cat(d_rows1[c]), cross_out_t).astype(BF)
        if c == g:
            d_mixed, q_back = tie(d_mixed, q_back)
            own_q, got_q = halves(q_back)
        dqw, dk, dv, qdot, qgain = attend_back_cross(
            cross_q[c], cross_k, cross_v, d_mixed, cross_lse[c], cross_qp[c], cross_qs[c], qg_full[1, 0]
        )
        if c == f:
            d_rows1[g][1], dqw, qdot = tie(d_rows1[g][1], dqw, qdot)
        else:
            got_q, dqw, qdot = tie(got_q, dqw, qdot)
        cross_dk = cross_dk + dk
        cross_dv = cross_dv + dv
        cross_qgain = cross_qgain + qgain[0]
        r = cross_qs[c]
        dot = row_totals(qdot)
        d_qpres[c] = (dqw * r - cross_qp[c] * (r * r * r * dot / D)).astype(BF)
        cross_qb = cross_qb + colsum(d_qpres[c].astype(F32))
        q_back = dot_nt(d_qpres[c], cross_w[0])
    backs = {f: own_q + got_q.astype(F32), g: spread(q_back)}
    for c in (f, g):
        back = backs[c]
        norm3_g = norm3_g + colsum(back * unit1[c])
        bias0 = bias0 + colsum(back)
        state[c] = d_afters[c] + normal_back(back * norm3_full, unit1[c], scale1[c])
        gate0_g = gate0_g + colsum(branch0[c] * state[c])
        d_self = (gate_attn * state[c]).astype(BF)
        bias1 = bias1 + colsum(d_self.astype(F32))
        d_rows0[c] = [d_self, swap(d_self)]

    cross_dkw = cross_dk * qg_full[1, 1]
    kdot = row_totals(jnp.sum(cross_dkw * cross_kp, axis=-1, keepdims=True))
    cross_kgain = colsum(cross_dk * cross_kp * cross_kr)
    d_kpre = (cross_dkw * cross_kr - cross_kp * (cross_kr**3 * kdot / D)).astype(BF)
    d_v = cross_dv.astype(BF)
    g_cross = head_grads(
        [
            list(zip(rows1, d_qpres)),
            [(text_pieces, d_kpre)],
            [(text_pieces, d_v)],
            list(zip(d_rows1, cross_mixed)),
        ]
    )
    own_text, got_text = halves(dot_nt(d_kpre, cross_w[1]) + dot_nt(d_v, cross_w[2]))
    cross_b = jnp.stack([cross_qb, colsum(d_kpre.astype(F32)), colsum(d_v.astype(F32))])

    g_self_out = head_grads([list(zip(d_rows0, self_mixed))])
    d_mixed = dot_nn(cat([x for pieces in d_rows0 for x in pieces]), self_out_t).astype(BF)
    d_mixed, g_self_out, g_cross, s_out, g_in = tie(d_mixed, g_self_out, g_cross, s_out, g_in)
    s_in = reduce_rows(g_in[None])
    ffn_out_g = s_out[0].astype(F32).T
    ffn_in_g = s_in[0].astype(F32)
    lse = jnp.concatenate(self_lse, axis=2)
    dqw, dkw, dv, qdot, kdot, self_qgain, self_kgain = attend_back_self(
        self_q, self_k, vv, d_mixed, lse, key_mask, qp, kp, qs, ks, qg_full[0, 0], qg_full[0, 1], cos, sin
    )
    dots = []
    for a, b in spans:
        dots.append(row_totals(jnp.concatenate([qdot[a:b], kdot[a:b]], axis=1)))
    dots = cat(dots)
    d_q = (dqw * qs - qp * (qs**3 * dots[:, 0:1] / D)).astype(BF)
    d_k = (dkw * ks - kp * (ks**3 * dots[:, 1:2] / D)).astype(BF)
    d_q, got_text = tie(d_q, got_text)
    text_g = own_text + got_text.astype(F32)
    g_self, part, other = self_back(rows0, spans, heads_w, [d_q, d_k, dv])
    self_b = jnp.stack([colsum(g.astype(F32)) for g in (d_q, d_k, dv)])

    blank = jnp.zeros((D,), F32)
    wide = jnp.stack(
        [blank, blank, gate0_g, shift2, scale2_g, gate_ffn_grad, bias0, bias1, bias2, bias3, norm3_g]
        + [jnp.broadcast_to(err_sq, (D,))]
        + [blank] * 4
    )
    narrow = jnp.concatenate(
        [
            self_b.reshape(-1, HD),
            cross_b.reshape(-1, HD),
            jnp.stack([self_qgain[0], self_kgain[0], cross_qgain, cross_kgain]).reshape(-1, HD),
            ffn_b_grad.reshape(-1, HD),
        ],
        axis=0,
    )
    n_narrow = narrow.shape[0]
    narrow = jnp.pad(narrow.reshape(-1), (0, -narrow.size % (8 * D))).reshape(-1, D)
    sums, hidden_g, small = tail(
        ndp,
        [g_self, g_self_out, g_cross],
        part,
        other,
        state,
        unit0,
        cat(scale0),
        1.0 + scale_attn,
        jnp.concatenate([wide, narrow]),
    )
    self_qkv_g = sums[:3]
    self_out_g = sums[3].T
    cross_qkv_g = sums[4:7]
    cross_out_g = sums[7].T
    wide = small[:16]
    narrow = small[16:].reshape(-1)[: n_narrow * HD].reshape(n_narrow, HD)
    narrow = lax.dynamic_slice_in_dim(narrow, dp * w_low, w_low, 1)
    mine = lax.dynamic_slice_in_dim(wide, (dp * 2 + mp) * w_f32, w_f32, 1)
    mean_loss = wide[11, 0] / (jnp.sum(lengths).astype(F32) * D)
    nh = head_bias.size // head_bias.shape[-1]
    ng = qk_gain.size // qk_gain.shape[-1]
    return (
        cat(results)[None, :own_len],
        mean_loss,
        hidden_g[None, :own_len],
        text_g[None],
        mine[:6],
        mine[6:10],
        mine[10],
        self_qkv_g,
        self_out_g,
        cross_qkv_g,
        cross_out_g,
        ffn_in_g,
        ffn_out_g,
        narrow[:nh].reshape(head_bias.shape),
        narrow[nh : nh + ng].reshape(qk_gain.shape),
        narrow[nh + ng :].reshape(ffn_bias.shape),
    )


def solution(mesh):
    in_specs = (
        P("dp", "mp", None),
        P("dp", "mp", None),
        P("dp", None, None),
        P(),
        P("dp", None, None),
        P("dp", "mp", None),
        P(None, ("dp", "mp")),
        P(None, ("dp", "mp")),
        P(("dp", "mp")),
        P(None, "dp", "mp"),
        P("mp", "dp"),
        P(None, "dp", "mp"),
        P("mp", "dp"),
        P("dp", "mp"),
        P("mp", "dp"),
        P(None, None, "mp", "dp"),
        P(None, None, "mp", "dp"),
        P("mp", "dp"),
    )
    out_specs = (
        P("dp", "mp", None),
        P(),
        P("dp", "mp", None),
        P("dp", "mp", None),
        P(None, ("dp", "mp")),
        P(None, ("dp", "mp")),
        P(("dp", "mp")),
        P(None, "dp", "mp"),
        P("mp", "dp"),
        P(None, "dp", "mp"),
        P("mp", "dp"),
        P("dp", "mp"),
        P("mp", "dp"),
        P(None, None, "mp", "dp"),
        P(None, None, "mp", "dp"),
        P("mp", "dp"),
    )
    return jax.shard_map(local, mesh=mesh, in_specs=in_specs, out_specs=out_specs, check_vma=False)
```

```python
import functools
import math

import jax
import jax.numpy as jnp
import numpy as np
from jax import lax
from jax.experimental import pallas as pl
from jax.experimental.pallas import tpu as pltpu
from jax.sharding import PartitionSpec as P

D = 1536
HD = 128
EPS = 1e-06
SCALE = HD ** (-0.5)
BF = jnp.bfloat16
F32 = jnp.float32
NEG = -1e30
SWAP = [(0, 1), (1, 0)]
VMEM_BYTES = 48 * 1024 * 1024


def rope_rates():
    pair_count = HD // 2
    third = pair_count // 3
    counts = [pair_count - 2 * third, third, third]
    rates = np.zeros((3, HD), np.float32)
    start = 0
    for axis_id, count in enumerate(counts):
        steps = np.arange(count, dtype=np.float32) / np.float32(count)
        values = np.exp(np.float32(-math.log(10000.0)) * steps).astype(np.float32)
        rates[axis_id, 2 * start : 2 * (start + count)] = np.repeat(values, 2)
        start += count
    return rates


def dot_nn(a, b):
    return lax.dot_general(a, b, (((1,), (0,)), ((), ())), preferred_element_type=F32)


def dot_nt(a, b):
    return lax.dot_general(a, b, (((1,), (1,)), ((), ())), preferred_element_type=F32)


def dot_tn(a, b):
    return lax.dot_general(a, b, (((0,), (0,)), ((), ())), preferred_element_type=F32)


def cost(flops, nbytes, trans=0):
    return pl.CostEstimate(flops=int(flops), bytes_accessed=int(nbytes), transcendentals=int(trans))


def params():
    return pltpu.CompilerParams(vmem_limit_bytes=VMEM_BYTES)


def turn(values):
    lane = lax.broadcasted_iota(jnp.int32, values.shape, 1)
    after = pltpu.roll(values, HD - 1, 1)
    before = pltpu.roll(values, 1, 1)
    return jnp.where(lane % 2 == 0, after, before)


def prep_kernel(qp, kp, qs, ks, qg, kg, cos, sin, q_out, k_out):
    c = cos[...]
    s = sin[...]
    for pre, scale, gain, out in ((qp, qs, qg, q_out), (kp, ks, kg, k_out)):
        v = pre[...] * scale[...] * gain[...]
        out[...] = (v * c + turn(v) * s).astype(BF)


def prep(qp, kp, qs, ks, qg, kg, cos, sin):
    rows, width = qp.shape
    head = pl.BlockSpec((rows, HD), lambda h: (0, h))
    col = pl.BlockSpec((rows, 1), lambda h: (0, 0))
    gain = pl.BlockSpec((1, HD), lambda h: (0, h))
    tab = pl.BlockSpec((rows, HD), lambda h: (0, 0))
    return pl.pallas_call(
        prep_kernel,
        grid=(width // HD,),
        in_specs=[head, head, col, col, gain, gain, tab, tab],
        out_specs=[head, head],
        out_shape=[jax.ShapeDtypeStruct((rows, width), BF)] * 2,
        compiler_params=params(),
        cost_estimate=cost(rows * width * 20, rows * width * 12),
        name="rope_prep",
    )(qp, kp, qs, ks, qg, kg, cos, sin)


def attend_kernel(masked, *refs):
    if masked:
        q, k, v, w, mask, out, lse, own, other = refs
    else:
        q, k, v, w, out, lse, own, other = refs
    st = dot_nt(k[...], q[...]) * SCALE
    if masked:
        st = st + mask[...]
    top = jnp.max(st, axis=0, keepdims=True)
    e = jnp.exp(st - top)
    total = jnp.sum(e, axis=0, keepdims=True)
    lse[0] = top + jnp.log(total)
    mixed = dot_tn(v[...], e.astype(BF)) * (1.0 / total)
    h = pl.program_id(0)
    out[:, pl.ds(pl.multiple_of(h * HD, HD), HD)] = mixed.T.astype(BF)

    @pl.when(h == pl.num_programs(0) - 1)
    def _():
        half = out.shape[0] // 2
        own[...] = dot_nt(out[:half], w[0])
        other[...] = dot_nt(out[half:], w[0]).astype(BF)


def attend(q, k, v, mask, weights, slab):
    nq, width = q.shape
    nk = k.shape[0]
    d = weights.shape[1]
    heads = width // HD
    qb = pl.BlockSpec((nq, HD), lambda h: (0, h))
    kb = pl.BlockSpec((nk, HD), lambda h: (0, h))
    ins = [qb, kb, kb, pl.BlockSpec((1, d, width), lambda h: (slab, 0, 0), pipeline_mode=pl.Buffered(1))]
    args = [q, k, v, weights]
    if mask is not None:
        ins.append(pl.BlockSpec((nk, 1), lambda h: (0, 0)))
        args.append(mask)
    return pl.pallas_call(
        functools.partial(attend_kernel, mask is not None),
        grid=(heads,),
        in_specs=ins,
        out_specs=[
            pl.BlockSpec((nq, width), lambda h: (0, 0)),
            pl.BlockSpec((1, 1, nq), lambda h: (h, 0, 0)),
            pl.BlockSpec((nq // 2, d), lambda h: (0, 0)),
            pl.BlockSpec((nq // 2, d), lambda h: (0, 0)),
        ],
        out_shape=[
            jax.ShapeDtypeStruct((nq, width), BF),
            jax.ShapeDtypeStruct((heads, 1, nq), F32),
            jax.ShapeDtypeStruct((nq // 2, d), F32),
            jax.ShapeDtypeStruct((nq // 2, d), BF),
        ],
        compiler_params=params(),
        cost_estimate=cost(4 * nq * nk * width * 3, 4 * nq * width + 4 * nk * width, nq * nk * heads),
        name="attend_fwd",
    )(*args)


def attend_back_kernel(self_form, *refs):
    if self_form:
        (q, k, v, do, lse, mask, qp, kp, qs, ks, qg, kg, cos, sin,
         dq_out, dk_out, dv_out, qdot, kdot, qgain, kgain) = refs
    else:
        q, k, v, do, lse, qp, qs, qg, dq_out, dk_out, dv_out, qdot, qgain = refs
    st = dot_nt(k[...], q[...]) * SCALE
    if self_form:
        st = st + mask[...]
    p = jnp.exp(st - lse[0])
    dp = dot_nt(v[...], do[...])
    inner = jnp.sum(dp * p, axis=0, keepdims=True)
    ds = (p * (dp - inner)).astype(BF)
    dv_out[...] = dot_nn(p.astype(BF), do[...]).astype(dv_out.dtype)
    dk = dot_nn(ds, q[...]) * SCALE
    dq = dot_tn(k[...], ds).T * SCALE
    sides = [(dq, qp, qs, qg, dq_out, qdot, qgain)]
    if self_form:
        dq = dq * cos[...] - turn(dq) * sin[...]
        dk = dk * cos[...] - turn(dk) * sin[...]
        sides = [(dq, qp, qs, qg, dq_out, qdot, qgain), (dk, kp, ks, kg, dk_out, kdot, kgain)]
    else:
        dk_out[...] = dk
    for grad, pre, scale, gain, out, dots, gains in sides:
        p_rows = pre[...]
        weighted = grad * gain[...]
        out[...] = weighted
        part = jnp.sum(weighted * p_rows, axis=1, keepdims=True)

        @pl.when(pl.program_id(0) == 0)
        def _():
            dots[...] = part

        @pl.when(pl.program_id(0) > 0)
        def _():
            dots[...] += part

        gains[...] = jnp.sum(grad * (p_rows * scale[...]), axis=0, keepdims=True)


def attend_back_self(q, k, v, do, lse, mask, qp, kp, qs, ks, qg, kg, cos, sin):
    n, width = q.shape
    heads = width // HD
    rows = pl.BlockSpec((n, HD), lambda h: (0, h))
    col = pl.BlockSpec((n, 1), lambda h: (0, 0))
    gain = pl.BlockSpec((1, HD), lambda h: (0, h))
    tab = pl.BlockSpec((n, HD), lambda h: (0, 0))
    lses = pl.BlockSpec((1, 1, n), lambda h: (h, 0, 0))
    full = jax.ShapeDtypeStruct((n, width), F32)
    cols = jax.ShapeDtypeStruct((n, 1), F32)
    gains = jax.ShapeDtypeStruct((1, width), F32)
    return pl.pallas_call(
        functools.partial(attend_back_kernel, True),
        grid=(heads,),
        in_specs=[rows, rows, rows, rows, lses, col, rows, rows, col, col, gain, gain, tab, tab],
        out_specs=[rows, rows, rows, col, col, gain, gain],
        out_shape=[full, full, jax.ShapeDtypeStruct((n, width), BF), cols, cols, gains, gains],
        compiler_params=params(),
        cost_estimate=cost(10 * n * n * width * 3, 26 * n * width, n * n * heads),
        name="attend_bwd_self",
    )(q, k, v, do, lse, mask, qp, kp, qs, ks, qg, kg, cos, sin)


def attend_back_cross(q, k, v, do, lse, qp, qs, qg):
    n, width = q.shape
    nk = k.shape[0]
    heads = width // HD
    rows = pl.BlockSpec((n, HD), lambda h: (0, h))
    keys = pl.BlockSpec((nk, HD), lambda h: (0, h))
    col = pl.BlockSpec((n, 1), lambda h: (0, 0))
    gain = pl.BlockSpec((1, HD), lambda h: (0, h))
    lses = pl.BlockSpec((1, 1, n), lambda h: (h, 0, 0))
    return pl.pallas_call(
        functools.partial(attend_back_kernel, False),
        grid=(heads,),
        in_specs=[rows, keys, keys, rows, lses, rows, col, gain],
        out_specs=[rows, keys, keys, col, gain],
        out_shape=[
            jax.ShapeDtypeStruct((n, width), F32),
            jax.ShapeDtypeStruct((nk, width), F32),
            jax.ShapeDtypeStruct((nk, width), F32),
            jax.ShapeDtypeStruct((n, 1), F32),
            jax.ShapeDtypeStruct((1, width), F32),
        ],
        compiler_params=params(),
        cost_estimate=cost(10 * n * nk * width * 3, 12 * n * width + 12 * nk * width, n * nk * heads),
        name="attend_bwd_cross",
    )(q, k, v, do, lse, qp, qs, qg)


def head_grads_kernel(plan, *refs):
    out = refs[-1]
    for i, terms in enumerate(plan):

        @pl.when(pl.program_id(0) == i)
        def _(terms=terms):
            total = None
            for a, b, lo, hi in terms:
                term = dot_tn(refs[a][...], refs[b][lo:hi])
                total = term if total is None else total + term
            out[0] = total.astype(BF)


def self_back_kernel(spans, *refs):
    n = 2 * len(spans)
    rows = refs[:n]
    weights = refs[n]
    heads = refs[n + 1 : n + 4]
    grads, part, other, acc = refs[n + 4 :]
    halves = [x for a, b in spans for x in ((a, (a + b) // 2), ((a + b) // 2, b))]
    for i in range(3):

        @pl.when(pl.program_id(0) == i)
        def _(i=i):
            total = None
            for x, (a, b) in zip(rows, halves):
                term = dot_tn(x[...], heads[i][a:b])
                total = term if total is None else total + term
            grads[0] = total.astype(BF)
            back = dot_nt(heads[i][...], weights[0])
            if i == 0:
                acc[...] = back
            elif i == 1:
                acc[...] += back
            else:
                back = acc[...] + back
                at = 0
                for a, b in spans:
                    half = (b - a) // 2
                    part[at : at + half] = back[a : a + half]
                    other[at : at + half] = back[a + half : b].astype(BF)
                    at += half


def self_back(rows, spans, weights, heads):
    n, width = heads[0].shape
    d = rows[0].shape[1]
    once = lambda x: pl.BlockSpec(x.shape, lambda i: (0, 0), pipeline_mode=pl.Buffered(1))
    return pl.pallas_call(
        functools.partial(self_back_kernel, spans),
        grid=(3,),
        in_specs=[once(x) for x in rows]
        + [pl.BlockSpec((1, d, width), lambda i: (i, 0, 0))]
        + [once(x) for x in heads],
        out_specs=[
            pl.BlockSpec((1, d, width), lambda i: (i, 0, 0)),
            pl.BlockSpec((n // 2, d), lambda i: (0, 0)),
            pl.BlockSpec((n // 2, d), lambda i: (0, 0)),
        ],
        out_shape=[
            jax.ShapeDtypeStruct((3, d, width), BF),
            jax.ShapeDtypeStruct((n // 2, d), F32),
            jax.ShapeDtypeStruct((n // 2, d), BF),
        ],
        scratch_shapes=[pltpu.VMEM((n, d), F32)],
        compiler_params=params(),
        cost_estimate=cost(12 * n * d * width, 30e6),
        name="self_back",
    )(*rows, weights, *heads)


def head_grads(products):
    arrays, plan = [], []

    def place(x):
        for i, y in enumerate(arrays):
            if x is y:
                return i
        arrays.append(x)
        return len(arrays) - 1

    for pairs in products:
        terms = []
        for pieces, b in pairs:
            at = 0
            for a in pieces:
                terms.append((place(a), place(b), at, at + a.shape[0]))
                at += a.shape[0]
        plan.append(terms)
    m, n = products[0][0][0][0].shape[1], products[0][0][1].shape[1]
    rows = sum(b.shape[0] for pairs in products for _, b in pairs)
    return pl.pallas_call(
        functools.partial(head_grads_kernel, plan),
        grid=(len(products),),
        in_specs=[
            pl.BlockSpec(x.shape, lambda i: (0, 0), pipeline_mode=pl.Buffered(1)) for x in arrays
        ],
        out_specs=pl.BlockSpec((1, m, n), lambda i: (i, 0, 0)),
        out_shape=jax.ShapeDtypeStruct((len(products), m, n), BF),
        compiler_params=params(),
        cost_estimate=cost(2 * rows * m * n, 2 * sum(x.size for x in arrays) + 2 * len(products) * m * n),
        name="head_grads",
    )(*arrays)


def tail_kernel(ndp, counts, nc, *refs):
    n = len(counts)
    g = refs[:n]
    state = refs[n : n + nc]
    unit = refs[n + nc : n + 2 * nc]
    (part, other, lns, ones, small, gsum, hgrad, small_out,
     mine, got, send, slot, ybuf, pbuf, stbuf, ubuf, vals, inbox,
     mine_sem, got_send, got_recv, ring_send, ring_recv, y_sem, load_sem, sum_send, sum_recv) = refs[n + 2 * nc :]
    chips = ndp // 2
    bits = ndp.bit_length() - 1
    dp = lax.axis_index("dp")
    mp = lax.axis_index("mp")
    core = lax.rem(dp, 2)
    chip = lax.div(dp, 2)
    odd = lax.rem(chip, 2)
    row = lax.div(chip, 2)
    place = row * (1 - odd) + (chips - 1 - row) * odd
    way = 1 - 2 * core

    def chip_at(shift):
        spot = lax.rem(place + way * shift + 2 * chips, chips)
        back = lax.div(spot, chips // 2)
        return 2 * spot * (1 - back) + (2 * (chips - 1 - spot) + 1) * back

    after = 2 * chip_at(1) + core
    before = 2 * chip_at(-1) + core
    mates = [dp + (1 - 2 * lax.rem(lax.div(dp, 1 << b), 2)) * (1 << b) for b in range(bits)]
    mesh_id = pl.DeviceIdType.MESH

    barrier = pltpu.get_barrier_semaphore()
    for device in (after, before, *mates):
        pl.semaphore_signal(barrier, inc=1, device_id=(device, mp), device_id_type=mesh_id)
    pl.semaphore_signal(barrier, inc=1, device_id=(dp, 1 - mp), device_id_type=mesh_id)
    pl.semaphore_wait(barrier, 3 + bits)

    def remote(src, dst, s_sem, r_sem, device):
        return pltpu.make_async_remote_copy(
            src_ref=src, dst_ref=dst, send_sem=s_sem, recv_sem=r_sem, device_id=device, device_id_type=mesh_id
        )

    starts = [sum(counts[:i]) for i in range(n)]
    total = sum(counts)
    cuts = [(0, (total + 1) // 2), ((total + 1) // 2, total)]

    def to_mate(s, i):
        return remote(
            g[i].at[:, chip_at(1 + s), 1 - core],
            got.at[s, pl.ds(starts[i], counts[i])],
            got_send.at[i, s],
            got_recv.at[i, s],
            (mates[0], mp),
        )

    def to_self(s, i):
        return pltpu.make_async_copy(
            g[i].at[:, chip_at(-1 - s), core], mine.at[s, pl.ds(starts[i], counts[i])], mine_sem.at[i, s]
        )

    def along(s, half):
        lo, hi = cuts[half]
        return remote(
            send.at[s, pl.ds(lo, hi - lo)],
            slot.at[s, pl.ds(lo, hi - lo)],
            ring_send.at[half, s],
            ring_recv.at[half, s],
            (after, mp),
        )

    def sum_copy(j):
        if j < bits:
            return remote(vals.at[j], inbox.at[j], sum_send.at[j], sum_recv.at[j], (mates[j], mp))
        return remote(
            vals.at[j, pl.ds(0, 16)], inbox.at[j, pl.ds(0, 16)], sum_send.at[j], sum_recv.at[j], (dp, 1 - mp)
        )

    y_copy = remote(other, ybuf, y_sem.at[0], y_sem.at[1], (dp, 1 - mp))
    for s in range(chips):
        for i in range(n):
            to_mate(s, i).start()
            to_self(s, i).start()
        if s == 0:
            y_copy.start()
    pairs = [(part, pbuf)]
    at = 0
    for st, un in zip(state, unit):
        span = pl.ds(at, st.shape[0])
        pairs += [(st, stbuf.at[span]), (un, ubuf.at[span])]
        at += st.shape[0]
    loads = [pltpu.make_async_copy(src, dst, load_sem.at[i]) for i, (src, dst) in enumerate(pairs)]
    for load in loads:
        load.start()

    def finish_rows():
        for load in loads:
            load.wait()
        y_copy.wait_recv()
        rows, width = pbuf.shape
        block = 80 if rows % 80 == 0 else 16
        gain = ones[...]

        def body(i, sums):
            at = pl.ds(pl.multiple_of(i * block, block), block)
            back = pbuf[at, :] + ybuf[at, :].astype(F32)
            z = ubuf[at, :]
            grad = back * gain
            mean_g = jnp.mean(grad, axis=1, keepdims=True)
            mean_gz = jnp.mean(grad * z, axis=1, keepdims=True)
            hgrad[at, :] = stbuf[at, :] + lns[at, :] * (grad - mean_g - z * mean_gz)
            return (
                sums[0] + jnp.sum(back, axis=0, keepdims=True),
                sums[1] + jnp.sum(back * z, axis=0, keepdims=True),
            )

        zero = jnp.zeros((1, width), F32)
        sums = lax.fori_loop(0, rows // block, body, (zero, zero))
        vals[0] = small[...]
        vals[0, 0:1, :] = sums[0]
        vals[0, 1:2, :] = sums[1]
        sum_copy(0).start()

    def sum_step(j):
        sum_copy(j).wait_recv()
        if j < bits:
            vals[j + 1] = vals[j] + inbox[j]
            sum_copy(j + 1).start()
        else:
            small_out[...] = vals[j]
            small_out[0:16, :] = vals[j, 0:16, :] + inbox[j, 0:16, :]

    first = min(2, chips - 1)
    done = 0
    for s in range(chips):
        for i in range(n):
            to_self(s, i).wait()
            to_mate(s, i).wait_recv()
        for half in range(2):
            lo, hi = cuts[half]
            value = mine[s, lo:hi].astype(F32) + got[s, lo:hi].astype(F32)
            if s > 0:
                along(s - 1, half).wait_recv()
                value = value + slot[s - 1, lo:hi].astype(F32)
            if s < chips - 1:
                send[s, lo:hi] = value.astype(BF)
                along(s, half).start()
            else:
                gsum[lo:hi] = value
        if s == first:
            finish_rows()
        elif s > first and done <= bits:
            sum_step(done)
            done += 1
    while done <= bits:
        sum_step(done)
        done += 1
    for s in range(chips):
        for i in range(n):
            to_mate(s, i).wait_send()
        if s < chips - 1:
            for half in range(2):
                along(s, half).wait_send()
    y_copy.wait_send()
    for j in range(bits + 1):
        sum_copy(j).wait_send()


def tail(ndp, grads, part, other, state, unit, lns, ones, small):
    chips = ndp // 2
    bits = ndp.bit_length() - 1
    split = [x.reshape(x.shape[0], chips, 2, x.shape[1] // ndp, x.shape[2]) for x in grads]
    counts = tuple(x.shape[0] for x in grads)
    total = sum(counts)
    r, w = split[0].shape[3:]
    rows, width = part.shape
    n = len(grads)
    nc = len(state)
    hbm = pl.BlockSpec(memory_space=pl.ANY)
    vmem = pl.BlockSpec(memory_space=pltpu.VMEM)
    dma = pltpu.SemaphoreType.DMA
    return pl.pallas_call(
        functools.partial(tail_kernel, ndp, counts, nc),
        in_specs=[hbm] * (n + 2 * nc) + [hbm, hbm, vmem, vmem, vmem],
        out_specs=[vmem] * 3,
        out_shape=[
            jax.ShapeDtypeStruct((total, r, w), F32),
            jax.ShapeDtypeStruct((rows, width), F32),
            jax.ShapeDtypeStruct(small.shape, F32),
        ],
        scratch_shapes=[
            pltpu.VMEM((chips, total, r, w), BF),
            pltpu.VMEM((chips, total, r, w), BF),
            pltpu.VMEM((chips - 1, total, r, w), BF),
            pltpu.VMEM((chips - 1, total, r, w), BF),
            pltpu.VMEM((rows, width), BF),
            pltpu.VMEM((rows, width), F32),
            pltpu.VMEM((rows, width), F32),
            pltpu.VMEM((rows, width), F32),
            pltpu.VMEM((bits + 1,) + small.shape, F32),
            pltpu.VMEM((bits + 1,) + small.shape, F32),
            dma((n, chips)),
            dma((n, chips)),
            dma((n, chips)),
            dma((2, chips - 1)),
            dma((2, chips - 1)),
            dma((2,)),
            dma((1 + 2 * nc,)),
            dma((bits + 1,)),
            dma((bits + 1,)),
        ],
        compiler_params=pltpu.CompilerParams(
            vmem_limit_bytes=58 * 1024 * 1024, collective_id=0, has_side_effects=True
        ),
        cost_estimate=cost(1e6, 1e6),
        name="tail_sums",
    )(*split, *state, *unit, part, other, lns, ones, small)


def normal(values):
    center = values - jnp.mean(values, axis=-1, keepdims=True)
    scale = lax.rsqrt(jnp.mean(center * center, axis=-1, keepdims=True) + EPS)
    return center * scale, scale


def normal_back(grad, unit, scale):
    mean_g = jnp.mean(grad, axis=-1, keepdims=True)
    mean_gz = jnp.mean(grad * unit, axis=-1, keepdims=True)
    return scale * (grad - mean_g - unit * mean_gz)


def swap(values):
    return lax.ppermute(values, "mp", SWAP)


def collect(own):
    pieces = [own, swap(own)]
    return jnp.concatenate(pieces, axis=0), pieces


def spread(partial):
    half = partial.shape[0] // 2
    return partial[:half] + swap(partial[half:].astype(BF)).astype(F32)


def halves(partial):
    half = partial.shape[0] // 2
    return partial[:half], swap(partial[half:].astype(BF))


def row_totals(own):
    half = own.shape[0] // 2
    return own + swap(jnp.concatenate([own[half:], own[:half]], axis=0))


def squares(values):
    return jnp.sum(values * values, axis=-1, keepdims=True)


def colsum(values):
    return jnp.sum(values, axis=0, dtype=F32)


def tie(*values):
    return lax.optimization_barrier(values)


def partners(ndp, bit):
    return [(i, i ^ (1 << bit)) for i in range(ndp)]


def gather_small(flat, ndp, dp, mp):
    rows = flat[None]
    got = swap(rows)
    rows = jnp.where(mp == 0, jnp.concatenate([rows, got]), jnp.concatenate([got, rows]))
    for bit in range(ndp.bit_length() - 1):
        got = lax.ppermute(rows, "dp", partners(ndp, bit))
        low = (dp >> bit) % 2 == 0
        rows = jnp.where(low, jnp.concatenate([rows, got]), jnp.concatenate([got, rows]))
    return rows


def chunks_of(padded):
    first = (padded // 2 + 15) // 16 * 16
    return [(0, first), (first, padded)]


def local(
    hidden,
    text_states,
    time_emb,
    lengths,
    positions,
    teacher,
    modulation,
    out_bias,
    norm3_gain,
    self_qkv,
    self_out,
    cross_qkv,
    cross_out,
    ffn_in,
    ffn_out,
    head_bias,
    qk_gain,
    ffn_bias,
):
    ndp = lax.axis_size("dp")
    dp = lax.axis_index("dp")
    mp = lax.axis_index("mp")
    own_len = hidden.shape[1]
    length = 2 * own_len
    padded = (own_len + 15) // 16 * 16
    pad = padded - own_len
    cuts = chunks_of(padded)

    f32_part = jnp.concatenate([modulation, out_bias, norm3_gain[None]], axis=0)
    hb = head_bias.reshape(-1, head_bias.shape[-1])
    qg = qk_gain.reshape(-1, qk_gain.shape[-1])
    low_part = jnp.concatenate([hb, qg, ffn_bias], axis=0).astype(F32)
    n_f32, w_f32 = f32_part.shape
    n_low, w_low = low_part.shape
    flat = jnp.concatenate([f32_part.reshape(-1), low_part.reshape(-1)])
    n_flat = flat.shape[0]
    flat_all = gather_small(jnp.pad(flat, (0, -n_flat % 128)), ndp, dp, mp)[:, :n_flat]
    f32_all = flat_all[:, : n_f32 * w_f32].reshape(2 * ndp, n_f32, w_f32)
    f32_all = f32_all.transpose(1, 0, 2).reshape(n_f32, -1)
    low_all = flat_all[:, n_f32 * w_f32 :].reshape(ndp, 2, n_low, w_low)
    low_all = lax.dynamic_index_in_dim(low_all, mp, 1, False)
    low_all = low_all.transpose(1, 0, 2).reshape(n_low, -1)
    mod_full = f32_all[:6]
    out_bias_full = f32_all[6:10]
    norm3_full = f32_all[10]
    hb_full = low_all[: hb.shape[0]].reshape(2, 3, -1)
    qg_full = low_all[hb.shape[0] : hb.shape[0] + qg.shape[0]].reshape(2, 2, 1, -1)
    ffn_bias_full = low_all[hb.shape[0] + qg.shape[0] :].reshape(-1)

    def whole(shards):
        return lax.all_gather(shards, "dp", axis=1, tiled=True)

    heads_w = whole(jnp.concatenate([self_qkv, self_out.T[None], cross_qkv, cross_out.T[None]]))
    self_w = heads_w[:4]
    cross_w = heads_w[4:]
    ffn_w = whole(jnp.stack([ffn_in, ffn_out.T]))
    self_out_t = self_w[3]
    cross_out_t = cross_w[3]
    ffn_in_w = ffn_w[0]
    ffn_out_t = ffn_w[1]

    signals = mod_full + time_emb[0]
    shift_attn, scale_attn, gate_attn, shift_ffn, scale_ffn, gate_ffn = [
        signals[i : i + 1] for i in range(6)
    ]
    clip_length = lax.dynamic_index_in_dim(lengths, dp, 0, False)

    def own_chunks(array):
        full = jnp.pad(array, ((0, pad), (0, 0)))
        return [full[a:b] for a, b in cuts]

    hid = own_chunks(hidden[0])
    teach = own_chunks(teacher[0])
    index = jnp.arange(padded)
    pos_pad = jnp.pad(positions[0].reshape(3, 2, own_len), ((0, 0), (0, 0), (0, pad)))

    def both(own, other):
        return jnp.concatenate([x[a:b] for a, b in cuts for x in (own, other)], axis=0)

    def slot_valid(half):
        return (index < own_len) & (half * own_len + index < clip_length)

    own_valid = slot_valid(mp)
    key_valid = both(own_valid, slot_valid(1 - mp))
    key_mask = jnp.where(key_valid, 0.0, NEG).astype(F32)[:, None]
    row_valid = [own_valid.astype(F32)[a:b, None] for a, b in cuts]
    pos_own = lax.dynamic_index_in_dim(pos_pad, mp, 1, False)
    pos_other = lax.dynamic_index_in_dim(pos_pad, 1 - mp, 1, False)
    rates = rope_rates()
    angle = sum(
        both(pos_own[i], pos_other[i]).astype(F32)[:, None] * rates[i][None, :] for i in range(3)
    )
    even = np.arange(HD) % 2 == 0
    cos = jnp.cos(angle)
    sin = jnp.sin(angle) * np.where(even, -1.0, 1.0).astype(np.float32)
    ends = np.cumsum([0] + [2 * (b - a) for a, b in cuts])
    spans = [(int(ends[i]), int(ends[i + 1])) for i in range(len(cuts))]
    nc = len(cuts)

    out_rows = [out_bias_full[i : i + 1] for i in range(4)]
    norm3_row = norm3_full[None]
    ffn_bias_row = ffn_bias_full[None]
    bias_rows = [hb_full[i, j][None] for i in range(2) for j in range(3)]
    late = [gate_attn, shift_ffn, scale_ffn, gate_ffn, norm3_row, ffn_bias_row, key_mask, cos, sin]
    late += out_rows + bias_rows + row_valid
    heads_w, *late = tie(heads_w, *late)
    gate_attn, shift_ffn, scale_ffn, gate_ffn, norm3_row, ffn_bias_row, key_mask, cos, sin = late[:9]
    out_rows, bias_rows, row_valid = late[9:13], late[13:19], late[19:]
    self_w = heads_w[:4]
    cross_w = heads_w[4:]
    self_out_t = heads_w[3]
    cross_out_t = heads_w[7]

    text_rows, text_pieces = collect(text_states[0])
    cross_kp = dot_nn(text_rows, cross_w[1]) + bias_rows[4]
    cross_v = (dot_nn(text_rows, cross_w[2]) + bias_rows[5]).astype(BF)
    cross_ks = row_totals(squares(cross_kp))
    cross_kr = lax.rsqrt(cross_ks / D + EPS)
    cross_k = (cross_kp * cross_kr * qg_full[1, 1]).astype(BF)

    res0, unit0, scale0, rows0 = [], [], [], []
    qp, kp, vv, qs, ks = [], [], [], [], []
    for c in range(nc):
        r = hid[c].astype(F32)
        z, s = normal(r)
        x = (z * (1.0 + scale_attn) + shift_attn).astype(BF)
        rows, pieces = collect(x)
        qc = dot_nn(rows, self_w[0]) + bias_rows[0]
        kc = dot_nn(rows, self_w[1]) + bias_rows[1]
        vc = (dot_nn(rows, self_w[2]) + bias_rows[2]).astype(BF)
        tot = row_totals(jnp.concatenate([squares(qc), squares(kc)], axis=1))
        res0.append(r)
        unit0.append(z)
        scale0.append(s)
        rows0 += pieces
        qp.append(qc)
        kp.append(kc)
        vv.append(vc)
        scales = lax.rsqrt(tot / D + EPS)
        qs.append(scales[:, 0:1])
        ks.append(scales[:, 1:2])
    qp, kp, vv = [jnp.concatenate(x, axis=0) for x in (qp, kp, vv)]
    qs, ks = [jnp.concatenate(x, axis=0) for x in (qs, ks)]
    self_q, self_k = prep(qp, kp, qs, ks, qg_full[0, 0], qg_full[0, 1], cos, sin)

    none = [None] * nc
    f, g = nc - 1, 0
    self_mixed, self_lse, branch0, unit1, scale1, after_self = [list(none) for _ in range(6)]
    cross_mixed, cross_lse, cross_q, cross_qp, cross_qs = [list(none) for _ in range(5)]
    rows1, rows2, unit2, scale2, after = [list(none) for _ in range(5)]

    def self_rows(c):
        a, b = spans[c]
        self_mixed[c], self_lse[c], own, other = attend(self_q[a:b], self_k, vv, key_mask, heads_w, 3)
        return own, swap(other)

    def cross_query(c, own, got):
        branch0[c] = own + got.astype(F32) + out_rows[1]
        after_self[c] = res0[c] + gate_attn * branch0[c]
        unit1[c], scale1[c] = normal(after_self[c])
        x = (unit1[c] * norm3_row + out_rows[0]).astype(BF)
        rows1[c] = [x, swap(x)]

    def cross_prepare(c, got=None):
        qc = dot_nn(jnp.concatenate(rows1[c], axis=0), heads_w[4]) + bias_rows[3]
        total = row_totals(squares(qc))
        if got is not None:
            qc, got = tie(qc, got)
        cross_qp[c] = qc
        cross_qs[c] = lax.rsqrt(total / D + EPS)
        cross_q[c] = (qc * cross_qs[c] * qg_full[1, 0]).astype(BF)
        return got

    def cross_attend(c):
        cross_mixed[c], cross_lse[c], own, other = attend(cross_q[c], cross_k, cross_v, None, heads_w, 7)
        return own, other

    def ffn_input(c, own, got):
        after[c] = after_self[c] + own + got.astype(F32) + out_rows[2]
        unit2[c], scale2[c] = normal(after[c])
        return (unit2[c] * (1.0 + scale_ffn) + shift_ffn).astype(BF)

    own_f, got_f = self_rows(f)
    own_g, got_g = self_rows(g)
    got_f, own_g = tie(got_f, own_g)
    cross_query(f, own_f, got_f)
    cross_query(g, own_g, got_g)
    cross_prepare(f)
    own_f, other_f = cross_attend(f)
    rows1[g][1], other_f = tie(rows1[g][1], other_f)
    got_f = swap(other_f)
    got_f = cross_prepare(g, got_f)
    x_f = ffn_input(f, own_f, got_f)
    cross_q[g], x_f = tie(cross_q[g], x_f)
    y_f = swap(x_f)
    own_g, other_g = cross_attend(g)
    y_f, own_g, other_g = tie(y_f, own_g, other_g)
    rows2[f] = jnp.concatenate([x_f, y_f], axis=0)
    got_g = swap(other_g)

    def cat(parts):
        return jnp.concatenate(parts, axis=0)

    def reduce_rows(full):
        return lax.psum_scatter(full, "dp", scatter_dimension=1, tiled=True)

    acts, slopes, results, errors, d_ffn, d_inners, d_afters, d_crosses = [list(none) for _ in range(8)]
    squares_of, gate_grads, ffn_backs = [list(none) for _ in range(3)]

    def inner_of(c):
        inner = dot_nn(rows2[c], ffn_in_w) + ffn_bias_row
        act, back = jax.vjp(functools.partial(jax.nn.gelu, approximate=True), inner)
        acts[c] = act.astype(BF)
        slopes[c] = back(jnp.ones_like(inner))[0].astype(BF)

    def loss_of(c, own, got):
        branch = own + got.astype(F32) + out_rows[3]
        result = after[c] + gate_ffn * branch
        results[c] = result.astype(BF)
        errors[c] = (result - teach[c].astype(F32)) * row_valid[c]
        d_ffn[c] = (gate_ffn * errors[c]).astype(BF)
        squares_of[c] = jnp.sum(errors[c] * errors[c])
        gate_grads[c] = colsum(branch * errors[c])

    def inner_back(c, rows):
        d_inners[c] = (dot_nn(rows, ffn_out_t) * slopes[c].astype(F32)).astype(BF)

    def after_back(c, own, got):
        back = own + got.astype(F32)
        ffn_backs[c] = back
        d_afters[c] = errors[c] + normal_back(back * (1.0 + scale_ffn), unit2[c], scale2[c])
        d_crosses[c] = d_afters[c].astype(BF)

    inner_of(f)
    got_g, acts[f] = tie(got_g, acts[f])
    x_g = ffn_input(g, own_g, got_g)
    acts[f], x_g = tie(acts[f], x_g)
    y_g = swap(x_g)
    branch_f = dot_nt(acts[f], ffn_out_t)
    y_g, branch_f = tie(y_g, branch_f)
    rows2[g] = jnp.concatenate([x_g, y_g], axis=0)
    own_f, got_f = halves(branch_f)
    inner_of(g)
    got_f, acts[g] = tie(got_f, acts[g])
    loss_of(f, own_f, got_f)
    acts[g], d_ffn[f] = tie(acts[g], d_ffn[f])
    d_f = swap(d_ffn[f])
    branch_g = dot_nt(acts[g], ffn_out_t)
    d_f, branch_g = tie(d_f, branch_g)
    own_g, got_g = halves(branch_g)
    d_f = cat([d_ffn[f], d_f])
    inner_back(f, d_f)
    d_inners[f], got_g = tie(d_inners[f], got_g)
    loss_of(g, own_g, got_g)
    d_inners[f], d_ffn[g] = tie(d_inners[f], d_ffn[g])
    d_g = swap(d_ffn[g])
    back_f = dot_nt(d_inners[f], ffn_in_w)
    d_g, back_f = tie(d_g, back_f)
    own_f, got_f = halves(back_f)
    d_g = cat([d_ffn[g], d_g])
    g_out = dot_tn(cat([d_f, d_g]), cat([acts[f], acts[g]])).astype(BF)
    got_f, d_g, g_out = tie(got_f, d_g, g_out)
    s_out = reduce_rows(g_out[None])
    inner_back(g, d_g)
    after_back(f, own_f, got_f)
    d_inners[g], d_crosses[f] = tie(d_inners[g], d_crosses[f])
    c_f = swap(d_crosses[f])
    back_g = dot_nt(d_inners[g], ffn_in_w)
    c_f, d_inners[g], back_g = tie(c_f, d_inners[g], back_g)
    own_g, got_g = halves(back_g)
    g_in = dot_tn(cat([rows2[f], rows2[g]]), cat([d_inners[f], d_inners[g]])).astype(BF)
    got_g, g_in = tie(got_g, g_in)
    after_back(g, own_g, got_g)
    c_f, d_crosses[g] = tie(c_f, d_crosses[g])
    c_g = swap(d_crosses[g])
    d_rows1 = list(none)
    d_rows1[f] = [d_crosses[f], c_f]
    d_rows1[g] = [d_crosses[g], c_g]
    err_sq = sum(squares_of)
    gate_ffn_grad = sum(gate_grads)
    bias3 = sum(colsum(x.astype(F32)) for x in d_ffn)
    bias2 = sum(colsum(x.astype(F32)) for x in d_crosses)
    ffn_b_grad = sum(colsum(x.astype(F32)) for x in d_inners)
    shift2 = sum(colsum(x) for x in ffn_backs)
    scale2_g = sum(colsum(x * z) for x, z in zip(ffn_backs, unit2))

    bias0 = bias1 = norm3_g = gate0_g = cross_qb = cross_qgain = cross_dk = cross_dv = 0.0
    d_qpres, d_rows0, state = [list(none) for _ in range(3)]
    for c in (f, g):
        d_mixed = dot_nn(cat(d_rows1[c]), cross_out_t).astype(BF)
        if c == g:
            d_mixed, q_back = tie(d_mixed, q_back)
            own_q, got_q = halves(q_back)
        dqw, dk, dv, qdot, qgain = attend_back_cross(
            cross_q[c], cross_k, cross_v, d_mixed, cross_lse[c], cross_qp[c], cross_qs[c], qg_full[1, 0]
        )
        if c == f:
            d_rows1[g][1], dqw, qdot = tie(d_rows1[g][1], dqw, qdot)
        else:
            got_q, dqw, qdot = tie(got_q, dqw, qdot)
        cross_dk = cross_dk + dk
        cross_dv = cross_dv + dv
        cross_qgain = cross_qgain + qgain[0]
        r = cross_qs[c]
        dot = row_totals(qdot)
        d_qpres[c] = (dqw * r - cross_qp[c] * (r * r * r * dot / D)).astype(BF)
        cross_qb = cross_qb + colsum(d_qpres[c].astype(F32))
        q_back = dot_nt(d_qpres[c], cross_w[0])
    backs = {f: own_q + got_q.astype(F32), g: spread(q_back)}
    for c in (f, g):
        back = backs[c]
        norm3_g = norm3_g + colsum(back * unit1[c])
        bias0 = bias0 + colsum(back)
        state[c] = d_afters[c] + normal_back(back * norm3_row, unit1[c], scale1[c])
        gate0_g = gate0_g + colsum(branch0[c] * state[c])
        d_self = (gate_attn * state[c]).astype(BF)
        bias1 = bias1 + colsum(d_self.astype(F32))
        d_rows0[c] = [d_self, swap(d_self)]

    cross_dkw = cross_dk * qg_full[1, 1]
    kdot = row_totals(jnp.sum(cross_dkw * cross_kp, axis=-1, keepdims=True))
    cross_kgain = colsum(cross_dk * cross_kp * cross_kr)
    d_kpre = (cross_dkw * cross_kr - cross_kp * (cross_kr**3 * kdot / D)).astype(BF)
    d_v = cross_dv.astype(BF)
    g_cross = head_grads(
        [
            list(zip(rows1, d_qpres)),
            [(text_pieces, d_kpre)],
            [(text_pieces, d_v)],
            list(zip(d_rows1, cross_mixed)),
        ]
    )
    own_text, got_text = halves(dot_nt(d_kpre, cross_w[1]) + dot_nt(d_v, cross_w[2]))
    cross_b = jnp.stack([cross_qb, colsum(d_kpre.astype(F32)), colsum(d_v.astype(F32))])

    g_self_out = head_grads([list(zip(d_rows0, self_mixed))])
    d_mixed = dot_nn(cat([x for pieces in d_rows0 for x in pieces]), self_out_t).astype(BF)
    d_mixed, g_self_out, g_cross, s_out, g_in = tie(d_mixed, g_self_out, g_cross, s_out, g_in)
    s_in = reduce_rows(g_in[None])
    ffn_out_g = s_out[0].astype(F32).T
    ffn_in_g = s_in[0].astype(F32)
    lse = jnp.concatenate(self_lse, axis=2)
    dqw, dkw, dv, qdot, kdot, self_qgain, self_kgain = attend_back_self(
        self_q, self_k, vv, d_mixed, lse, key_mask, qp, kp, qs, ks, qg_full[0, 0], qg_full[0, 1], cos, sin
    )
    dots = []
    for a, b in spans:
        dots.append(row_totals(jnp.concatenate([qdot[a:b], kdot[a:b]], axis=1)))
    dots = cat(dots)
    d_q = (dqw * qs - qp * (qs**3 * dots[:, 0:1] / D)).astype(BF)
    d_k = (dkw * ks - kp * (ks**3 * dots[:, 1:2] / D)).astype(BF)
    d_q, got_text = tie(d_q, got_text)
    text_g = own_text + got_text.astype(F32)
    text_g, d_k = tie(text_g, d_k)
    g_self, part, other = self_back(rows0, spans, heads_w, [d_q, d_k, dv])
    self_b = jnp.stack([colsum(g.astype(F32)) for g in (d_q, d_k, dv)])

    blank = jnp.zeros((D,), F32)
    wide = jnp.stack(
        [blank, blank, gate0_g, shift2, scale2_g, gate_ffn_grad, bias0, bias1, bias2, bias3, norm3_g]
        + [jnp.broadcast_to(err_sq, (D,))]
        + [blank] * 4
    )
    narrow = jnp.concatenate(
        [
            self_b.reshape(-1, HD),
            cross_b.reshape(-1, HD),
            jnp.stack([self_qgain[0], self_kgain[0], cross_qgain, cross_kgain]).reshape(-1, HD),
            ffn_b_grad.reshape(-1, HD),
        ],
        axis=0,
    )
    n_narrow = narrow.shape[0]
    narrow = jnp.pad(narrow.reshape(-1), (0, -narrow.size % (8 * D))).reshape(-1, D)
    sums, hidden_g, small = tail(
        ndp,
        [g_self, g_self_out, g_cross],
        part,
        other,
        state,
        unit0,
        cat(scale0),
        1.0 + scale_attn,
        jnp.concatenate([wide, narrow]),
    )
    self_qkv_g = sums[:3]
    self_out_g = sums[3].T
    cross_qkv_g = sums[4:7]
    cross_out_g = sums[7].T
    wide = small[:16]
    narrow = small[16:].reshape(-1)[: n_narrow * HD].reshape(n_narrow, HD)
    narrow = lax.dynamic_slice_in_dim(narrow, dp * w_low, w_low, 1)
    mine = lax.dynamic_slice_in_dim(wide, (dp * 2 + mp) * w_f32, w_f32, 1)
    mean_loss = wide[11, 0] / (jnp.sum(lengths).astype(F32) * D)
    nh = head_bias.size // head_bias.shape[-1]
    ng = qk_gain.size // qk_gain.shape[-1]
    return (
        cat(results)[None, :own_len],
        mean_loss,
        hidden_g[None, :own_len],
        text_g[None],
        mine[:6],
        mine[6:10],
        mine[10],
        self_qkv_g,
        self_out_g,
        cross_qkv_g,
        cross_out_g,
        ffn_in_g,
        ffn_out_g,
        narrow[:nh].reshape(head_bias.shape),
        narrow[nh : nh + ng].reshape(qk_gain.shape),
        narrow[nh + ng :].reshape(ffn_bias.shape),
    )


def solution(mesh):
    in_specs = (
        P("dp", "mp", None),
        P("dp", "mp", None),
        P("dp", None, None),
        P(),
        P("dp", None, None),
        P("dp", "mp", None),
        P(None, ("dp", "mp")),
        P(None, ("dp", "mp")),
        P(("dp", "mp")),
        P(None, "dp", "mp"),
        P("mp", "dp"),
        P(None, "dp", "mp"),
        P("mp", "dp"),
        P("dp", "mp"),
        P("mp", "dp"),
        P(None, None, "mp", "dp"),
        P(None, None, "mp", "dp"),
        P("mp", "dp"),
    )
    out_specs = (
        P("dp", "mp", None),
        P(),
        P("dp", "mp", None),
        P("dp", "mp", None),
        P(None, ("dp", "mp")),
        P(None, ("dp", "mp")),
        P(("dp", "mp")),
        P(None, "dp", "mp"),
        P("mp", "dp"),
        P(None, "dp", "mp"),
        P("mp", "dp"),
        P("dp", "mp"),
        P("mp", "dp"),
        P(None, None, "mp", "dp"),
        P(None, None, "mp", "dp"),
        P("mp", "dp"),
    )
    return jax.shard_map(local, mesh=mesh, in_specs=in_specs, out_specs=out_specs, check_vma=False)
```

```python
import functools
import math

import jax
import jax.numpy as jnp
import numpy as np
from jax import lax
from jax.experimental import pallas as pl
from jax.experimental.pallas import tpu as pltpu
from jax.sharding import PartitionSpec as P

D = 1536
HD = 128
EPS = 1e-06
SCALE = HD ** (-0.5)
BF = jnp.bfloat16
F32 = jnp.float32
NEG = -1e30
SWAP = [(0, 1), (1, 0)]
VMEM_BYTES = 48 * 1024 * 1024


def rope_rates():
    pair_count = HD // 2
    third = pair_count // 3
    counts = [pair_count - 2 * third, third, third]
    rates = np.zeros((3, HD), np.float32)
    start = 0
    for axis_id, count in enumerate(counts):
        steps = np.arange(count, dtype=np.float32) / np.float32(count)
        values = np.exp(np.float32(-math.log(10000.0)) * steps).astype(np.float32)
        rates[axis_id, 2 * start : 2 * (start + count)] = np.repeat(values, 2)
        start += count
    return rates


def dot_nn(a, b):
    return lax.dot_general(a, b, (((1,), (0,)), ((), ())), preferred_element_type=F32)


def dot_nt(a, b):
    return lax.dot_general(a, b, (((1,), (1,)), ((), ())), preferred_element_type=F32)


def dot_tn(a, b):
    return lax.dot_general(a, b, (((0,), (0,)), ((), ())), preferred_element_type=F32)


def cost(flops, nbytes, trans=0):
    return pl.CostEstimate(flops=int(flops), bytes_accessed=int(nbytes), transcendentals=int(trans))


def params():
    return pltpu.CompilerParams(vmem_limit_bytes=VMEM_BYTES)


def turn(values):
    lane = lax.broadcasted_iota(jnp.int32, values.shape, 1)
    after = pltpu.roll(values, HD - 1, 1)
    before = pltpu.roll(values, 1, 1)
    return jnp.where(lane % 2 == 0, after, before)


def prep_kernel(qp, kp, qs, ks, qg, kg, cos, sin, q_out, k_out):
    c = cos[...]
    s = sin[...]
    for pre, scale, gain, out in ((qp, qs, qg, q_out), (kp, ks, kg, k_out)):
        v = pre[...] * scale[...] * gain[...]
        out[...] = (v * c + turn(v) * s).astype(BF)


def prep(qp, kp, qs, ks, qg, kg, cos, sin):
    rows, width = qp.shape
    head = pl.BlockSpec((rows, HD), lambda h: (0, h))
    col = pl.BlockSpec((rows, 1), lambda h: (0, 0))
    gain = pl.BlockSpec((1, HD), lambda h: (0, h))
    tab = pl.BlockSpec((rows, HD), lambda h: (0, 0))
    return pl.pallas_call(
        prep_kernel,
        grid=(width // HD,),
        in_specs=[head, head, col, col, gain, gain, tab, tab],
        out_specs=[head, head],
        out_shape=[jax.ShapeDtypeStruct((rows, width), BF)] * 2,
        compiler_params=params(),
        cost_estimate=cost(rows * width * 20, rows * width * 12),
        name="rope_prep",
    )(qp, kp, qs, ks, qg, kg, cos, sin)


def attend_kernel(masked, *refs):
    if masked:
        q, k, v, w, mask, out, lse, own, other = refs
    else:
        q, k, v, w, out, lse, own, other = refs
    st = dot_nt(k[...], q[...]) * SCALE
    if masked:
        st = st + mask[...]
    top = jnp.max(st, axis=0, keepdims=True)
    e = jnp.exp(st - top)
    total = jnp.sum(e, axis=0, keepdims=True)
    lse[0] = top + jnp.log(total)
    mixed = dot_tn(v[...], e.astype(BF)) * (1.0 / total)
    h = pl.program_id(0)
    out[:, pl.ds(pl.multiple_of(h * HD, HD), HD)] = mixed.T.astype(BF)

    @pl.when(h == pl.num_programs(0) - 1)
    def _():
        half = out.shape[0] // 2
        own[...] = dot_nt(out[:half], w[0])
        other[...] = dot_nt(out[half:], w[0]).astype(BF)


def attend(q, k, v, mask, weights, slab):
    nq, width = q.shape
    nk = k.shape[0]
    d = weights.shape[1]
    heads = width // HD
    qb = pl.BlockSpec((nq, HD), lambda h: (0, h))
    kb = pl.BlockSpec((nk, HD), lambda h: (0, h))
    ins = [qb, kb, kb, pl.BlockSpec((1, d, width), lambda h: (slab, 0, 0), pipeline_mode=pl.Buffered(1))]
    args = [q, k, v, weights]
    if mask is not None:
        ins.append(pl.BlockSpec((nk, 1), lambda h: (0, 0)))
        args.append(mask)
    return pl.pallas_call(
        functools.partial(attend_kernel, mask is not None),
        grid=(heads,),
        in_specs=ins,
        out_specs=[
            pl.BlockSpec((nq, width), lambda h: (0, 0)),
            pl.BlockSpec((1, 1, nq), lambda h: (h, 0, 0)),
            pl.BlockSpec((nq // 2, d), lambda h: (0, 0)),
            pl.BlockSpec((nq // 2, d), lambda h: (0, 0)),
        ],
        out_shape=[
            jax.ShapeDtypeStruct((nq, width), BF),
            jax.ShapeDtypeStruct((heads, 1, nq), F32),
            jax.ShapeDtypeStruct((nq // 2, d), F32),
            jax.ShapeDtypeStruct((nq // 2, d), BF),
        ],
        compiler_params=params(),
        cost_estimate=cost(4 * nq * nk * width * 3, 4 * nq * width + 4 * nk * width, nq * nk * heads),
        name="attend_fwd",
    )(*args)


def attend_back_kernel(self_form, *refs):
    if self_form:
        (q, k, v, do, lse, mask, qp, kp, qs, ks, qg, kg, cos, sin,
         dq_out, dk_out, dv_out, qdot, kdot, qgain, kgain) = refs
    else:
        q, k, v, do, lse, qp, qs, qg, dq_out, dk_out, dv_out, qdot, qgain = refs
    st = dot_nt(k[...], q[...]) * SCALE
    if self_form:
        st = st + mask[...]
    p = jnp.exp(st - lse[0])
    dp = dot_nt(v[...], do[...])
    inner = jnp.sum(dp * p, axis=0, keepdims=True)
    ds = (p * (dp - inner)).astype(BF)
    dv_out[...] = dot_nn(p.astype(BF), do[...]).astype(dv_out.dtype)
    dk = dot_nn(ds, q[...]) * SCALE
    dq = dot_tn(k[...], ds).T * SCALE
    sides = [(dq, qp, qs, qg, dq_out, qdot, qgain)]
    if self_form:
        dq = dq * cos[...] - turn(dq) * sin[...]
        dk = dk * cos[...] - turn(dk) * sin[...]
        sides = [(dq, qp, qs, qg, dq_out, qdot, qgain), (dk, kp, ks, kg, dk_out, kdot, kgain)]
    else:
        dk_out[...] = dk
    for grad, pre, scale, gain, out, dots, gains in sides:
        p_rows = pre[...]
        weighted = grad * gain[...]
        out[...] = weighted
        part = jnp.sum(weighted * p_rows, axis=1, keepdims=True)

        @pl.when(pl.program_id(0) == 0)
        def _():
            dots[...] = part

        @pl.when(pl.program_id(0) > 0)
        def _():
            dots[...] += part

        gains[...] = jnp.sum(grad * (p_rows * scale[...]), axis=0, keepdims=True)


def attend_back_self(q, k, v, do, lse, mask, qp, kp, qs, ks, qg, kg, cos, sin):
    n, width = q.shape
    heads = width // HD
    rows = pl.BlockSpec((n, HD), lambda h: (0, h))
    col = pl.BlockSpec((n, 1), lambda h: (0, 0))
    gain = pl.BlockSpec((1, HD), lambda h: (0, h))
    tab = pl.BlockSpec((n, HD), lambda h: (0, 0))
    lses = pl.BlockSpec((1, 1, n), lambda h: (h, 0, 0))
    full = jax.ShapeDtypeStruct((n, width), F32)
    cols = jax.ShapeDtypeStruct((n, 1), F32)
    gains = jax.ShapeDtypeStruct((1, width), F32)
    return pl.pallas_call(
        functools.partial(attend_back_kernel, True),
        grid=(heads,),
        in_specs=[rows, rows, rows, rows, lses, col, rows, rows, col, col, gain, gain, tab, tab],
        out_specs=[rows, rows, rows, col, col, gain, gain],
        out_shape=[full, full, jax.ShapeDtypeStruct((n, width), BF), cols, cols, gains, gains],
        compiler_params=params(),
        cost_estimate=cost(10 * n * n * width * 3, 26 * n * width, n * n * heads),
        name="attend_bwd_self",
    )(q, k, v, do, lse, mask, qp, kp, qs, ks, qg, kg, cos, sin)


def attend_back_cross(q, k, v, do, lse, qp, qs, qg):
    n, width = q.shape
    nk = k.shape[0]
    heads = width // HD
    rows = pl.BlockSpec((n, HD), lambda h: (0, h))
    keys = pl.BlockSpec((nk, HD), lambda h: (0, h))
    col = pl.BlockSpec((n, 1), lambda h: (0, 0))
    gain = pl.BlockSpec((1, HD), lambda h: (0, h))
    lses = pl.BlockSpec((1, 1, n), lambda h: (h, 0, 0))
    return pl.pallas_call(
        functools.partial(attend_back_kernel, False),
        grid=(heads,),
        in_specs=[rows, keys, keys, rows, lses, rows, col, gain],
        out_specs=[rows, keys, keys, col, gain],
        out_shape=[
            jax.ShapeDtypeStruct((n, width), F32),
            jax.ShapeDtypeStruct((nk, width), F32),
            jax.ShapeDtypeStruct((nk, width), F32),
            jax.ShapeDtypeStruct((n, 1), F32),
            jax.ShapeDtypeStruct((1, width), F32),
        ],
        compiler_params=params(),
        cost_estimate=cost(10 * n * nk * width * 3, 12 * n * width + 12 * nk * width, n * nk * heads),
        name="attend_bwd_cross",
    )(q, k, v, do, lse, qp, qs, qg)


def head_grads_kernel(plan, *refs):
    out = refs[-1]
    for i, terms in enumerate(plan):

        @pl.when(pl.program_id(0) == i)
        def _(terms=terms):
            total = None
            for a, b, lo, hi in terms:
                term = dot_tn(refs[a][...], refs[b][lo:hi])
                total = term if total is None else total + term
            out[0] = total.astype(BF)


def self_back_kernel(spans, *refs):
    n = 2 * len(spans)
    rows = refs[:n]
    weights = refs[n]
    heads = refs[n + 1 : n + 4]
    grads, part, other, acc = refs[n + 4 :]
    halves = [x for a, b in spans for x in ((a, (a + b) // 2), ((a + b) // 2, b))]
    for i in range(3):

        @pl.when(pl.program_id(0) == i)
        def _(i=i):
            total = None
            for x, (a, b) in zip(rows, halves):
                term = dot_tn(x[...], heads[i][a:b])
                total = term if total is None else total + term
            grads[0] = total.astype(BF)
            back = dot_nt(heads[i][...], weights[0])
            if i == 0:
                acc[...] = back
            elif i == 1:
                acc[...] += back
            else:
                back = acc[...] + back
                at = 0
                for a, b in spans:
                    half = (b - a) // 2
                    part[at : at + half] = back[a : a + half]
                    other[at : at + half] = back[a + half : b].astype(BF)
                    at += half


def self_back(rows, spans, weights, heads):
    n, width = heads[0].shape
    d = rows[0].shape[1]
    once = lambda x: pl.BlockSpec(x.shape, lambda i: (0, 0), pipeline_mode=pl.Buffered(1))
    return pl.pallas_call(
        functools.partial(self_back_kernel, spans),
        grid=(3,),
        in_specs=[once(x) for x in rows]
        + [pl.BlockSpec((1, d, width), lambda i: (i, 0, 0))]
        + [once(x) for x in heads],
        out_specs=[
            pl.BlockSpec((1, d, width), lambda i: (i, 0, 0)),
            pl.BlockSpec((n // 2, d), lambda i: (0, 0)),
            pl.BlockSpec((n // 2, d), lambda i: (0, 0)),
        ],
        out_shape=[
            jax.ShapeDtypeStruct((3, d, width), BF),
            jax.ShapeDtypeStruct((n // 2, d), F32),
            jax.ShapeDtypeStruct((n // 2, d), BF),
        ],
        scratch_shapes=[pltpu.VMEM((n, d), F32)],
        compiler_params=params(),
        cost_estimate=cost(12 * n * d * width, 30e6),
        name="self_back",
    )(*rows, weights, *heads)


def head_grads(products):
    arrays, plan = [], []

    def place(x):
        for i, y in enumerate(arrays):
            if x is y:
                return i
        arrays.append(x)
        return len(arrays) - 1

    for pairs in products:
        terms = []
        for pieces, b in pairs:
            at = 0
            for a in pieces:
                terms.append((place(a), place(b), at, at + a.shape[0]))
                at += a.shape[0]
        plan.append(terms)
    m, n = products[0][0][0][0].shape[1], products[0][0][1].shape[1]
    rows = sum(b.shape[0] for pairs in products for _, b in pairs)
    return pl.pallas_call(
        functools.partial(head_grads_kernel, plan),
        grid=(len(products),),
        in_specs=[
            pl.BlockSpec(x.shape, lambda i: (0, 0), pipeline_mode=pl.Buffered(1)) for x in arrays
        ],
        out_specs=pl.BlockSpec((1, m, n), lambda i: (i, 0, 0)),
        out_shape=jax.ShapeDtypeStruct((len(products), m, n), BF),
        compiler_params=params(),
        cost_estimate=cost(2 * rows * m * n, 2 * sum(x.size for x in arrays) + 2 * len(products) * m * n),
        name="head_grads",
    )(*arrays)


def tail_kernel(ndp, counts, nc, *refs):
    n = len(counts)
    g = refs[:n]
    state = refs[n : n + nc]
    unit = refs[n + nc : n + 2 * nc]
    (part, other, lns, ones, small, gsum, hgrad, small_out,
     mine, got, send, slot, ybuf, pbuf, stbuf, ubuf, vals, inbox,
     mine_sem, got_send, got_recv, ring_send, ring_recv, y_sem, load_sem, sum_send, sum_recv) = refs[n + 2 * nc :]
    chips = ndp // 2
    bits = ndp.bit_length() - 1
    dp = lax.axis_index("dp")
    mp = lax.axis_index("mp")
    core = lax.rem(dp, 2)
    chip = lax.div(dp, 2)
    odd = lax.rem(chip, 2)
    row = lax.div(chip, 2)
    place = row * (1 - odd) + (chips - 1 - row) * odd
    way = 1 - 2 * core

    def chip_at(shift):
        spot = lax.rem(place + way * shift + 2 * chips, chips)
        back = lax.div(spot, chips // 2)
        return 2 * spot * (1 - back) + (2 * (chips - 1 - spot) + 1) * back

    after = 2 * chip_at(1) + core
    before = 2 * chip_at(-1) + core
    mates = [dp + (1 - 2 * lax.rem(lax.div(dp, 1 << b), 2)) * (1 << b) for b in range(bits)]
    mesh_id = pl.DeviceIdType.MESH

    barrier = pltpu.get_barrier_semaphore()
    for device in (after, before, *mates):
        pl.semaphore_signal(barrier, inc=1, device_id=(device, mp), device_id_type=mesh_id)
    pl.semaphore_signal(barrier, inc=1, device_id=(dp, 1 - mp), device_id_type=mesh_id)
    pl.semaphore_wait(barrier, 3 + bits)

    def remote(src, dst, s_sem, r_sem, device):
        return pltpu.make_async_remote_copy(
            src_ref=src, dst_ref=dst, send_sem=s_sem, recv_sem=r_sem, device_id=device, device_id_type=mesh_id
        )

    starts = [sum(counts[:i]) for i in range(n)]
    total = sum(counts)
    cuts = [(0, (total + 1) // 2), ((total + 1) // 2, total)]

    def to_mate(s, i):
        return remote(
            g[i].at[:, chip_at(1 + s), 1 - core],
            got.at[s, pl.ds(starts[i], counts[i])],
            got_send.at[i, s],
            got_recv.at[i, s],
            (mates[0], mp),
        )

    def to_self(s, i):
        return pltpu.make_async_copy(
            g[i].at[:, chip_at(-1 - s), core], mine.at[s, pl.ds(starts[i], counts[i])], mine_sem.at[i, s]
        )

    def along(s, half):
        lo, hi = cuts[half]
        return remote(
            send.at[s, pl.ds(lo, hi - lo)],
            slot.at[s, pl.ds(lo, hi - lo)],
            ring_send.at[half, s],
            ring_recv.at[half, s],
            (after, mp),
        )

    def sum_copy(j):
        if j < bits:
            return remote(vals.at[j], inbox.at[j], sum_send.at[j], sum_recv.at[j], (mates[j], mp))
        return remote(
            vals.at[j, pl.ds(0, 16)], inbox.at[j, pl.ds(0, 16)], sum_send.at[j], sum_recv.at[j], (dp, 1 - mp)
        )

    y_copy = remote(other, ybuf, y_sem.at[0], y_sem.at[1], (dp, 1 - mp))
    for s in range(chips):
        for i in range(n):
            to_mate(s, i).start()
            to_self(s, i).start()
        if s == 0:
            y_copy.start()
    pairs = [(part, pbuf)]
    at = 0
    for st, un in zip(state, unit):
        span = pl.ds(at, st.shape[0])
        pairs += [(st, stbuf.at[span]), (un, ubuf.at[span])]
        at += st.shape[0]
    loads = [pltpu.make_async_copy(src, dst, load_sem.at[i]) for i, (src, dst) in enumerate(pairs)]
    for load in loads:
        load.start()

    def finish_rows():
        for load in loads:
            load.wait()
        y_copy.wait_recv()
        rows, width = pbuf.shape
        block = 80 if rows % 80 == 0 else 16
        gain = ones[...]

        def body(i, sums):
            at = pl.ds(pl.multiple_of(i * block, block), block)
            back = pbuf[at, :] + ybuf[at, :].astype(F32)
            z = ubuf[at, :]
            grad = back * gain
            mean_g = jnp.mean(grad, axis=1, keepdims=True)
            mean_gz = jnp.mean(grad * z, axis=1, keepdims=True)
            hgrad[at, :] = stbuf[at, :] + lns[at, :] * (grad - mean_g - z * mean_gz)
            return (
                sums[0] + jnp.sum(back, axis=0, keepdims=True),
                sums[1] + jnp.sum(back * z, axis=0, keepdims=True),
            )

        zero = jnp.zeros((1, width), F32)
        sums = lax.fori_loop(0, rows // block, body, (zero, zero))
        vals[0] = small[...]
        vals[0, 0:1, :] = sums[0]
        vals[0, 1:2, :] = sums[1]
        sum_copy(0).start()

    def sum_step(j):
        sum_copy(j).wait_recv()
        if j < bits:
            vals[j + 1] = vals[j] + inbox[j]
            sum_copy(j + 1).start()
        else:
            small_out[...] = vals[j]
            small_out[0:16, :] = vals[j, 0:16, :] + inbox[j, 0:16, :]

    first = min(2, chips - 1)
    done = 0
    for s in range(chips):
        for i in range(n):
            to_self(s, i).wait()
            to_mate(s, i).wait_recv()
        for half in range(2):
            lo, hi = cuts[half]
            value = mine[s, lo:hi].astype(F32) + got[s, lo:hi].astype(F32)
            if s > 0:
                along(s - 1, half).wait_recv()
                value = value + slot[s - 1, lo:hi].astype(F32)
            if s < chips - 1:
                send[s, lo:hi] = value.astype(BF)
                along(s, half).start()
            else:
                gsum[lo:hi] = value
        if s == first:
            finish_rows()
        elif s > first and done <= bits:
            sum_step(done)
            done += 1
    while done <= bits:
        sum_step(done)
        done += 1
    for s in range(chips):
        for i in range(n):
            to_mate(s, i).wait_send()
        if s < chips - 1:
            for half in range(2):
                along(s, half).wait_send()
    y_copy.wait_send()
    for j in range(bits + 1):
        sum_copy(j).wait_send()


def tail(ndp, grads, part, other, state, unit, lns, ones, small):
    chips = ndp // 2
    bits = ndp.bit_length() - 1
    split = [x.reshape(x.shape[0], chips, 2, x.shape[1] // ndp, x.shape[2]) for x in grads]
    counts = tuple(x.shape[0] for x in grads)
    total = sum(counts)
    r, w = split[0].shape[3:]
    rows, width = part.shape
    n = len(grads)
    nc = len(state)
    hbm = pl.BlockSpec(memory_space=pl.ANY)
    vmem = pl.BlockSpec(memory_space=pltpu.VMEM)
    dma = pltpu.SemaphoreType.DMA
    return pl.pallas_call(
        functools.partial(tail_kernel, ndp, counts, nc),
        in_specs=[hbm] * (n + 2 * nc) + [hbm, hbm, vmem, vmem, vmem],
        out_specs=[vmem] * 3,
        out_shape=[
            jax.ShapeDtypeStruct((total, r, w), F32),
            jax.ShapeDtypeStruct((rows, width), F32),
            jax.ShapeDtypeStruct(small.shape, F32),
        ],
        scratch_shapes=[
            pltpu.VMEM((chips, total, r, w), BF),
            pltpu.VMEM((chips, total, r, w), BF),
            pltpu.VMEM((chips - 1, total, r, w), BF),
            pltpu.VMEM((chips - 1, total, r, w), BF),
            pltpu.VMEM((rows, width), BF),
            pltpu.VMEM((rows, width), F32),
            pltpu.VMEM((rows, width), F32),
            pltpu.VMEM((rows, width), F32),
            pltpu.VMEM((bits + 1,) + small.shape, F32),
            pltpu.VMEM((bits + 1,) + small.shape, F32),
            dma((n, chips)),
            dma((n, chips)),
            dma((n, chips)),
            dma((2, chips - 1)),
            dma((2, chips - 1)),
            dma((2,)),
            dma((1 + 2 * nc,)),
            dma((bits + 1,)),
            dma((bits + 1,)),
        ],
        compiler_params=pltpu.CompilerParams(
            vmem_limit_bytes=58 * 1024 * 1024, collective_id=0, has_side_effects=True
        ),
        cost_estimate=cost(1e6, 1e6),
        name="tail_sums",
    )(*split, *state, *unit, part, other, lns, ones, small)


def normal(values):
    center = values - jnp.mean(values, axis=-1, keepdims=True)
    scale = lax.rsqrt(jnp.mean(center * center, axis=-1, keepdims=True) + EPS)
    return center * scale, scale


def normal_back(grad, unit, scale):
    mean_g = jnp.mean(grad, axis=-1, keepdims=True)
    mean_gz = jnp.mean(grad * unit, axis=-1, keepdims=True)
    return scale * (grad - mean_g - unit * mean_gz)


def swap(values):
    return lax.ppermute(values, "mp", SWAP)


def collect(own):
    pieces = [own, swap(own)]
    return jnp.concatenate(pieces, axis=0), pieces


def spread(partial):
    half = partial.shape[0] // 2
    return partial[:half] + swap(partial[half:].astype(BF)).astype(F32)


def halves(partial):
    half = partial.shape[0] // 2
    return partial[:half], swap(partial[half:].astype(BF))


def row_totals(own):
    half = own.shape[0] // 2
    return own + swap(jnp.concatenate([own[half:], own[:half]], axis=0))


def squares(values):
    return jnp.sum(values * values, axis=-1, keepdims=True)


def colsum(values):
    return jnp.sum(values, axis=0, dtype=F32)


def tie(*values):
    return lax.optimization_barrier(values)


def partners(ndp, bit):
    return [(i, i ^ (1 << bit)) for i in range(ndp)]


def gather_small(flat, ndp, dp, mp):
    rows = flat[None]
    got = swap(rows)
    rows = jnp.where(mp == 0, jnp.concatenate([rows, got]), jnp.concatenate([got, rows]))
    for bit in range(ndp.bit_length() - 1):
        got = lax.ppermute(rows, "dp", partners(ndp, bit))
        low = (dp >> bit) % 2 == 0
        rows = jnp.where(low, jnp.concatenate([rows, got]), jnp.concatenate([got, rows]))
    return rows


def chunks_of(padded):
    first = (padded // 2 + 15) // 16 * 16
    return [(0, first), (first, padded)]


def local(
    hidden,
    text_states,
    time_emb,
    lengths,
    positions,
    teacher,
    modulation,
    out_bias,
    norm3_gain,
    self_qkv,
    self_out,
    cross_qkv,
    cross_out,
    ffn_in,
    ffn_out,
    head_bias,
    qk_gain,
    ffn_bias,
):
    ndp = lax.axis_size("dp")
    dp = lax.axis_index("dp")
    mp = lax.axis_index("mp")
    own_len = hidden.shape[1]
    length = 2 * own_len
    padded = (own_len + 15) // 16 * 16
    pad = padded - own_len
    cuts = chunks_of(padded)

    f32_part = jnp.concatenate([modulation, out_bias, norm3_gain[None]], axis=0)
    hb = head_bias.reshape(-1, head_bias.shape[-1])
    qg = qk_gain.reshape(-1, qk_gain.shape[-1])
    low_part = jnp.concatenate([hb, qg, ffn_bias], axis=0).astype(F32)
    n_f32, w_f32 = f32_part.shape
    n_low, w_low = low_part.shape
    flat = jnp.concatenate([f32_part.reshape(-1), low_part.reshape(-1)])
    n_flat = flat.shape[0]
    flat_all = gather_small(jnp.pad(flat, (0, -n_flat % 128)), ndp, dp, mp)[:, :n_flat]
    f32_all = flat_all[:, : n_f32 * w_f32].reshape(2 * ndp, n_f32, w_f32)
    f32_all = f32_all.transpose(1, 0, 2).reshape(n_f32, -1)
    low_all = flat_all[:, n_f32 * w_f32 :].reshape(ndp, 2, n_low, w_low)
    low_all = lax.dynamic_index_in_dim(low_all, mp, 1, False)
    low_all = low_all.transpose(1, 0, 2).reshape(n_low, -1)
    mod_full = f32_all[:6]
    out_bias_full = f32_all[6:10]
    norm3_full = f32_all[10]
    hb_full = low_all[: hb.shape[0]].reshape(2, 3, -1)
    qg_full = low_all[hb.shape[0] : hb.shape[0] + qg.shape[0]].reshape(2, 2, 1, -1)
    ffn_bias_full = low_all[hb.shape[0] + qg.shape[0] :].reshape(-1)

    def whole(shards):
        return lax.all_gather(shards, "dp", axis=1, tiled=True)

    heads_w = whole(jnp.concatenate([self_qkv, self_out.T[None], cross_qkv, cross_out.T[None]]))
    self_w = heads_w[:4]
    cross_w = heads_w[4:]
    ffn_w = whole(jnp.stack([ffn_in, ffn_out.T]))
    self_out_t = self_w[3]
    cross_out_t = cross_w[3]
    ffn_in_w = ffn_w[0]
    ffn_out_t = ffn_w[1]

    signals = mod_full + time_emb[0]
    shift_attn, scale_attn, gate_attn, shift_ffn, scale_ffn, gate_ffn = [
        signals[i : i + 1] for i in range(6)
    ]
    clip_length = lax.dynamic_index_in_dim(lengths, dp, 0, False)

    def own_chunks(array):
        full = jnp.pad(array, ((0, pad), (0, 0)))
        return [full[a:b] for a, b in cuts]

    hid = own_chunks(hidden[0])
    teach = own_chunks(teacher[0])
    index = jnp.arange(padded)
    pos_pad = jnp.pad(positions[0].reshape(3, 2, own_len), ((0, 0), (0, 0), (0, pad)))

    def both(own, other):
        return jnp.concatenate([x[a:b] for a, b in cuts for x in (own, other)], axis=0)

    def slot_valid(half):
        return (index < own_len) & (half * own_len + index < clip_length)

    own_valid = slot_valid(mp)
    key_valid = both(own_valid, slot_valid(1 - mp))
    key_mask = jnp.where(key_valid, 0.0, NEG).astype(F32)[:, None]
    row_valid = [own_valid.astype(F32)[a:b, None] for a, b in cuts]
    pos_own = lax.dynamic_index_in_dim(pos_pad, mp, 1, False)
    pos_other = lax.dynamic_index_in_dim(pos_pad, 1 - mp, 1, False)
    rates = rope_rates()
    angle = sum(
        both(pos_own[i], pos_other[i]).astype(F32)[:, None] * rates[i][None, :] for i in range(3)
    )
    even = np.arange(HD) % 2 == 0
    cos = jnp.cos(angle)
    sin = jnp.sin(angle) * np.where(even, -1.0, 1.0).astype(np.float32)
    ends = np.cumsum([0] + [2 * (b - a) for a, b in cuts])
    spans = [(int(ends[i]), int(ends[i + 1])) for i in range(len(cuts))]
    nc = len(cuts)

    out_rows = [out_bias_full[i : i + 1] for i in range(4)]
    norm3_row = norm3_full[None]
    ffn_bias_row = ffn_bias_full[None]
    bias_rows = [hb_full[i, j][None] for i in range(2) for j in range(3)]
    late = [gate_attn, shift_ffn, scale_ffn, gate_ffn, norm3_row, ffn_bias_row, key_mask, cos, sin]
    late += out_rows + bias_rows + row_valid
    heads_w, *late = tie(heads_w, *late)
    gate_attn, shift_ffn, scale_ffn, gate_ffn, norm3_row, ffn_bias_row, key_mask, cos, sin = late[:9]
    out_rows, bias_rows, row_valid = late[9:13], late[13:19], late[19:]
    self_w = heads_w[:4]
    cross_w = heads_w[4:]
    self_out_t = heads_w[3]
    cross_out_t = heads_w[7]

    text_rows, text_pieces = collect(text_states[0])

    res0, unit0, scale0, rows0 = [], [], [], []
    qp, kp, vv, qs, ks = [], [], [], [], []
    for c in range(nc):
        r = hid[c].astype(F32)
        z, s = normal(r)
        x = (z * (1.0 + scale_attn) + shift_attn).astype(BF)
        rows, pieces = collect(x)
        qc = dot_nn(rows, self_w[0]) + bias_rows[0]
        kc = dot_nn(rows, self_w[1]) + bias_rows[1]
        vc = (dot_nn(rows, self_w[2]) + bias_rows[2]).astype(BF)
        tot = row_totals(jnp.concatenate([squares(qc), squares(kc)], axis=1))
        res0.append(r)
        unit0.append(z)
        scale0.append(s)
        rows0 += pieces
        qp.append(qc)
        kp.append(kc)
        vv.append(vc)
        scales = lax.rsqrt(tot / D + EPS)
        qs.append(scales[:, 0:1])
        ks.append(scales[:, 1:2])
    qp, kp, vv = [jnp.concatenate(x, axis=0) for x in (qp, kp, vv)]
    qs, ks = [jnp.concatenate(x, axis=0) for x in (qs, ks)]
    self_q, self_k = prep(qp, kp, qs, ks, qg_full[0, 0], qg_full[0, 1], cos, sin)

    none = [None] * nc
    f, g = nc - 1, 0
    self_mixed, self_lse, branch0, unit1, scale1, after_self = [list(none) for _ in range(6)]
    cross_mixed, cross_lse, cross_q, cross_qp, cross_qs = [list(none) for _ in range(5)]
    rows1, rows2, unit2, scale2, after = [list(none) for _ in range(5)]

    def self_rows(c):
        a, b = spans[c]
        self_mixed[c], self_lse[c], own, other = attend(self_q[a:b], self_k, vv, key_mask, heads_w, 3)
        return own, swap(other)

    def cross_query(c, own, got):
        branch0[c] = own + got.astype(F32) + out_rows[1]
        after_self[c] = res0[c] + gate_attn * branch0[c]
        unit1[c], scale1[c] = normal(after_self[c])
        x = (unit1[c] * norm3_row + out_rows[0]).astype(BF)
        rows1[c] = [x, swap(x)]

    def cross_prepare(c, got=None):
        qc = dot_nn(jnp.concatenate(rows1[c], axis=0), heads_w[4]) + bias_rows[3]
        if got is not None:
            qc, got = tie(qc, got)
        cross_qp[c] = qc
        cross_qs[c] = lax.rsqrt(row_totals(squares(qc)) / D + EPS)
        cross_q[c] = (qc * cross_qs[c] * qg_full[1, 0]).astype(BF)
        return got

    def cross_attend(c):
        cross_mixed[c], cross_lse[c], own, other = attend(cross_q[c], cross_k, cross_v, None, heads_w, 7)
        return own, other

    def ffn_input(c, own, got):
        after[c] = after_self[c] + own + got.astype(F32) + out_rows[2]
        unit2[c], scale2[c] = normal(after[c])
        return (unit2[c] * (1.0 + scale_ffn) + shift_ffn).astype(BF)

    own_f, got_f = self_rows(f)
    own_g, got_g = self_rows(g)
    got_f, own_g = tie(got_f, own_g)
    cross_query(f, own_f, got_f)
    rows1[f][0], text_rows = tie(rows1[f][0], text_rows)
    cross_query(g, own_g, got_g)
    cross_kp = dot_nn(text_rows, cross_w[1]) + bias_rows[4]
    cross_v = (dot_nn(text_rows, cross_w[2]) + bias_rows[5]).astype(BF)
    rows1[f][1], cross_kp, cross_v = tie(rows1[f][1], cross_kp, cross_v)
    cross_ks = row_totals(squares(cross_kp))
    cross_kr = lax.rsqrt(cross_ks / D + EPS)
    cross_k = (cross_kp * cross_kr * qg_full[1, 1]).astype(BF)
    cross_prepare(f)
    own_f, other_f = cross_attend(f)
    rows1[g][1], other_f = tie(rows1[g][1], other_f)
    got_f = swap(other_f)
    got_f = cross_prepare(g, got_f)
    x_f = ffn_input(f, own_f, got_f)
    cross_q[g], x_f = tie(cross_q[g], x_f)
    y_f = swap(x_f)
    own_g, other_g = cross_attend(g)
    y_f, own_g, other_g = tie(y_f, own_g, other_g)
    rows2[f] = jnp.concatenate([x_f, y_f], axis=0)
    got_g = swap(other_g)

    def cat(parts):
        return jnp.concatenate(parts, axis=0)

    def reduce_rows(full):
        return lax.psum_scatter(full, "dp", scatter_dimension=1, tiled=True)

    acts, slopes, results, errors, d_ffn, d_inners, d_afters, d_crosses = [list(none) for _ in range(8)]
    squares_of, gate_grads, ffn_backs = [list(none) for _ in range(3)]

    def inner_of(c):
        inner = dot_nn(rows2[c], ffn_in_w) + ffn_bias_row
        act, back = jax.vjp(functools.partial(jax.nn.gelu, approximate=True), inner)
        acts[c] = act.astype(BF)
        slopes[c] = back(jnp.ones_like(inner))[0].astype(BF)

    def loss_of(c, own, got):
        branch = own + got.astype(F32) + out_rows[3]
        result = after[c] + gate_ffn * branch
        results[c] = result.astype(BF)
        errors[c] = (result - teach[c].astype(F32)) * row_valid[c]
        d_ffn[c] = (gate_ffn * errors[c]).astype(BF)
        squares_of[c] = jnp.sum(errors[c] * errors[c])
        gate_grads[c] = colsum(branch * errors[c])

    def inner_back(c, rows):
        d_inners[c] = (dot_nn(rows, ffn_out_t) * slopes[c].astype(F32)).astype(BF)

    def after_back(c, own, got):
        back = own + got.astype(F32)
        ffn_backs[c] = back
        d_afters[c] = errors[c] + normal_back(back * (1.0 + scale_ffn), unit2[c], scale2[c])
        d_crosses[c] = d_afters[c].astype(BF)

    inner_of(f)
    got_g, acts[f] = tie(got_g, acts[f])
    x_g = ffn_input(g, own_g, got_g)
    acts[f], x_g = tie(acts[f], x_g)
    y_g = swap(x_g)
    branch_f = dot_nt(acts[f], ffn_out_t)
    y_g, branch_f = tie(y_g, branch_f)
    rows2[g] = jnp.concatenate([x_g, y_g], axis=0)
    own_f, got_f = halves(branch_f)
    inner_of(g)
    got_f, acts[g] = tie(got_f, acts[g])
    loss_of(f, own_f, got_f)
    acts[g], d_ffn[f] = tie(acts[g], d_ffn[f])
    d_f = swap(d_ffn[f])
    branch_g = dot_nt(acts[g], ffn_out_t)
    d_f, branch_g = tie(d_f, branch_g)
    own_g, got_g = halves(branch_g)
    d_f = cat([d_ffn[f], d_f])
    inner_back(f, d_f)
    d_inners[f], got_g = tie(d_inners[f], got_g)
    loss_of(g, own_g, got_g)
    d_inners[f], d_ffn[g] = tie(d_inners[f], d_ffn[g])
    d_g = swap(d_ffn[g])
    back_f = dot_nt(d_inners[f], ffn_in_w)
    d_g, back_f = tie(d_g, back_f)
    own_f, got_f = halves(back_f)
    d_g = cat([d_ffn[g], d_g])
    g_out = dot_tn(cat([d_f, d_g]), cat([acts[f], acts[g]])).astype(BF)
    got_f, d_g, g_out = tie(got_f, d_g, g_out)
    s_out = reduce_rows(g_out[None])
    inner_back(g, d_g)
    after_back(f, own_f, got_f)
    d_inners[g], d_crosses[f] = tie(d_inners[g], d_crosses[f])
    c_f = swap(d_crosses[f])
    back_g = dot_nt(d_inners[g], ffn_in_w)
    c_f, d_inners[g], back_g = tie(c_f, d_inners[g], back_g)
    own_g, got_g = halves(back_g)
    g_in = dot_tn(cat([rows2[f], rows2[g]]), cat([d_inners[f], d_inners[g]])).astype(BF)
    got_g, g_in = tie(got_g, g_in)
    after_back(g, own_g, got_g)
    c_f, d_crosses[g] = tie(c_f, d_crosses[g])
    c_g = swap(d_crosses[g])
    d_rows1 = list(none)
    d_rows1[f] = [d_crosses[f], c_f]
    d_rows1[g] = [d_crosses[g], c_g]
    err_sq = sum(squares_of)
    gate_ffn_grad = sum(gate_grads)
    bias3 = sum(colsum(x.astype(F32)) for x in d_ffn)
    bias2 = sum(colsum(x.astype(F32)) for x in d_crosses)
    ffn_b_grad = sum(colsum(x.astype(F32)) for x in d_inners)
    shift2 = sum(colsum(x) for x in ffn_backs)
    scale2_g = sum(colsum(x * z) for x, z in zip(ffn_backs, unit2))

    bias0 = bias1 = norm3_g = gate0_g = cross_qb = cross_qgain = cross_dk = cross_dv = 0.0
    d_qpres, d_rows0, state = [list(none) for _ in range(3)]
    for c in (f, g):
        d_mixed = dot_nn(cat(d_rows1[c]), cross_out_t).astype(BF)
        if c == g:
            d_mixed, q_back = tie(d_mixed, q_back)
            own_q, got_q = halves(q_back)
        dqw, dk, dv, qdot, qgain = attend_back_cross(
            cross_q[c], cross_k, cross_v, d_mixed, cross_lse[c], cross_qp[c], cross_qs[c], qg_full[1, 0]
        )
        if c == f:
            d_rows1[g][1], dqw, qdot = tie(d_rows1[g][1], dqw, qdot)
        else:
            got_q, dqw, qdot = tie(got_q, dqw, qdot)
        cross_dk = cross_dk + dk
        cross_dv = cross_dv + dv
        cross_qgain = cross_qgain + qgain[0]
        r = cross_qs[c]
        dot = row_totals(qdot)
        d_qpres[c] = (dqw * r - cross_qp[c] * (r * r * r * dot / D)).astype(BF)
        cross_qb = cross_qb + colsum(d_qpres[c].astype(F32))
        q_back = dot_nt(d_qpres[c], cross_w[0])
    backs = {f: own_q + got_q.astype(F32), g: spread(q_back)}
    for c in (f, g):
        back = backs[c]
        norm3_g = norm3_g + colsum(back * unit1[c])
        bias0 = bias0 + colsum(back)
        state[c] = d_afters[c] + normal_back(back * norm3_row, unit1[c], scale1[c])
        gate0_g = gate0_g + colsum(branch0[c] * state[c])
        d_self = (gate_attn * state[c]).astype(BF)
        bias1 = bias1 + colsum(d_self.astype(F32))
        d_rows0[c] = [d_self, swap(d_self)]

    cross_dkw = cross_dk * qg_full[1, 1]
    kdot = row_totals(jnp.sum(cross_dkw * cross_kp, axis=-1, keepdims=True))
    cross_kgain = colsum(cross_dk * cross_kp * cross_kr)
    d_kpre = (cross_dkw * cross_kr - cross_kp * (cross_kr**3 * kdot / D)).astype(BF)
    d_v = cross_dv.astype(BF)
    g_cross = head_grads(
        [
            list(zip(rows1, d_qpres)),
            [(text_pieces, d_kpre)],
            [(text_pieces, d_v)],
            list(zip(d_rows1, cross_mixed)),
        ]
    )
    own_text, got_text = halves(dot_nt(d_kpre, cross_w[1]) + dot_nt(d_v, cross_w[2]))
    cross_b = jnp.stack([cross_qb, colsum(d_kpre.astype(F32)), colsum(d_v.astype(F32))])

    g_self_out = head_grads([list(zip(d_rows0, self_mixed))])
    d_mixed = dot_nn(cat([x for pieces in d_rows0 for x in pieces]), self_out_t).astype(BF)
    d_mixed, g_self_out, g_cross, s_out, g_in = tie(d_mixed, g_self_out, g_cross, s_out, g_in)
    s_in = reduce_rows(g_in[None])
    ffn_out_g = s_out[0].astype(F32).T
    ffn_in_g = s_in[0].astype(F32)
    lse = jnp.concatenate(self_lse, axis=2)
    dqw, dkw, dv, qdot, kdot, self_qgain, self_kgain = attend_back_self(
        self_q, self_k, vv, d_mixed, lse, key_mask, qp, kp, qs, ks, qg_full[0, 0], qg_full[0, 1], cos, sin
    )
    dots = []
    for a, b in spans:
        dots.append(row_totals(jnp.concatenate([qdot[a:b], kdot[a:b]], axis=1)))
    dots = cat(dots)
    d_q = (dqw * qs - qp * (qs**3 * dots[:, 0:1] / D)).astype(BF)
    d_k = (dkw * ks - kp * (ks**3 * dots[:, 1:2] / D)).astype(BF)
    d_q, got_text = tie(d_q, got_text)
    text_g = own_text + got_text.astype(F32)
    text_g, d_k = tie(text_g, d_k)
    g_self, part, other = self_back(rows0, spans, heads_w, [d_q, d_k, dv])
    self_b = jnp.stack([colsum(g.astype(F32)) for g in (d_q, d_k, dv)])

    blank = jnp.zeros((D,), F32)
    wide = jnp.stack(
        [blank, blank, gate0_g, shift2, scale2_g, gate_ffn_grad, bias0, bias1, bias2, bias3, norm3_g]
        + [jnp.broadcast_to(err_sq, (D,))]
        + [blank] * 4
    )
    narrow = jnp.concatenate(
        [
            self_b.reshape(-1, HD),
            cross_b.reshape(-1, HD),
            jnp.stack([self_qgain[0], self_kgain[0], cross_qgain, cross_kgain]).reshape(-1, HD),
            ffn_b_grad.reshape(-1, HD),
        ],
        axis=0,
    )
    n_narrow = narrow.shape[0]
    narrow = jnp.pad(narrow.reshape(-1), (0, -narrow.size % (8 * D))).reshape(-1, D)
    sums, hidden_g, small = tail(
        ndp,
        [g_self, g_self_out, g_cross],
        part,
        other,
        state,
        unit0,
        cat(scale0),
        1.0 + scale_attn,
        jnp.concatenate([wide, narrow]),
    )
    self_qkv_g = sums[:3]
    self_out_g = sums[3].T
    cross_qkv_g = sums[4:7]
    cross_out_g = sums[7].T
    wide = small[:16]
    narrow = small[16:].reshape(-1)[: n_narrow * HD].reshape(n_narrow, HD)
    narrow = lax.dynamic_slice_in_dim(narrow, dp * w_low, w_low, 1)
    mine = lax.dynamic_slice_in_dim(wide, (dp * 2 + mp) * w_f32, w_f32, 1)
    mean_loss = wide[11, 0] / (jnp.sum(lengths).astype(F32) * D)
    nh = head_bias.size // head_bias.shape[-1]
    ng = qk_gain.size // qk_gain.shape[-1]
    return (
        cat(results)[None, :own_len],
        mean_loss,
        hidden_g[None, :own_len],
        text_g[None],
        mine[:6],
        mine[6:10],
        mine[10],
        self_qkv_g,
        self_out_g,
        cross_qkv_g,
        cross_out_g,
        ffn_in_g,
        ffn_out_g,
        narrow[:nh].reshape(head_bias.shape),
        narrow[nh : nh + ng].reshape(qk_gain.shape),
        narrow[nh + ng :].reshape(ffn_bias.shape),
    )


def solution(mesh):
    in_specs = (
        P("dp", "mp", None),
        P("dp", "mp", None),
        P("dp", None, None),
        P(),
        P("dp", None, None),
        P("dp", "mp", None),
        P(None, ("dp", "mp")),
        P(None, ("dp", "mp")),
        P(("dp", "mp")),
        P(None, "dp", "mp"),
        P("mp", "dp"),
        P(None, "dp", "mp"),
        P("mp", "dp"),
        P("dp", "mp"),
        P("mp", "dp"),
        P(None, None, "mp", "dp"),
        P(None, None, "mp", "dp"),
        P("mp", "dp"),
    )
    out_specs = (
        P("dp", "mp", None),
        P(),
        P("dp", "mp", None),
        P("dp", "mp", None),
        P(None, ("dp", "mp")),
        P(None, ("dp", "mp")),
        P(("dp", "mp")),
        P(None, "dp", "mp"),
        P("mp", "dp"),
        P(None, "dp", "mp"),
        P("mp", "dp"),
        P("dp", "mp"),
        P("mp", "dp"),
        P(None, None, "mp", "dp"),
        P(None, None, "mp", "dp"),
        P("mp", "dp"),
    )
    return jax.shard_map(local, mesh=mesh, in_specs=in_specs, out_specs=out_specs, check_vma=False)
```

```python
import functools
import math

import jax
import jax.numpy as jnp
import numpy as np
from jax import lax
from jax.experimental import pallas as pl
from jax.experimental.pallas import tpu as pltpu
from jax.sharding import PartitionSpec as P

D = 1536
HD = 128
EPS = 1e-06
SCALE = HD ** (-0.5)
BF = jnp.bfloat16
F32 = jnp.float32
NEG = -1e30
SWAP = [(0, 1), (1, 0)]
VMEM_BYTES = 48 * 1024 * 1024


def rope_rates():
    pair_count = HD // 2
    third = pair_count // 3
    counts = [pair_count - 2 * third, third, third]
    rates = np.zeros((3, HD), np.float32)
    start = 0
    for axis_id, count in enumerate(counts):
        steps = np.arange(count, dtype=np.float32) / np.float32(count)
        values = np.exp(np.float32(-math.log(10000.0)) * steps).astype(np.float32)
        rates[axis_id, 2 * start : 2 * (start + count)] = np.repeat(values, 2)
        start += count
    return rates


def dot_nn(a, b):
    return lax.dot_general(a, b, (((1,), (0,)), ((), ())), preferred_element_type=F32)


def dot_nt(a, b):
    return lax.dot_general(a, b, (((1,), (1,)), ((), ())), preferred_element_type=F32)


def dot_tn(a, b):
    return lax.dot_general(a, b, (((0,), (0,)), ((), ())), preferred_element_type=F32)


def cost(flops, nbytes, trans=0):
    return pl.CostEstimate(flops=int(flops), bytes_accessed=int(nbytes), transcendentals=int(trans))


def params():
    return pltpu.CompilerParams(vmem_limit_bytes=VMEM_BYTES)


def turn(values):
    lane = lax.broadcasted_iota(jnp.int32, values.shape, 1)
    after = pltpu.roll(values, HD - 1, 1)
    before = pltpu.roll(values, 1, 1)
    return jnp.where(lane % 2 == 0, after, before)


def prep_kernel(qp, kp, qs, ks, qg, kg, cos, sin, q_out, k_out):
    c = cos[...]
    s = sin[...]
    for pre, scale, gain, out in ((qp, qs, qg, q_out), (kp, ks, kg, k_out)):
        v = pre[...] * scale[...] * gain[...]
        out[...] = (v * c + turn(v) * s).astype(BF)


def prep(qp, kp, qs, ks, qg, kg, cos, sin):
    rows, width = qp.shape
    head = pl.BlockSpec((rows, HD), lambda h: (0, h))
    col = pl.BlockSpec((rows, 1), lambda h: (0, 0))
    gain = pl.BlockSpec((1, HD), lambda h: (0, h))
    tab = pl.BlockSpec((rows, HD), lambda h: (0, 0))
    return pl.pallas_call(
        prep_kernel,
        grid=(width // HD,),
        in_specs=[head, head, col, col, gain, gain, tab, tab],
        out_specs=[head, head],
        out_shape=[jax.ShapeDtypeStruct((rows, width), BF)] * 2,
        compiler_params=params(),
        cost_estimate=cost(rows * width * 20, rows * width * 12),
        name="rope_prep",
    )(qp, kp, qs, ks, qg, kg, cos, sin)


def attend_kernel(masked, *refs):
    if masked:
        q, k, v, w, mask, out, lse, own, other = refs
    else:
        q, k, v, w, out, lse, own, other = refs
    st = dot_nt(k[...], q[...]) * SCALE
    if masked:
        st = st + mask[...]
    top = jnp.max(st, axis=0, keepdims=True)
    e = jnp.exp(st - top)
    total = jnp.sum(e, axis=0, keepdims=True)
    lse[0] = top + jnp.log(total)
    mixed = dot_tn(v[...], e.astype(BF)) * (1.0 / total)
    h = pl.program_id(0)
    out[:, pl.ds(pl.multiple_of(h * HD, HD), HD)] = mixed.T.astype(BF)

    @pl.when(h == pl.num_programs(0) - 1)
    def _():
        half = out.shape[0] // 2
        own[...] = dot_nt(out[:half], w[0])
        other[...] = dot_nt(out[half:], w[0]).astype(BF)


def attend(q, k, v, mask, weights, slab):
    nq, width = q.shape
    nk = k.shape[0]
    d = weights.shape[1]
    heads = width // HD
    qb = pl.BlockSpec((nq, HD), lambda h: (0, h))
    kb = pl.BlockSpec((nk, HD), lambda h: (0, h))
    ins = [qb, kb, kb, pl.BlockSpec((1, d, width), lambda h: (slab, 0, 0), pipeline_mode=pl.Buffered(1))]
    args = [q, k, v, weights]
    if mask is not None:
        ins.append(pl.BlockSpec((nk, 1), lambda h: (0, 0)))
        args.append(mask)
    return pl.pallas_call(
        functools.partial(attend_kernel, mask is not None),
        grid=(heads,),
        in_specs=ins,
        out_specs=[
            pl.BlockSpec((nq, width), lambda h: (0, 0)),
            pl.BlockSpec((1, 1, nq), lambda h: (h, 0, 0)),
            pl.BlockSpec((nq // 2, d), lambda h: (0, 0)),
            pl.BlockSpec((nq // 2, d), lambda h: (0, 0)),
        ],
        out_shape=[
            jax.ShapeDtypeStruct((nq, width), BF),
            jax.ShapeDtypeStruct((heads, 1, nq), F32),
            jax.ShapeDtypeStruct((nq // 2, d), F32),
            jax.ShapeDtypeStruct((nq // 2, d), BF),
        ],
        compiler_params=params(),
        cost_estimate=cost(4 * nq * nk * width * 3, 4 * nq * width + 4 * nk * width, nq * nk * heads),
        name="attend_fwd",
    )(*args)


def attend_back_kernel(self_form, *refs):
    if self_form:
        (q, k, v, do, lse, mask, qp, kp, qs, ks, qg, kg, cos, sin,
         dq_out, dk_out, dv_out, qdot, kdot, qgain, kgain) = refs
    else:
        q, k, v, do, lse, qp, qs, qg, dq_out, dk_out, dv_out, qdot, qgain = refs
    st = dot_nt(k[...], q[...]) * SCALE
    if self_form:
        st = st + mask[...]
    p = jnp.exp(st - lse[0])
    dp = dot_nt(v[...], do[...])
    inner = jnp.sum(dp * p, axis=0, keepdims=True)
    ds = (p * (dp - inner)).astype(BF)
    dv_out[...] = dot_nn(p.astype(BF), do[...]).astype(dv_out.dtype)
    dk = dot_nn(ds, q[...]) * SCALE
    dq = dot_tn(k[...], ds).T * SCALE
    sides = [(dq, qp, qs, qg, dq_out, qdot, qgain)]
    if self_form:
        dq = dq * cos[...] - turn(dq) * sin[...]
        dk = dk * cos[...] - turn(dk) * sin[...]
        sides = [(dq, qp, qs, qg, dq_out, qdot, qgain), (dk, kp, ks, kg, dk_out, kdot, kgain)]
    else:
        dk_out[...] = dk
    for grad, pre, scale, gain, out, dots, gains in sides:
        p_rows = pre[...]
        weighted = grad * gain[...]
        out[...] = weighted
        part = jnp.sum(weighted * p_rows, axis=1, keepdims=True)

        @pl.when(pl.program_id(0) == 0)
        def _():
            dots[...] = part

        @pl.when(pl.program_id(0) > 0)
        def _():
            dots[...] += part

        gains[...] = jnp.sum(grad * (p_rows * scale[...]), axis=0, keepdims=True)


def attend_back_self(q, k, v, do, lse, mask, qp, kp, qs, ks, qg, kg, cos, sin):
    n, width = q.shape
    heads = width // HD
    rows = pl.BlockSpec((n, HD), lambda h: (0, h))
    col = pl.BlockSpec((n, 1), lambda h: (0, 0))
    gain = pl.BlockSpec((1, HD), lambda h: (0, h))
    tab = pl.BlockSpec((n, HD), lambda h: (0, 0))
    lses = pl.BlockSpec((1, 1, n), lambda h: (h, 0, 0))
    full = jax.ShapeDtypeStruct((n, width), F32)
    cols = jax.ShapeDtypeStruct((n, 1), F32)
    gains = jax.ShapeDtypeStruct((1, width), F32)
    return pl.pallas_call(
        functools.partial(attend_back_kernel, True),
        grid=(heads,),
        in_specs=[rows, rows, rows, rows, lses, col, rows, rows, col, col, gain, gain, tab, tab],
        out_specs=[rows, rows, rows, col, col, gain, gain],
        out_shape=[full, full, jax.ShapeDtypeStruct((n, width), BF), cols, cols, gains, gains],
        compiler_params=params(),
        cost_estimate=cost(10 * n * n * width * 3, 26 * n * width, n * n * heads),
        name="attend_bwd_self",
    )(q, k, v, do, lse, mask, qp, kp, qs, ks, qg, kg, cos, sin)


def attend_back_cross(q, k, v, do, lse, qp, qs, qg):
    n, width = q.shape
    nk = k.shape[0]
    heads = width // HD
    rows = pl.BlockSpec((n, HD), lambda h: (0, h))
    keys = pl.BlockSpec((nk, HD), lambda h: (0, h))
    col = pl.BlockSpec((n, 1), lambda h: (0, 0))
    gain = pl.BlockSpec((1, HD), lambda h: (0, h))
    lses = pl.BlockSpec((1, 1, n), lambda h: (h, 0, 0))
    return pl.pallas_call(
        functools.partial(attend_back_kernel, False),
        grid=(heads,),
        in_specs=[rows, keys, keys, rows, lses, rows, col, gain],
        out_specs=[rows, keys, keys, col, gain],
        out_shape=[
            jax.ShapeDtypeStruct((n, width), F32),
            jax.ShapeDtypeStruct((nk, width), F32),
            jax.ShapeDtypeStruct((nk, width), F32),
            jax.ShapeDtypeStruct((n, 1), F32),
            jax.ShapeDtypeStruct((1, width), F32),
        ],
        compiler_params=params(),
        cost_estimate=cost(10 * n * nk * width * 3, 12 * n * width + 12 * nk * width, n * nk * heads),
        name="attend_bwd_cross",
    )(q, k, v, do, lse, qp, qs, qg)


def head_grads_kernel(plan, *refs):
    out = refs[-1]
    for i, terms in enumerate(plan):

        @pl.when(pl.program_id(0) == i)
        def _(terms=terms):
            total = None
            for a, b, lo, hi in terms:
                term = dot_tn(refs[a][...], refs[b][lo:hi])
                total = term if total is None else total + term
            out[0] = total.astype(BF)


def self_back_kernel(spans, *refs):
    n = 2 * len(spans)
    rows = refs[:n]
    weights = refs[n]
    heads = refs[n + 1 : n + 4]
    grads, part, other, acc = refs[n + 4 :]
    halves = [x for a, b in spans for x in ((a, (a + b) // 2), ((a + b) // 2, b))]
    for i in range(3):

        @pl.when(pl.program_id(0) == i)
        def _(i=i):
            total = None
            for x, (a, b) in zip(rows, halves):
                term = dot_tn(x[...], heads[i][a:b])
                total = term if total is None else total + term
            grads[0] = total.astype(BF)
            back = dot_nt(heads[i][...], weights[0])
            if i == 0:
                acc[...] = back
            elif i == 1:
                acc[...] += back
            else:
                back = acc[...] + back
                at = 0
                for a, b in spans:
                    half = (b - a) // 2
                    part[at : at + half] = back[a : a + half]
                    other[at : at + half] = back[a + half : b].astype(BF)
                    at += half


def self_back(rows, spans, weights, heads):
    n, width = heads[0].shape
    d = rows[0].shape[1]
    once = lambda x: pl.BlockSpec(x.shape, lambda i: (0, 0), pipeline_mode=pl.Buffered(1))
    return pl.pallas_call(
        functools.partial(self_back_kernel, spans),
        grid=(3,),
        in_specs=[once(x) for x in rows]
        + [pl.BlockSpec((1, d, width), lambda i: (i, 0, 0))]
        + [once(x) for x in heads],
        out_specs=[
            pl.BlockSpec((1, d, width), lambda i: (i, 0, 0)),
            pl.BlockSpec((n // 2, d), lambda i: (0, 0)),
            pl.BlockSpec((n // 2, d), lambda i: (0, 0)),
        ],
        out_shape=[
            jax.ShapeDtypeStruct((3, d, width), BF),
            jax.ShapeDtypeStruct((n // 2, d), F32),
            jax.ShapeDtypeStruct((n // 2, d), BF),
        ],
        scratch_shapes=[pltpu.VMEM((n, d), F32)],
        compiler_params=params(),
        cost_estimate=cost(12 * n * d * width, 30e6),
        name="self_back",
    )(*rows, weights, *heads)


def head_grads(products):
    arrays, plan = [], []

    def place(x):
        for i, y in enumerate(arrays):
            if x is y:
                return i
        arrays.append(x)
        return len(arrays) - 1

    for pairs in products:
        terms = []
        for pieces, b in pairs:
            at = 0
            for a in pieces:
                terms.append((place(a), place(b), at, at + a.shape[0]))
                at += a.shape[0]
        plan.append(terms)
    m, n = products[0][0][0][0].shape[1], products[0][0][1].shape[1]
    rows = sum(b.shape[0] for pairs in products for _, b in pairs)
    return pl.pallas_call(
        functools.partial(head_grads_kernel, plan),
        grid=(len(products),),
        in_specs=[
            pl.BlockSpec(x.shape, lambda i: (0, 0), pipeline_mode=pl.Buffered(1)) for x in arrays
        ],
        out_specs=pl.BlockSpec((1, m, n), lambda i: (i, 0, 0)),
        out_shape=jax.ShapeDtypeStruct((len(products), m, n), BF),
        compiler_params=params(),
        cost_estimate=cost(2 * rows * m * n, 2 * sum(x.size for x in arrays) + 2 * len(products) * m * n),
        name="head_grads",
    )(*arrays)


def tail_kernel(ndp, counts, nc, *refs):
    n = len(counts)
    g = refs[:n]
    state = refs[n : n + nc]
    unit = refs[n + nc : n + 2 * nc]
    (part, other, lns, ones, small, gsum, hgrad, small_out,
     mine, got, send, slot, ybuf, pbuf, stbuf, ubuf, vals, inbox,
     mine_sem, got_send, got_recv, ring_send, ring_recv, y_sem, load_sem, sum_send, sum_recv) = refs[n + 2 * nc :]
    chips = ndp // 2
    bits = ndp.bit_length() - 1
    dp = lax.axis_index("dp")
    mp = lax.axis_index("mp")
    core = lax.rem(dp, 2)
    chip = lax.div(dp, 2)
    odd = lax.rem(chip, 2)
    row = lax.div(chip, 2)
    place = row * (1 - odd) + (chips - 1 - row) * odd
    way = 1 - 2 * core

    def chip_at(shift):
        spot = lax.rem(place + way * shift + 2 * chips, chips)
        back = lax.div(spot, chips // 2)
        return 2 * spot * (1 - back) + (2 * (chips - 1 - spot) + 1) * back

    after = 2 * chip_at(1) + core
    before = 2 * chip_at(-1) + core
    mates = [dp + (1 - 2 * lax.rem(lax.div(dp, 1 << b), 2)) * (1 << b) for b in range(bits)]
    mesh_id = pl.DeviceIdType.MESH

    barrier = pltpu.get_barrier_semaphore()
    for device in (after, before, *mates):
        pl.semaphore_signal(barrier, inc=1, device_id=(device, mp), device_id_type=mesh_id)
    pl.semaphore_signal(barrier, inc=1, device_id=(dp, 1 - mp), device_id_type=mesh_id)
    pl.semaphore_wait(barrier, 3 + bits)

    def remote(src, dst, s_sem, r_sem, device):
        return pltpu.make_async_remote_copy(
            src_ref=src, dst_ref=dst, send_sem=s_sem, recv_sem=r_sem, device_id=device, device_id_type=mesh_id
        )

    starts = [sum(counts[:i]) for i in range(n)]
    total = sum(counts)
    cuts = [(0, (total + 1) // 2), ((total + 1) // 2, total)]

    def to_mate(s, i):
        return remote(
            g[i].at[:, chip_at(1 + s), 1 - core],
            got.at[s, pl.ds(starts[i], counts[i])],
            got_send.at[i, s],
            got_recv.at[i, s],
            (mates[0], mp),
        )

    def to_self(s, i):
        return pltpu.make_async_copy(
            g[i].at[:, chip_at(-1 - s), core], mine.at[s, pl.ds(starts[i], counts[i])], mine_sem.at[i, s]
        )

    def along(s, half):
        lo, hi = cuts[half]
        return remote(
            send.at[s, pl.ds(lo, hi - lo)],
            slot.at[s, pl.ds(lo, hi - lo)],
            ring_send.at[half, s],
            ring_recv.at[half, s],
            (after, mp),
        )

    def sum_copy(j):
        if j < bits:
            return remote(vals.at[j], inbox.at[j], sum_send.at[j], sum_recv.at[j], (mates[j], mp))
        return remote(
            vals.at[j, pl.ds(0, 16)], inbox.at[j, pl.ds(0, 16)], sum_send.at[j], sum_recv.at[j], (dp, 1 - mp)
        )

    y_copy = remote(other, ybuf, y_sem.at[0], y_sem.at[1], (dp, 1 - mp))
    for s in range(chips):
        for i in range(n):
            to_mate(s, i).start()
            to_self(s, i).start()
        if s == 0:
            y_copy.start()
    pairs = [(part, pbuf)]
    at = 0
    for st, un in zip(state, unit):
        span = pl.ds(at, st.shape[0])
        pairs += [(st, stbuf.at[span]), (un, ubuf.at[span])]
        at += st.shape[0]
    loads = [pltpu.make_async_copy(src, dst, load_sem.at[i]) for i, (src, dst) in enumerate(pairs)]
    for load in loads:
        load.start()

    def finish_rows():
        for load in loads:
            load.wait()
        y_copy.wait_recv()
        rows, width = pbuf.shape
        block = 80 if rows % 80 == 0 else 16
        gain = ones[...]

        def piece(at, sums):
            back = pbuf[at, :] + ybuf[at, :].astype(F32)
            z = ubuf[at, :]
            grad = back * gain
            mean_g = jnp.mean(grad, axis=1, keepdims=True)
            mean_gz = jnp.mean(grad * z, axis=1, keepdims=True)
            hgrad[at, 0, :] = stbuf[at, :] + lns[at, :] * (grad - mean_g - z * mean_gz)
            return (
                sums[0] + jnp.sum(back, axis=0, keepdims=True),
                sums[1] + jnp.sum(back * z, axis=0, keepdims=True),
            )

        def body(i, sums):
            return piece(pl.ds(pl.multiple_of(i * block, block), block), sums)

        kept = hgrad.shape[0]
        zero = jnp.zeros((1, width), F32)
        sums = lax.fori_loop(0, kept // block, body, (zero, zero))
        if kept % block:
            sums = piece(pl.ds(kept // block * block, kept % block), sums)
        vals[0] = small[...]
        vals[0, 0:1, :] = sums[0]
        vals[0, 1:2, :] = sums[1]
        sum_copy(0).start()

    def sum_step(j):
        sum_copy(j).wait_recv()
        if j < bits:
            vals[j + 1] = vals[j] + inbox[j]
            sum_copy(j + 1).start()
        else:
            small_out[...] = vals[j]
            small_out[0:16, :] = vals[j, 0:16, :] + inbox[j, 0:16, :]

    first = min(2, chips - 1)
    done = 0
    for s in range(chips):
        for i in range(n):
            to_self(s, i).wait()
            to_mate(s, i).wait_recv()
        for half in range(2):
            lo, hi = cuts[half]
            value = mine[s, lo:hi].astype(F32) + got[s, lo:hi].astype(F32)
            if s > 0:
                along(s - 1, half).wait_recv()
                value = value + slot[s - 1, lo:hi].astype(F32)
            if s < chips - 1:
                send[s, lo:hi] = value.astype(BF)
                along(s, half).start()
            else:
                gsum[lo:hi] = value
        if s == first:
            finish_rows()
        elif s > first and done <= bits:
            sum_step(done)
            done += 1
    while done <= bits:
        sum_step(done)
        done += 1
    for s in range(chips):
        for i in range(n):
            to_mate(s, i).wait_send()
        if s < chips - 1:
            for half in range(2):
                along(s, half).wait_send()
    y_copy.wait_send()
    for j in range(bits + 1):
        sum_copy(j).wait_send()


def tail(ndp, grads, part, other, state, unit, lns, ones, small, kept):
    chips = ndp // 2
    bits = ndp.bit_length() - 1
    split = [x.reshape(x.shape[0], chips, 2, x.shape[1] // ndp, x.shape[2]) for x in grads]
    counts = tuple(x.shape[0] for x in grads)
    total = sum(counts)
    r, w = split[0].shape[3:]
    rows, width = part.shape
    n = len(grads)
    nc = len(state)
    hbm = pl.BlockSpec(memory_space=pl.ANY)
    vmem = pl.BlockSpec(memory_space=pltpu.VMEM)
    dma = pltpu.SemaphoreType.DMA
    return pl.pallas_call(
        functools.partial(tail_kernel, ndp, counts, nc),
        in_specs=[hbm] * (n + 2 * nc) + [hbm, hbm, vmem, vmem, vmem],
        out_specs=[vmem] * 3,
        out_shape=[
            jax.ShapeDtypeStruct((total, r, w), F32),
            jax.ShapeDtypeStruct((kept, 1, width), F32),
            jax.ShapeDtypeStruct(small.shape, F32),
        ],
        scratch_shapes=[
            pltpu.VMEM((chips, total, r, w), BF),
            pltpu.VMEM((chips, total, r, w), BF),
            pltpu.VMEM((chips - 1, total, r, w), BF),
            pltpu.VMEM((chips - 1, total, r, w), BF),
            pltpu.VMEM((rows, width), BF),
            pltpu.VMEM((rows, width), F32),
            pltpu.VMEM((rows, width), F32),
            pltpu.VMEM((rows, width), F32),
            pltpu.VMEM((bits + 1,) + small.shape, F32),
            pltpu.VMEM((bits + 1,) + small.shape, F32),
            dma((n, chips)),
            dma((n, chips)),
            dma((n, chips)),
            dma((2, chips - 1)),
            dma((2, chips - 1)),
            dma((2,)),
            dma((1 + 2 * nc,)),
            dma((bits + 1,)),
            dma((bits + 1,)),
        ],
        compiler_params=pltpu.CompilerParams(
            vmem_limit_bytes=58 * 1024 * 1024, collective_id=0, has_side_effects=True
        ),
        cost_estimate=cost(1e6, 1e6),
        name="tail_sums",
    )(*split, *state, *unit, part, other, lns, ones, small)


def normal(values):
    center = values - jnp.mean(values, axis=-1, keepdims=True)
    scale = lax.rsqrt(jnp.mean(center * center, axis=-1, keepdims=True) + EPS)
    return center * scale, scale


def normal_back(grad, unit, scale):
    mean_g = jnp.mean(grad, axis=-1, keepdims=True)
    mean_gz = jnp.mean(grad * unit, axis=-1, keepdims=True)
    return scale * (grad - mean_g - unit * mean_gz)


def swap(values):
    return lax.ppermute(values, "mp", SWAP)


def collect(own):
    pieces = [own, swap(own)]
    return jnp.concatenate(pieces, axis=0), pieces


def spread(partial):
    half = partial.shape[0] // 2
    return partial[:half] + swap(partial[half:].astype(BF)).astype(F32)


def halves(partial):
    half = partial.shape[0] // 2
    return partial[:half], swap(partial[half:].astype(BF))


def row_totals(own):
    half = own.shape[0] // 2
    return own + swap(jnp.concatenate([own[half:], own[:half]], axis=0))


def squares(values):
    return jnp.sum(values * values, axis=-1, keepdims=True)


def colsum(values):
    return jnp.sum(values, axis=0, dtype=F32)


def tie(*values):
    return lax.optimization_barrier(values)


def partners(ndp, bit):
    return [(i, i ^ (1 << bit)) for i in range(ndp)]


def gather_small(flat, ndp, dp, mp):
    rows = flat[None]
    got = swap(rows)
    rows = jnp.where(mp == 0, jnp.concatenate([rows, got]), jnp.concatenate([got, rows]))
    for bit in range(ndp.bit_length() - 1):
        got = lax.ppermute(rows, "dp", partners(ndp, bit))
        low = (dp >> bit) % 2 == 0
        rows = jnp.where(low, jnp.concatenate([rows, got]), jnp.concatenate([got, rows]))
    return rows


def chunks_of(padded):
    first = (padded // 2 + 15) // 16 * 16
    return [(0, first), (first, padded)]


def local(
    hidden,
    text_states,
    time_emb,
    lengths,
    positions,
    teacher,
    modulation,
    out_bias,
    norm3_gain,
    self_qkv,
    self_out,
    cross_qkv,
    cross_out,
    ffn_in,
    ffn_out,
    head_bias,
    qk_gain,
    ffn_bias,
):
    ndp = lax.axis_size("dp")
    dp = lax.axis_index("dp")
    mp = lax.axis_index("mp")
    own_len = hidden.shape[1]
    length = 2 * own_len
    padded = (own_len + 15) // 16 * 16
    pad = padded - own_len
    cuts = chunks_of(padded)

    f32_part = jnp.concatenate([modulation, out_bias, norm3_gain[None]], axis=0)
    hb = head_bias.reshape(-1, head_bias.shape[-1])
    qg = qk_gain.reshape(-1, qk_gain.shape[-1])
    low_part = jnp.concatenate([hb, qg, ffn_bias], axis=0).astype(F32)
    n_f32, w_f32 = f32_part.shape
    n_low, w_low = low_part.shape
    flat = jnp.concatenate([f32_part.reshape(-1), low_part.reshape(-1)])
    n_flat = flat.shape[0]
    flat_all = gather_small(jnp.pad(flat, (0, -n_flat % 128)), ndp, dp, mp)[:, :n_flat]
    f32_all = flat_all[:, : n_f32 * w_f32].reshape(2 * ndp, n_f32, w_f32)
    f32_all = f32_all.transpose(1, 0, 2).reshape(n_f32, -1)
    low_all = flat_all[:, n_f32 * w_f32 :].reshape(ndp, 2, n_low, w_low)
    low_all = lax.dynamic_index_in_dim(low_all, mp, 1, False)
    low_all = low_all.transpose(1, 0, 2).reshape(n_low, -1)
    mod_full = f32_all[:6]
    out_bias_full = f32_all[6:10]
    norm3_full = f32_all[10]
    hb_full = low_all[: hb.shape[0]].reshape(2, 3, -1)
    qg_full = low_all[hb.shape[0] : hb.shape[0] + qg.shape[0]].reshape(2, 2, 1, -1)
    ffn_bias_full = low_all[hb.shape[0] + qg.shape[0] :].reshape(-1)

    def whole(shards):
        return lax.all_gather(shards, "dp", axis=1, tiled=True)

    heads_w = whole(jnp.concatenate([self_qkv, self_out.T[None], cross_qkv, cross_out.T[None]]))
    self_w = heads_w[:4]
    cross_w = heads_w[4:]
    ffn_w = whole(jnp.stack([ffn_in, ffn_out.T]))
    self_out_t = self_w[3]
    cross_out_t = cross_w[3]
    ffn_in_w = ffn_w[0]
    ffn_out_t = ffn_w[1]

    signals = mod_full + time_emb[0]
    shift_attn, scale_attn, gate_attn, shift_ffn, scale_ffn, gate_ffn = [
        signals[i : i + 1] for i in range(6)
    ]
    clip_length = lax.dynamic_index_in_dim(lengths, dp, 0, False)

    def own_chunks(array):
        full = jnp.pad(array, ((0, pad), (0, 0)))
        return [full[a:b] for a, b in cuts]

    hid = own_chunks(hidden[0])
    teach = own_chunks(teacher[0])
    index = jnp.arange(padded)
    pos_pad = jnp.pad(positions[0].reshape(3, 2, own_len), ((0, 0), (0, 0), (0, pad)))

    def both(own, other):
        return jnp.concatenate([x[a:b] for a, b in cuts for x in (own, other)], axis=0)

    def slot_valid(half):
        return (index < own_len) & (half * own_len + index < clip_length)

    own_valid = slot_valid(mp)
    key_valid = both(own_valid, slot_valid(1 - mp))
    key_mask = jnp.where(key_valid, 0.0, NEG).astype(F32)[:, None]
    row_valid = [own_valid.astype(F32)[a:b, None] for a, b in cuts]
    pos_own = lax.dynamic_index_in_dim(pos_pad, mp, 1, False)
    pos_other = lax.dynamic_index_in_dim(pos_pad, 1 - mp, 1, False)
    rates = rope_rates()
    angle = sum(
        both(pos_own[i], pos_other[i]).astype(F32)[:, None] * rates[i][None, :] for i in range(3)
    )
    even = np.arange(HD) % 2 == 0
    cos = jnp.cos(angle)
    sin = jnp.sin(angle) * np.where(even, -1.0, 1.0).astype(np.float32)
    ends = np.cumsum([0] + [2 * (b - a) for a, b in cuts])
    spans = [(int(ends[i]), int(ends[i + 1])) for i in range(len(cuts))]
    nc = len(cuts)

    out_rows = [out_bias_full[i : i + 1] for i in range(4)]
    norm3_row = norm3_full[None]
    ffn_bias_row = ffn_bias_full[None]
    bias_rows = [hb_full[i, j][None] for i in range(2) for j in range(3)]
    late = [gate_attn, shift_ffn, scale_ffn, gate_ffn, norm3_row, ffn_bias_row, key_mask, cos, sin]
    late += out_rows + bias_rows + row_valid
    heads_w, *late = tie(heads_w, *late)
    gate_attn, shift_ffn, scale_ffn, gate_ffn, norm3_row, ffn_bias_row, key_mask, cos, sin = late[:9]
    out_rows, bias_rows, row_valid = late[9:13], late[13:19], late[19:]
    self_w = heads_w[:4]
    cross_w = heads_w[4:]
    self_out_t = heads_w[3]
    cross_out_t = heads_w[7]

    text_rows, text_pieces = collect(text_states[0])

    res0, unit0, scale0, rows0 = [], [], [], []
    qp, kp, vv, qs, ks = [], [], [], [], []
    for c in range(nc):
        r = hid[c].astype(F32)
        z, s = normal(r)
        x = (z * (1.0 + scale_attn) + shift_attn).astype(BF)
        rows, pieces = collect(x)
        qc = dot_nn(rows, self_w[0]) + bias_rows[0]
        kc = dot_nn(rows, self_w[1]) + bias_rows[1]
        vc = (dot_nn(rows, self_w[2]) + bias_rows[2]).astype(BF)
        tot = row_totals(jnp.concatenate([squares(qc), squares(kc)], axis=1))
        res0.append(r)
        unit0.append(z)
        scale0.append(s)
        rows0 += pieces
        qp.append(qc)
        kp.append(kc)
        vv.append(vc)
        scales = lax.rsqrt(tot / D + EPS)
        qs.append(scales[:, 0:1])
        ks.append(scales[:, 1:2])
    qp, kp, vv = [jnp.concatenate(x, axis=0) for x in (qp, kp, vv)]
    qs, ks = [jnp.concatenate(x, axis=0) for x in (qs, ks)]
    self_q, self_k = prep(qp, kp, qs, ks, qg_full[0, 0], qg_full[0, 1], cos, sin)

    none = [None] * nc
    f, g = nc - 1, 0
    self_mixed, self_lse, branch0, unit1, scale1, after_self = [list(none) for _ in range(6)]
    cross_mixed, cross_lse, cross_q, cross_qp, cross_qs = [list(none) for _ in range(5)]
    rows1, rows2, unit2, scale2, after = [list(none) for _ in range(5)]

    def self_rows(c):
        a, b = spans[c]
        self_mixed[c], self_lse[c], own, other = attend(self_q[a:b], self_k, vv, key_mask, heads_w, 3)
        return own, swap(other)

    def cross_query(c, own, got):
        branch0[c] = own + got.astype(F32) + out_rows[1]
        after_self[c] = res0[c] + gate_attn * branch0[c]
        unit1[c], scale1[c] = normal(after_self[c])
        x = (unit1[c] * norm3_row + out_rows[0]).astype(BF)
        rows1[c] = [x, swap(x)]

    def cross_prepare(c, got=None):
        qc = dot_nn(jnp.concatenate(rows1[c], axis=0), heads_w[4]) + bias_rows[3]
        if got is not None:
            qc, got = tie(qc, got)
        cross_qp[c] = qc
        cross_qs[c] = lax.rsqrt(row_totals(squares(qc)) / D + EPS)
        cross_q[c] = (qc * cross_qs[c] * qg_full[1, 0]).astype(BF)
        return got

    def cross_attend(c):
        cross_mixed[c], cross_lse[c], own, other = attend(cross_q[c], cross_k, cross_v, None, heads_w, 7)
        return own, other

    def ffn_input(c, own, got):
        after[c] = after_self[c] + own + got.astype(F32) + out_rows[2]
        unit2[c], scale2[c] = normal(after[c])
        return (unit2[c] * (1.0 + scale_ffn) + shift_ffn).astype(BF)

    own_f, got_f = self_rows(f)
    own_g, got_g = self_rows(g)
    got_f, own_g = tie(got_f, own_g)
    cross_query(f, own_f, got_f)
    rows1[f][0], text_rows = tie(rows1[f][0], text_rows)
    cross_query(g, own_g, got_g)
    cross_kp = dot_nn(text_rows, cross_w[1]) + bias_rows[4]
    cross_v = (dot_nn(text_rows, cross_w[2]) + bias_rows[5]).astype(BF)
    rows1[f][1], cross_kp, cross_v = tie(rows1[f][1], cross_kp, cross_v)
    cross_ks = row_totals(squares(cross_kp))
    cross_kr = lax.rsqrt(cross_ks / D + EPS)
    cross_k = (cross_kp * cross_kr * qg_full[1, 1]).astype(BF)
    cross_prepare(f)
    own_f, other_f = cross_attend(f)
    rows1[g][1], other_f = tie(rows1[g][1], other_f)
    got_f = swap(other_f)
    got_f = cross_prepare(g, got_f)
    x_f = ffn_input(f, own_f, got_f)
    cross_q[g], x_f = tie(cross_q[g], x_f)
    y_f = swap(x_f)
    own_g, other_g = cross_attend(g)
    y_f, own_g, other_g = tie(y_f, own_g, other_g)
    rows2[f] = jnp.concatenate([x_f, y_f], axis=0)
    got_g = swap(other_g)

    def cat(parts):
        return jnp.concatenate(parts, axis=0)

    def reduce_rows(full):
        return lax.psum_scatter(full, "dp", scatter_dimension=1, tiled=True)

    acts, slopes, results, errors, d_ffn, d_inners, d_afters, d_crosses = [list(none) for _ in range(8)]
    squares_of, gate_grads, ffn_backs = [list(none) for _ in range(3)]

    def inner_of(c):
        inner = dot_nn(rows2[c], ffn_in_w) + ffn_bias_row
        act, back = jax.vjp(functools.partial(jax.nn.gelu, approximate=True), inner)
        acts[c] = act.astype(BF)
        slopes[c] = back(jnp.ones_like(inner))[0].astype(BF)

    def loss_of(c, own, got):
        branch = own + got.astype(F32) + out_rows[3]
        result = after[c] + gate_ffn * branch
        results[c] = result.astype(BF)
        errors[c] = (result - teach[c].astype(F32)) * row_valid[c]
        d_ffn[c] = (gate_ffn * errors[c]).astype(BF)
        squares_of[c] = jnp.sum(errors[c] * errors[c])
        gate_grads[c] = colsum(branch * errors[c])

    def inner_back(c, rows):
        d_inners[c] = (dot_nn(rows, ffn_out_t) * slopes[c].astype(F32)).astype(BF)

    def after_back(c, own, got):
        back = own + got.astype(F32)
        ffn_backs[c] = back
        d_afters[c] = errors[c] + normal_back(back * (1.0 + scale_ffn), unit2[c], scale2[c])
        d_crosses[c] = d_afters[c].astype(BF)

    inner_of(f)
    got_g, acts[f] = tie(got_g, acts[f])
    x_g = ffn_input(g, own_g, got_g)
    acts[f], x_g = tie(acts[f], x_g)
    y_g = swap(x_g)
    branch_f = dot_nt(acts[f], ffn_out_t)
    y_g, branch_f = tie(y_g, branch_f)
    rows2[g] = jnp.concatenate([x_g, y_g], axis=0)
    own_f, got_f = halves(branch_f)
    inner_of(g)
    got_f, acts[g] = tie(got_f, acts[g])
    loss_of(f, own_f, got_f)
    acts[g], d_ffn[f] = tie(acts[g], d_ffn[f])
    d_f = swap(d_ffn[f])
    branch_g = dot_nt(acts[g], ffn_out_t)
    d_f, branch_g = tie(d_f, branch_g)
    own_g, got_g = halves(branch_g)
    d_f = cat([d_ffn[f], d_f])
    inner_back(f, d_f)
    d_inners[f], got_g = tie(d_inners[f], got_g)
    loss_of(g, own_g, got_g)
    d_inners[f], d_ffn[g] = tie(d_inners[f], d_ffn[g])
    d_g = swap(d_ffn[g])
    back_f = dot_nt(d_inners[f], ffn_in_w)
    d_g, back_f = tie(d_g, back_f)
    own_f, got_f = halves(back_f)
    d_g = cat([d_ffn[g], d_g])
    g_out = dot_tn(cat([d_f, d_g]), cat([acts[f], acts[g]])).astype(BF)
    got_f, d_g, g_out = tie(got_f, d_g, g_out)
    s_out = reduce_rows(g_out[None])
    inner_back(g, d_g)
    after_back(f, own_f, got_f)
    d_inners[g], d_crosses[f] = tie(d_inners[g], d_crosses[f])
    c_f = swap(d_crosses[f])
    back_g = dot_nt(d_inners[g], ffn_in_w)
    c_f, d_inners[g], back_g = tie(c_f, d_inners[g], back_g)
    own_g, got_g = halves(back_g)
    g_in = dot_tn(cat([rows2[f], rows2[g]]), cat([d_inners[f], d_inners[g]])).astype(BF)
    got_g, g_in = tie(got_g, g_in)
    after_back(g, own_g, got_g)
    c_f, d_crosses[g] = tie(c_f, d_crosses[g])
    c_g = swap(d_crosses[g])
    d_rows1 = list(none)
    d_rows1[f] = [d_crosses[f], c_f]
    d_rows1[g] = [d_crosses[g], c_g]
    err_sq = sum(squares_of)
    gate_ffn_grad = sum(gate_grads)
    bias3 = sum(colsum(x.astype(F32)) for x in d_ffn)
    bias2 = sum(colsum(x.astype(F32)) for x in d_crosses)
    ffn_b_grad = sum(colsum(x.astype(F32)) for x in d_inners)
    shift2 = sum(colsum(x) for x in ffn_backs)
    scale2_g = sum(colsum(x * z) for x, z in zip(ffn_backs, unit2))

    bias0 = bias1 = norm3_g = gate0_g = cross_qb = cross_qgain = cross_dk = cross_dv = 0.0
    d_qpres, d_rows0, state = [list(none) for _ in range(3)]
    for c in (f, g):
        d_mixed = dot_nn(cat(d_rows1[c]), cross_out_t).astype(BF)
        if c == g:
            d_mixed, q_back = tie(d_mixed, q_back)
            own_q, got_q = halves(q_back)
        dqw, dk, dv, qdot, qgain = attend_back_cross(
            cross_q[c], cross_k, cross_v, d_mixed, cross_lse[c], cross_qp[c], cross_qs[c], qg_full[1, 0]
        )
        if c == f:
            d_rows1[g][1], dqw, qdot = tie(d_rows1[g][1], dqw, qdot)
        else:
            got_q, dqw, qdot = tie(got_q, dqw, qdot)
        cross_dk = cross_dk + dk
        cross_dv = cross_dv + dv
        cross_qgain = cross_qgain + qgain[0]
        r = cross_qs[c]
        dot = row_totals(qdot)
        d_qpres[c] = (dqw * r - cross_qp[c] * (r * r * r * dot / D)).astype(BF)
        cross_qb = cross_qb + colsum(d_qpres[c].astype(F32))
        q_back = dot_nt(d_qpres[c], cross_w[0])
    backs = {f: own_q + got_q.astype(F32), g: spread(q_back)}
    for c in (f, g):
        back = backs[c]
        norm3_g = norm3_g + colsum(back * unit1[c])
        bias0 = bias0 + colsum(back)
        state[c] = d_afters[c] + normal_back(back * norm3_row, unit1[c], scale1[c])
        gate0_g = gate0_g + colsum(branch0[c] * state[c])
        d_self = (gate_attn * state[c]).astype(BF)
        bias1 = bias1 + colsum(d_self.astype(F32))
        d_rows0[c] = [d_self, swap(d_self)]

    cross_dkw = cross_dk * qg_full[1, 1]
    kdot = row_totals(jnp.sum(cross_dkw * cross_kp, axis=-1, keepdims=True))
    cross_kgain = colsum(cross_dk * cross_kp * cross_kr)
    d_kpre = (cross_dkw * cross_kr - cross_kp * (cross_kr**3 * kdot / D)).astype(BF)
    d_v = cross_dv.astype(BF)
    g_cross = head_grads(
        [
            list(zip(rows1, d_qpres)),
            [(text_pieces, d_kpre)],
            [(text_pieces, d_v)],
            list(zip(d_rows1, cross_mixed)),
        ]
    )
    own_text, got_text = halves(dot_nt(d_kpre, cross_w[1]) + dot_nt(d_v, cross_w[2]))
    cross_b = jnp.stack([cross_qb, colsum(d_kpre.astype(F32)), colsum(d_v.astype(F32))])

    g_self_out = head_grads([list(zip(d_rows0, self_mixed))])
    d_mixed = dot_nn(cat([x for pieces in d_rows0 for x in pieces]), self_out_t).astype(BF)
    g_self_out, g_cross, s_out, g_in = tie(g_self_out, g_cross, s_out, g_in)
    d_mixed, g_self_out = tie(d_mixed, g_self_out)
    s_in = reduce_rows(g_in[None])
    ffn_out_g = s_out[0].astype(F32).T
    ffn_in_g = s_in[0].astype(F32)
    lse = jnp.concatenate(self_lse, axis=2)
    dqw, dkw, dv, qdot, kdot, self_qgain, self_kgain = attend_back_self(
        self_q, self_k, vv, d_mixed, lse, key_mask, qp, kp, qs, ks, qg_full[0, 0], qg_full[0, 1], cos, sin
    )
    dots = []
    for a, b in spans:
        dots.append(row_totals(jnp.concatenate([qdot[a:b], kdot[a:b]], axis=1)))
    dots = cat(dots)
    d_q = (dqw * qs - qp * (qs**3 * dots[:, 0:1] / D)).astype(BF)
    d_k = (dkw * ks - kp * (ks**3 * dots[:, 1:2] / D)).astype(BF)
    d_q, got_text = tie(d_q, got_text)
    text_g = own_text + got_text.astype(F32)
    text_g, d_k = tie(text_g, d_k)
    g_self, part, other = self_back(rows0, spans, heads_w, [d_q, d_k, dv])
    self_b = jnp.stack([colsum(g.astype(F32)) for g in (d_q, d_k, dv)])

    blank = jnp.zeros((D,), F32)
    wide = jnp.stack(
        [blank, blank, gate0_g, shift2, scale2_g, gate_ffn_grad, bias0, bias1, bias2, bias3, norm3_g]
        + [jnp.broadcast_to(err_sq, (D,))]
        + [blank] * 4
    )
    narrow = jnp.concatenate(
        [
            self_b.reshape(-1, HD),
            cross_b.reshape(-1, HD),
            jnp.stack([self_qgain[0], self_kgain[0], cross_qgain, cross_kgain]).reshape(-1, HD),
            ffn_b_grad.reshape(-1, HD),
        ],
        axis=0,
    )
    n_narrow = narrow.shape[0]
    narrow = jnp.pad(narrow.reshape(-1), (0, -narrow.size % (8 * D))).reshape(-1, D)
    sums, hidden_g, small = tail(
        ndp,
        [g_self, g_self_out, g_cross],
        part,
        other,
        state,
        unit0,
        cat(scale0),
        1.0 + scale_attn,
        jnp.concatenate([wide, narrow]),
        own_len,
    )
    self_qkv_g = sums[:3]
    self_out_g = sums[3].T
    cross_qkv_g = sums[4:7]
    cross_out_g = sums[7].T
    wide = small[:16]
    narrow = small[16:].reshape(-1)[: n_narrow * HD].reshape(n_narrow, HD)
    narrow = lax.dynamic_slice_in_dim(narrow, dp * w_low, w_low, 1)
    mine = lax.dynamic_slice_in_dim(wide, (dp * 2 + mp) * w_f32, w_f32, 1)
    mean_loss = wide[11, 0] / (jnp.sum(lengths).astype(F32) * D)
    nh = head_bias.size // head_bias.shape[-1]
    ng = qk_gain.size // qk_gain.shape[-1]
    return (
        cat(results)[None, :own_len],
        mean_loss,
        hidden_g.transpose(1, 0, 2),
        text_g[None],
        mine[:6],
        mine[6:10],
        mine[10],
        self_qkv_g,
        self_out_g,
        cross_qkv_g,
        cross_out_g,
        ffn_in_g,
        ffn_out_g,
        narrow[:nh].reshape(head_bias.shape),
        narrow[nh : nh + ng].reshape(qk_gain.shape),
        narrow[nh + ng :].reshape(ffn_bias.shape),
    )


def solution(mesh):
    in_specs = (
        P("dp", "mp", None),
        P("dp", "mp", None),
        P("dp", None, None),
        P(),
        P("dp", None, None),
        P("dp", "mp", None),
        P(None, ("dp", "mp")),
        P(None, ("dp", "mp")),
        P(("dp", "mp")),
        P(None, "dp", "mp"),
        P("mp", "dp"),
        P(None, "dp", "mp"),
        P("mp", "dp"),
        P("dp", "mp"),
        P("mp", "dp"),
        P(None, None, "mp", "dp"),
        P(None, None, "mp", "dp"),
        P("mp", "dp"),
    )
    out_specs = (
        P("dp", "mp", None),
        P(),
        P("dp", "mp", None),
        P("dp", "mp", None),
        P(None, ("dp", "mp")),
        P(None, ("dp", "mp")),
        P(("dp", "mp")),
        P(None, "dp", "mp"),
        P("mp", "dp"),
        P(None, "dp", "mp"),
        P("mp", "dp"),
        P("dp", "mp"),
        P("mp", "dp"),
        P(None, None, "mp", "dp"),
        P(None, None, "mp", "dp"),
        P("mp", "dp"),
    )
    return jax.shard_map(local, mesh=mesh, in_specs=in_specs, out_specs=out_specs, check_vma=False)
```

```python
import functools
import math

import jax
import jax.numpy as jnp
import numpy as np
from jax import lax
from jax.experimental import pallas as pl
from jax.experimental.pallas import tpu as pltpu
from jax.sharding import PartitionSpec as P

D = 1536
HD = 128
EPS = 1e-06
SCALE = HD ** (-0.5)
BF = jnp.bfloat16
F32 = jnp.float32
NEG = -1e30
SWAP = [(0, 1), (1, 0)]
VMEM_BYTES = 48 * 1024 * 1024


def rope_rates():
    pair_count = HD // 2
    third = pair_count // 3
    counts = [pair_count - 2 * third, third, third]
    rates = np.zeros((3, HD), np.float32)
    start = 0
    for axis_id, count in enumerate(counts):
        steps = np.arange(count, dtype=np.float32) / np.float32(count)
        values = np.exp(np.float32(-math.log(10000.0)) * steps).astype(np.float32)
        rates[axis_id, 2 * start : 2 * (start + count)] = np.repeat(values, 2)
        start += count
    return rates


def dot_nn(a, b):
    return lax.dot_general(a, b, (((1,), (0,)), ((), ())), preferred_element_type=F32)


def dot_nt(a, b):
    return lax.dot_general(a, b, (((1,), (1,)), ((), ())), preferred_element_type=F32)


def dot_tn(a, b):
    return lax.dot_general(a, b, (((0,), (0,)), ((), ())), preferred_element_type=F32)


def cost(flops, nbytes, trans=0):
    return pl.CostEstimate(flops=int(flops), bytes_accessed=int(nbytes), transcendentals=int(trans))


def params():
    return pltpu.CompilerParams(vmem_limit_bytes=VMEM_BYTES)


def turn(values):
    lane = lax.broadcasted_iota(jnp.int32, values.shape, 1)
    after = pltpu.roll(values, HD - 1, 1)
    before = pltpu.roll(values, 1, 1)
    return jnp.where(lane % 2 == 0, after, before)


def prep_kernel(qp, kp, qs, ks, qg, kg, cos, sin, q_out, k_out):
    c = cos[...]
    s = sin[...]
    for pre, scale, gain, out in ((qp, qs, qg, q_out), (kp, ks, kg, k_out)):
        v = pre[...] * scale[...] * gain[...]
        out[...] = (v * c + turn(v) * s).astype(BF)


def prep(qp, kp, qs, ks, qg, kg, cos, sin):
    rows, width = qp.shape
    head = pl.BlockSpec((rows, HD), lambda h: (0, h))
    col = pl.BlockSpec((rows, 1), lambda h: (0, 0))
    gain = pl.BlockSpec((1, HD), lambda h: (0, h))
    tab = pl.BlockSpec((rows, HD), lambda h: (0, 0))
    return pl.pallas_call(
        prep_kernel,
        grid=(width // HD,),
        in_specs=[head, head, col, col, gain, gain, tab, tab],
        out_specs=[head, head],
        out_shape=[jax.ShapeDtypeStruct((rows, width), BF)] * 2,
        compiler_params=params(),
        cost_estimate=cost(rows * width * 20, rows * width * 12),
        name="rope_prep",
    )(qp, kp, qs, ks, qg, kg, cos, sin)


def attend_kernel(masked, *refs):
    if masked:
        q, k, v, w, mask, out, lse, own, other = refs
    else:
        q, k, v, w, out, lse, own, other = refs
    st = dot_nt(k[...], q[...]) * SCALE
    if masked:
        st = st + mask[...]
    top = jnp.max(st, axis=0, keepdims=True)
    e = jnp.exp(st - top)
    total = jnp.sum(e, axis=0, keepdims=True)
    lse[0] = top + jnp.log(total)
    mixed = dot_tn(v[...], e.astype(BF)) * (1.0 / total)
    h = pl.program_id(0)
    out[:, pl.ds(pl.multiple_of(h * HD, HD), HD)] = mixed.T.astype(BF)

    @pl.when(h == pl.num_programs(0) - 1)
    def _():
        half = out.shape[0] // 2
        own[...] = dot_nt(out[:half], w[0])
        other[...] = dot_nt(out[half:], w[0]).astype(BF)


def attend(q, k, v, mask, weights, slab):
    nq, width = q.shape
    nk = k.shape[0]
    d = weights.shape[1]
    heads = width // HD
    qb = pl.BlockSpec((nq, HD), lambda h: (0, h))
    kb = pl.BlockSpec((nk, HD), lambda h: (0, h))
    ins = [qb, kb, kb, pl.BlockSpec((1, d, width), lambda h: (slab, 0, 0), pipeline_mode=pl.Buffered(1))]
    args = [q, k, v, weights]
    if mask is not None:
        ins.append(pl.BlockSpec((nk, 1), lambda h: (0, 0)))
        args.append(mask)
    return pl.pallas_call(
        functools.partial(attend_kernel, mask is not None),
        grid=(heads,),
        in_specs=ins,
        out_specs=[
            pl.BlockSpec((nq, width), lambda h: (0, 0)),
            pl.BlockSpec((1, 1, nq), lambda h: (h, 0, 0)),
            pl.BlockSpec((nq // 2, d), lambda h: (0, 0)),
            pl.BlockSpec((nq // 2, d), lambda h: (0, 0)),
        ],
        out_shape=[
            jax.ShapeDtypeStruct((nq, width), BF),
            jax.ShapeDtypeStruct((heads, 1, nq), F32),
            jax.ShapeDtypeStruct((nq // 2, d), F32),
            jax.ShapeDtypeStruct((nq // 2, d), BF),
        ],
        compiler_params=params(),
        cost_estimate=cost(4 * nq * nk * width * 3, 4 * nq * width + 4 * nk * width, nq * nk * heads),
        name="attend_fwd",
    )(*args)


def attend_back_kernel(self_form, *refs):
    if self_form:
        (q, k, v, do, lse, mask, qp, kp, qs, ks, qg, kg, cos, sin,
         dq_out, dk_out, dv_out, qdot, kdot, qgain, kgain) = refs
    else:
        q, k, v, do, lse, qp, qs, qg, dq_out, dk_out, dv_out, qdot, qgain = refs
    st = dot_nt(k[...], q[...]) * SCALE
    if self_form:
        st = st + mask[...]
    p = jnp.exp(st - lse[0])
    dp = dot_nt(v[...], do[...])
    inner = jnp.sum(dp * p, axis=0, keepdims=True)
    ds = (p * (dp - inner)).astype(BF)
    dv_out[...] = dot_nn(p.astype(BF), do[...]).astype(dv_out.dtype)
    dk = dot_nn(ds, q[...]) * SCALE
    dq = dot_tn(k[...], ds).T * SCALE
    sides = [(dq, qp, qs, qg, dq_out, qdot, qgain)]
    if self_form:
        dq = dq * cos[...] - turn(dq) * sin[...]
        dk = dk * cos[...] - turn(dk) * sin[...]
        sides = [(dq, qp, qs, qg, dq_out, qdot, qgain), (dk, kp, ks, kg, dk_out, kdot, kgain)]
    else:
        dk_out[...] = dk
    for grad, pre, scale, gain, out, dots, gains in sides:
        p_rows = pre[...]
        weighted = grad * gain[...]
        out[...] = weighted
        part = jnp.sum(weighted * p_rows, axis=1, keepdims=True)

        @pl.when(pl.program_id(0) == 0)
        def _():
            dots[...] = part

        @pl.when(pl.program_id(0) > 0)
        def _():
            dots[...] += part

        gains[...] = jnp.sum(grad * (p_rows * scale[...]), axis=0, keepdims=True)


def attend_back_self(q, k, v, do, lse, mask, qp, kp, qs, ks, qg, kg, cos, sin):
    n, width = q.shape
    heads = width // HD
    rows = pl.BlockSpec((n, HD), lambda h: (0, h))
    col = pl.BlockSpec((n, 1), lambda h: (0, 0))
    gain = pl.BlockSpec((1, HD), lambda h: (0, h))
    tab = pl.BlockSpec((n, HD), lambda h: (0, 0))
    lses = pl.BlockSpec((1, 1, n), lambda h: (h, 0, 0))
    full = jax.ShapeDtypeStruct((n, width), F32)
    cols = jax.ShapeDtypeStruct((n, 1), F32)
    gains = jax.ShapeDtypeStruct((1, width), F32)
    return pl.pallas_call(
        functools.partial(attend_back_kernel, True),
        grid=(heads,),
        in_specs=[rows, rows, rows, rows, lses, col, rows, rows, col, col, gain, gain, tab, tab],
        out_specs=[rows, rows, rows, col, col, gain, gain],
        out_shape=[full, full, jax.ShapeDtypeStruct((n, width), BF), cols, cols, gains, gains],
        compiler_params=params(),
        cost_estimate=cost(10 * n * n * width * 3, 26 * n * width, n * n * heads),
        name="attend_bwd_self",
    )(q, k, v, do, lse, mask, qp, kp, qs, ks, qg, kg, cos, sin)


def attend_back_cross(q, k, v, do, lse, qp, qs, qg):
    n, width = q.shape
    nk = k.shape[0]
    heads = width // HD
    rows = pl.BlockSpec((n, HD), lambda h: (0, h))
    keys = pl.BlockSpec((nk, HD), lambda h: (0, h))
    col = pl.BlockSpec((n, 1), lambda h: (0, 0))
    gain = pl.BlockSpec((1, HD), lambda h: (0, h))
    lses = pl.BlockSpec((1, 1, n), lambda h: (h, 0, 0))
    return pl.pallas_call(
        functools.partial(attend_back_kernel, False),
        grid=(heads,),
        in_specs=[rows, keys, keys, rows, lses, rows, col, gain],
        out_specs=[rows, keys, keys, col, gain],
        out_shape=[
            jax.ShapeDtypeStruct((n, width), F32),
            jax.ShapeDtypeStruct((nk, width), F32),
            jax.ShapeDtypeStruct((nk, width), F32),
            jax.ShapeDtypeStruct((n, 1), F32),
            jax.ShapeDtypeStruct((1, width), F32),
        ],
        compiler_params=params(),
        cost_estimate=cost(10 * n * nk * width * 3, 12 * n * width + 12 * nk * width, n * nk * heads),
        name="attend_bwd_cross",
    )(q, k, v, do, lse, qp, qs, qg)


def head_grads_kernel(plan, *refs):
    out = refs[-1]
    for i, terms in enumerate(plan):

        @pl.when(pl.program_id(0) == i)
        def _(terms=terms):
            total = None
            for a, b, lo, hi in terms:
                term = dot_tn(refs[a][...], refs[b][lo:hi])
                total = term if total is None else total + term
            out[0] = total.astype(BF)


def self_back_kernel(spans, *refs):
    n = 2 * len(spans)
    rows = refs[:n]
    weights = refs[n]
    heads = refs[n + 1 : n + 4]
    grads, part, other, acc = refs[n + 4 :]
    halves = [x for a, b in spans for x in ((a, (a + b) // 2), ((a + b) // 2, b))]
    for i in range(3):

        @pl.when(pl.program_id(0) == i)
        def _(i=i):
            total = None
            for x, (a, b) in zip(rows, halves):
                term = dot_tn(x[...], heads[i][a:b])
                total = term if total is None else total + term
            grads[0] = total.astype(BF)
            back = dot_nt(heads[i][...], weights[0])
            if i == 0:
                acc[...] = back
            elif i == 1:
                acc[...] += back
            else:
                back = acc[...] + back
                at = 0
                for a, b in spans:
                    half = (b - a) // 2
                    part[at : at + half] = back[a : a + half]
                    other[at : at + half] = back[a + half : b].astype(BF)
                    at += half


def self_back(rows, spans, weights, heads):
    n, width = heads[0].shape
    d = rows[0].shape[1]
    once = lambda x: pl.BlockSpec(x.shape, lambda i: (0, 0), pipeline_mode=pl.Buffered(1))
    return pl.pallas_call(
        functools.partial(self_back_kernel, spans),
        grid=(3,),
        in_specs=[once(x) for x in rows]
        + [pl.BlockSpec((1, d, width), lambda i: (i, 0, 0))]
        + [once(x) for x in heads],
        out_specs=[
            pl.BlockSpec((1, d, width), lambda i: (i, 0, 0)),
            pl.BlockSpec((n // 2, d), lambda i: (0, 0)),
            pl.BlockSpec((n // 2, d), lambda i: (0, 0)),
        ],
        out_shape=[
            jax.ShapeDtypeStruct((3, d, width), BF),
            jax.ShapeDtypeStruct((n // 2, d), F32),
            jax.ShapeDtypeStruct((n // 2, d), BF),
        ],
        scratch_shapes=[pltpu.VMEM((n, d), F32)],
        compiler_params=params(),
        cost_estimate=cost(12 * n * d * width, 30e6),
        name="self_back",
    )(*rows, weights, *heads)


def head_grads(products):
    arrays, plan = [], []

    def place(x):
        for i, y in enumerate(arrays):
            if x is y:
                return i
        arrays.append(x)
        return len(arrays) - 1

    for pairs in products:
        terms = []
        for pieces, b in pairs:
            at = 0
            for a in pieces:
                terms.append((place(a), place(b), at, at + a.shape[0]))
                at += a.shape[0]
        plan.append(terms)
    m, n = products[0][0][0][0].shape[1], products[0][0][1].shape[1]
    rows = sum(b.shape[0] for pairs in products for _, b in pairs)
    return pl.pallas_call(
        functools.partial(head_grads_kernel, plan),
        grid=(len(products),),
        in_specs=[
            pl.BlockSpec(x.shape, lambda i: (0, 0), pipeline_mode=pl.Buffered(1)) for x in arrays
        ],
        out_specs=pl.BlockSpec((1, m, n), lambda i: (i, 0, 0)),
        out_shape=jax.ShapeDtypeStruct((len(products), m, n), BF),
        compiler_params=params(),
        cost_estimate=cost(2 * rows * m * n, 2 * sum(x.size for x in arrays) + 2 * len(products) * m * n),
        name="head_grads",
    )(*arrays)


def tail_kernel(ndp, counts, nc, *refs):
    n = len(counts)
    g = refs[:n]
    state = refs[n : n + nc]
    unit = refs[n + nc : n + 2 * nc]
    (part, other, lns, ones, small, gsum, hgrad, small_out,
     mine, got, send, slot, ybuf, pbuf, stbuf, ubuf, vals, inbox,
     mine_sem, got_send, got_recv, ring_send, ring_recv, y_sem, load_sem, sum_send, sum_recv) = refs[n + 2 * nc :]
    chips = ndp // 2
    bits = ndp.bit_length() - 1
    dp = lax.axis_index("dp")
    mp = lax.axis_index("mp")
    core = lax.rem(dp, 2)
    chip = lax.div(dp, 2)
    odd = lax.rem(chip, 2)
    row = lax.div(chip, 2)
    place = row * (1 - odd) + (chips - 1 - row) * odd
    way = 1 - 2 * core

    def chip_at(shift):
        spot = lax.rem(place + way * shift + 2 * chips, chips)
        back = lax.div(spot, chips // 2)
        return 2 * spot * (1 - back) + (2 * (chips - 1 - spot) + 1) * back

    after = 2 * chip_at(1) + core
    before = 2 * chip_at(-1) + core
    mates = [dp + (1 - 2 * lax.rem(lax.div(dp, 1 << b), 2)) * (1 << b) for b in range(bits)]
    mesh_id = pl.DeviceIdType.MESH

    barrier = pltpu.get_barrier_semaphore()
    for device in (after, before, *mates):
        pl.semaphore_signal(barrier, inc=1, device_id=(device, mp), device_id_type=mesh_id)
    pl.semaphore_signal(barrier, inc=1, device_id=(dp, 1 - mp), device_id_type=mesh_id)
    pl.semaphore_wait(barrier, 3 + bits)

    def remote(src, dst, s_sem, r_sem, device):
        return pltpu.make_async_remote_copy(
            src_ref=src, dst_ref=dst, send_sem=s_sem, recv_sem=r_sem, device_id=device, device_id_type=mesh_id
        )

    starts = [sum(counts[:i]) for i in range(n)]
    total = sum(counts)
    cuts = [(0, (total + 1) // 2), ((total + 1) // 2, total)]

    def to_mate(s, i):
        return remote(
            g[i].at[:, chip_at(1 + s), 1 - core],
            got.at[s, pl.ds(starts[i], counts[i])],
            got_send.at[i, s],
            got_recv.at[i, s],
            (mates[0], mp),
        )

    def to_self(s, i):
        return pltpu.make_async_copy(
            g[i].at[:, chip_at(-1 - s), core], mine.at[s, pl.ds(starts[i], counts[i])], mine_sem.at[i, s]
        )

    def along(s, half):
        lo, hi = cuts[half]
        return remote(
            send.at[s, pl.ds(lo, hi - lo)],
            slot.at[s, pl.ds(lo, hi - lo)],
            ring_send.at[half, s],
            ring_recv.at[half, s],
            (after, mp),
        )

    def sum_copy(j):
        if j < bits:
            return remote(vals.at[j], inbox.at[j], sum_send.at[j], sum_recv.at[j], (mates[j], mp))
        return remote(
            vals.at[j, pl.ds(0, 16)], inbox.at[j, pl.ds(0, 16)], sum_send.at[j], sum_recv.at[j], (dp, 1 - mp)
        )

    y_copy = remote(other, ybuf, y_sem.at[0], y_sem.at[1], (dp, 1 - mp))
    for s in range(chips):
        for i in range(n):
            to_mate(s, i).start()
            to_self(s, i).start()
        if s == 0:
            y_copy.start()
    pairs = [(part, pbuf)]
    at = 0
    for st, un in zip(state, unit):
        span = pl.ds(at, st.shape[0])
        pairs += [(st, stbuf.at[span]), (un, ubuf.at[span])]
        at += st.shape[0]
    loads = [pltpu.make_async_copy(src, dst, load_sem.at[i]) for i, (src, dst) in enumerate(pairs)]
    for load in loads:
        load.start()

    def finish_rows():
        for load in loads:
            load.wait()
        y_copy.wait_recv()
        rows, width = pbuf.shape
        block = 80 if rows % 80 == 0 else 16
        gain = ones[...]

        def body(i, sums):
            at = pl.ds(pl.multiple_of(i * block, block), block)
            back = pbuf[at, :] + ybuf[at, :].astype(F32)
            z = ubuf[at, :]
            grad = back * gain
            mean_g = jnp.mean(grad, axis=1, keepdims=True)
            mean_gz = jnp.mean(grad * z, axis=1, keepdims=True)
            hgrad[at, :] = stbuf[at, :] + lns[at, :] * (grad - mean_g - z * mean_gz)
            return (
                sums[0] + jnp.sum(back, axis=0, keepdims=True),
                sums[1] + jnp.sum(back * z, axis=0, keepdims=True),
            )

        zero = jnp.zeros((1, width), F32)
        sums = lax.fori_loop(0, rows // block, body, (zero, zero))
        vals[0] = small[...]
        vals[0, 0:1, :] = sums[0]
        vals[0, 1:2, :] = sums[1]
        sum_copy(0).start()

    def sum_step(j):
        sum_copy(j).wait_recv()
        if j < bits:
            vals[j + 1] = vals[j] + inbox[j]
            sum_copy(j + 1).start()
        else:
            small_out[...] = vals[j]
            small_out[0:16, :] = vals[j, 0:16, :] + inbox[j, 0:16, :]

    first = min(2, chips - 1)
    done = 0
    for s in range(chips):
        for i in range(n):
            to_self(s, i).wait()
            to_mate(s, i).wait_recv()
        for half in range(2):
            lo, hi = cuts[half]
            value = mine[s, lo:hi].astype(F32) + got[s, lo:hi].astype(F32)
            if s > 0:
                along(s - 1, half).wait_recv()
                value = value + slot[s - 1, lo:hi].astype(F32)
            if s < chips - 1:
                send[s, lo:hi] = value.astype(BF)
                along(s, half).start()
            else:
                gsum[lo:hi] = value
        if s == first:
            finish_rows()
        elif s > first and done <= bits:
            sum_step(done)
            done += 1
    while done <= bits:
        sum_step(done)
        done += 1
    for s in range(chips):
        for i in range(n):
            to_mate(s, i).wait_send()
        if s < chips - 1:
            for half in range(2):
                along(s, half).wait_send()
    y_copy.wait_send()
    for j in range(bits + 1):
        sum_copy(j).wait_send()


def tail(ndp, grads, part, other, state, unit, lns, ones, small):
    chips = ndp // 2
    bits = ndp.bit_length() - 1
    split = [x.reshape(x.shape[0], chips, 2, x.shape[1] // ndp, x.shape[2]) for x in grads]
    counts = tuple(x.shape[0] for x in grads)
    total = sum(counts)
    r, w = split[0].shape[3:]
    rows, width = part.shape
    n = len(grads)
    nc = len(state)
    hbm = pl.BlockSpec(memory_space=pl.ANY)
    vmem = pl.BlockSpec(memory_space=pltpu.VMEM)
    dma = pltpu.SemaphoreType.DMA
    return pl.pallas_call(
        functools.partial(tail_kernel, ndp, counts, nc),
        in_specs=[hbm] * (n + 2 * nc) + [hbm, hbm, vmem, vmem, vmem],
        out_specs=[vmem] * 3,
        out_shape=[
            jax.ShapeDtypeStruct((total, r, w), F32),
            jax.ShapeDtypeStruct((rows, width), F32),
            jax.ShapeDtypeStruct(small.shape, F32),
        ],
        scratch_shapes=[
            pltpu.VMEM((chips, total, r, w), BF),
            pltpu.VMEM((chips, total, r, w), BF),
            pltpu.VMEM((chips - 1, total, r, w), BF),
            pltpu.VMEM((chips - 1, total, r, w), BF),
            pltpu.VMEM((rows, width), BF),
            pltpu.VMEM((rows, width), F32),
            pltpu.VMEM((rows, width), F32),
            pltpu.VMEM((rows, width), F32),
            pltpu.VMEM((bits + 1,) + small.shape, F32),
            pltpu.VMEM((bits + 1,) + small.shape, F32),
            dma((n, chips)),
            dma((n, chips)),
            dma((n, chips)),
            dma((2, chips - 1)),
            dma((2, chips - 1)),
            dma((2,)),
            dma((1 + 2 * nc,)),
            dma((bits + 1,)),
            dma((bits + 1,)),
        ],
        compiler_params=pltpu.CompilerParams(
            vmem_limit_bytes=58 * 1024 * 1024, collective_id=0, has_side_effects=True
        ),
        cost_estimate=cost(1e6, 1e6),
        name="tail_sums",
    )(*split, *state, *unit, part, other, lns, ones, small)


def normal(values):
    center = values - jnp.mean(values, axis=-1, keepdims=True)
    scale = lax.rsqrt(jnp.mean(center * center, axis=-1, keepdims=True) + EPS)
    return center * scale, scale


def normal_back(grad, unit, scale):
    mean_g = jnp.mean(grad, axis=-1, keepdims=True)
    mean_gz = jnp.mean(grad * unit, axis=-1, keepdims=True)
    return scale * (grad - mean_g - unit * mean_gz)


def swap(values):
    return lax.ppermute(values, "mp", SWAP)


def collect(own):
    pieces = [own, swap(own)]
    return jnp.concatenate(pieces, axis=0), pieces


def spread(partial):
    half = partial.shape[0] // 2
    return partial[:half] + swap(partial[half:].astype(BF)).astype(F32)


def halves(partial):
    half = partial.shape[0] // 2
    return partial[:half], swap(partial[half:].astype(BF))


def row_totals(own):
    half = own.shape[0] // 2
    return own + swap(jnp.concatenate([own[half:], own[:half]], axis=0))


def squares(values):
    return jnp.sum(values * values, axis=-1, keepdims=True)


def colsum(values):
    return jnp.sum(values, axis=0, dtype=F32)


def tie(*values):
    return lax.optimization_barrier(values)


def partners(ndp, bit):
    return [(i, i ^ (1 << bit)) for i in range(ndp)]


def gather_small(flat, ndp, dp, mp):
    rows = flat[None]
    got = swap(rows)
    rows = jnp.where(mp == 0, jnp.concatenate([rows, got]), jnp.concatenate([got, rows]))
    for bit in range(ndp.bit_length() - 1):
        got = lax.ppermute(rows, "dp", partners(ndp, bit))
        low = (dp >> bit) % 2 == 0
        rows = jnp.where(low, jnp.concatenate([rows, got]), jnp.concatenate([got, rows]))
    return rows


def chunks_of(padded):
    first = padded // 2 // 16 * 16
    return [(0, first), (first, padded)]


def local(
    hidden,
    text_states,
    time_emb,
    lengths,
    positions,
    teacher,
    modulation,
    out_bias,
    norm3_gain,
    self_qkv,
    self_out,
    cross_qkv,
    cross_out,
    ffn_in,
    ffn_out,
    head_bias,
    qk_gain,
    ffn_bias,
):
    ndp = lax.axis_size("dp")
    dp = lax.axis_index("dp")
    mp = lax.axis_index("mp")
    own_len = hidden.shape[1]
    length = 2 * own_len
    padded = (own_len + 15) // 16 * 16
    pad = padded - own_len
    cuts = chunks_of(padded)

    f32_part = jnp.concatenate([modulation, out_bias, norm3_gain[None]], axis=0)
    hb = head_bias.reshape(-1, head_bias.shape[-1])
    qg = qk_gain.reshape(-1, qk_gain.shape[-1])
    low_part = jnp.concatenate([hb, qg, ffn_bias], axis=0).astype(F32)
    n_f32, w_f32 = f32_part.shape
    n_low, w_low = low_part.shape
    flat = jnp.concatenate([f32_part.reshape(-1), low_part.reshape(-1)])
    n_flat = flat.shape[0]
    flat_all = gather_small(jnp.pad(flat, (0, -n_flat % 128)), ndp, dp, mp)[:, :n_flat]
    f32_all = flat_all[:, : n_f32 * w_f32].reshape(2 * ndp, n_f32, w_f32)
    f32_all = f32_all.transpose(1, 0, 2).reshape(n_f32, -1)
    low_all = flat_all[:, n_f32 * w_f32 :].reshape(ndp, 2, n_low, w_low)
    low_all = lax.dynamic_index_in_dim(low_all, mp, 1, False)
    low_all = low_all.transpose(1, 0, 2).reshape(n_low, -1)
    mod_full = f32_all[:6]
    out_bias_full = f32_all[6:10]
    norm3_full = f32_all[10]
    hb_full = low_all[: hb.shape[0]].reshape(2, 3, -1)
    qg_full = low_all[hb.shape[0] : hb.shape[0] + qg.shape[0]].reshape(2, 2, 1, -1)
    ffn_bias_full = low_all[hb.shape[0] + qg.shape[0] :].reshape(-1)

    def whole(shards):
        return lax.all_gather(shards, "dp", axis=1, tiled=True)

    heads_w = whole(jnp.concatenate([self_qkv, self_out.T[None], cross_qkv, cross_out.T[None]]))
    self_w = heads_w[:4]
    cross_w = heads_w[4:]
    ffn_w = whole(jnp.stack([ffn_in, ffn_out.T]))
    self_out_t = self_w[3]
    cross_out_t = cross_w[3]
    ffn_in_w = ffn_w[0]
    ffn_out_t = ffn_w[1]

    signals = mod_full + time_emb[0]
    shift_attn, scale_attn, gate_attn, shift_ffn, scale_ffn, gate_ffn = [
        signals[i : i + 1] for i in range(6)
    ]
    clip_length = lax.dynamic_index_in_dim(lengths, dp, 0, False)

    def own_chunks(array):
        full = jnp.pad(array, ((0, pad), (0, 0)))
        return [full[a:b] for a, b in cuts]

    hid = own_chunks(hidden[0])
    teach = own_chunks(teacher[0])
    index = jnp.arange(padded)
    pos_pad = jnp.pad(positions[0].reshape(3, 2, own_len), ((0, 0), (0, 0), (0, pad)))

    def both(own, other):
        return jnp.concatenate([x[a:b] for a, b in cuts for x in (own, other)], axis=0)

    def slot_valid(half):
        return (index < own_len) & (half * own_len + index < clip_length)

    own_valid = slot_valid(mp)
    key_valid = both(own_valid, slot_valid(1 - mp))
    key_mask = jnp.where(key_valid, 0.0, NEG).astype(F32)[:, None]
    row_valid = [own_valid.astype(F32)[a:b, None] for a, b in cuts]
    pos_own = lax.dynamic_index_in_dim(pos_pad, mp, 1, False)
    pos_other = lax.dynamic_index_in_dim(pos_pad, 1 - mp, 1, False)
    rates = rope_rates()
    angle = sum(
        both(pos_own[i], pos_other[i]).astype(F32)[:, None] * rates[i][None, :] for i in range(3)
    )
    even = np.arange(HD) % 2 == 0
    cos = jnp.cos(angle)
    sin = jnp.sin(angle) * np.where(even, -1.0, 1.0).astype(np.float32)
    ends = np.cumsum([0] + [2 * (b - a) for a, b in cuts])
    spans = [(int(ends[i]), int(ends[i + 1])) for i in range(len(cuts))]
    nc = len(cuts)

    out_rows = [out_bias_full[i : i + 1] for i in range(4)]
    norm3_row = norm3_full[None]
    ffn_bias_row = ffn_bias_full[None]
    bias_rows = [hb_full[i, j][None] for i in range(2) for j in range(3)]
    late = [gate_attn, shift_ffn, scale_ffn, gate_ffn, norm3_row, ffn_bias_row, key_mask, cos, sin]
    late += out_rows + bias_rows + row_valid
    heads_w, *late = tie(heads_w, *late)
    gate_attn, shift_ffn, scale_ffn, gate_ffn, norm3_row, ffn_bias_row, key_mask, cos, sin = late[:9]
    out_rows, bias_rows, row_valid = late[9:13], late[13:19], late[19:]
    self_w = heads_w[:4]
    cross_w = heads_w[4:]
    self_out_t = heads_w[3]
    cross_out_t = heads_w[7]

    text_rows, text_pieces = collect(text_states[0])

    res0, unit0, scale0, rows0 = [], [], [], []
    qp, kp, vv, qs, ks = [], [], [], [], []
    for c in range(nc):
        r = hid[c].astype(F32)
        z, s = normal(r)
        x = (z * (1.0 + scale_attn) + shift_attn).astype(BF)
        rows, pieces = collect(x)
        qc = dot_nn(rows, self_w[0]) + bias_rows[0]
        kc = dot_nn(rows, self_w[1]) + bias_rows[1]
        vc = (dot_nn(rows, self_w[2]) + bias_rows[2]).astype(BF)
        tot = row_totals(jnp.concatenate([squares(qc), squares(kc)], axis=1))
        res0.append(r)
        unit0.append(z)
        scale0.append(s)
        rows0 += pieces
        qp.append(qc)
        kp.append(kc)
        vv.append(vc)
        scales = lax.rsqrt(tot / D + EPS)
        qs.append(scales[:, 0:1])
        ks.append(scales[:, 1:2])
    qp, kp, vv = [jnp.concatenate(x, axis=0) for x in (qp, kp, vv)]
    qs, ks = [jnp.concatenate(x, axis=0) for x in (qs, ks)]
    self_q, self_k = prep(qp, kp, qs, ks, qg_full[0, 0], qg_full[0, 1], cos, sin)

    none = [None] * nc
    f, g = nc - 1, 0
    self_mixed, self_lse, branch0, unit1, scale1, after_self = [list(none) for _ in range(6)]
    cross_mixed, cross_lse, cross_q, cross_qp, cross_qs = [list(none) for _ in range(5)]
    rows1, rows2, unit2, scale2, after = [list(none) for _ in range(5)]

    def self_rows(c):
        a, b = spans[c]
        self_mixed[c], self_lse[c], own, other = attend(self_q[a:b], self_k, vv, key_mask, heads_w, 3)
        return own, swap(other)

    def cross_query(c, own, got):
        branch0[c] = own + got.astype(F32) + out_rows[1]
        after_self[c] = res0[c] + gate_attn * branch0[c]
        unit1[c], scale1[c] = normal(after_self[c])
        x = (unit1[c] * norm3_row + out_rows[0]).astype(BF)
        rows1[c] = [x, swap(x)]

    def cross_prepare(c, got=None):
        qc = dot_nn(jnp.concatenate(rows1[c], axis=0), heads_w[4]) + bias_rows[3]
        if got is not None:
            qc, got = tie(qc, got)
        cross_qp[c] = qc
        cross_qs[c] = lax.rsqrt(row_totals(squares(qc)) / D + EPS)
        cross_q[c] = (qc * cross_qs[c] * qg_full[1, 0]).astype(BF)
        return got

    def cross_attend(c):
        cross_mixed[c], cross_lse[c], own, other = attend(cross_q[c], cross_k, cross_v, None, heads_w, 7)
        return own, other

    def ffn_input(c, own, got):
        after[c] = after_self[c] + own + got.astype(F32) + out_rows[2]
        unit2[c], scale2[c] = normal(after[c])
        return (unit2[c] * (1.0 + scale_ffn) + shift_ffn).astype(BF)

    own_f, got_f = self_rows(f)
    own_g, got_g = self_rows(g)
    got_f, own_g = tie(got_f, own_g)
    cross_query(f, own_f, got_f)
    rows1[f][0], text_rows = tie(rows1[f][0], text_rows)
    cross_query(g, own_g, got_g)
    cross_kp = dot_nn(text_rows, cross_w[1]) + bias_rows[4]
    cross_v = (dot_nn(text_rows, cross_w[2]) + bias_rows[5]).astype(BF)
    rows1[f][1], cross_kp, cross_v = tie(rows1[f][1], cross_kp, cross_v)
    cross_ks = row_totals(squares(cross_kp))
    cross_kr = lax.rsqrt(cross_ks / D + EPS)
    cross_k = (cross_kp * cross_kr * qg_full[1, 1]).astype(BF)
    cross_prepare(f)
    own_f, other_f = cross_attend(f)
    rows1[g][1], other_f = tie(rows1[g][1], other_f)
    got_f = swap(other_f)
    got_f = cross_prepare(g, got_f)
    x_f = ffn_input(f, own_f, got_f)
    cross_q[g], x_f = tie(cross_q[g], x_f)
    y_f = swap(x_f)
    own_g, other_g = cross_attend(g)
    y_f, own_g, other_g = tie(y_f, own_g, other_g)
    rows2[f] = jnp.concatenate([x_f, y_f], axis=0)
    got_g = swap(other_g)

    def cat(parts):
        return jnp.concatenate(parts, axis=0)

    def reduce_rows(full):
        return lax.psum_scatter(full, "dp", scatter_dimension=1, tiled=True)

    acts, slopes, results, errors, d_ffn, d_inners, d_afters, d_crosses = [list(none) for _ in range(8)]
    squares_of, gate_grads, ffn_backs = [list(none) for _ in range(3)]

    def inner_of(c):
        inner = dot_nn(rows2[c], ffn_in_w) + ffn_bias_row
        act, back = jax.vjp(functools.partial(jax.nn.gelu, approximate=True), inner)
        acts[c] = act.astype(BF)
        slopes[c] = back(jnp.ones_like(inner))[0].astype(BF)

    def loss_of(c, own, got):
        branch = own + got.astype(F32) + out_rows[3]
        result = after[c] + gate_ffn * branch
        results[c] = result.astype(BF)
        errors[c] = (result - teach[c].astype(F32)) * row_valid[c]
        d_ffn[c] = (gate_ffn * errors[c]).astype(BF)
        squares_of[c] = jnp.sum(errors[c] * errors[c])
        gate_grads[c] = colsum(branch * errors[c])

    def inner_back(c, rows):
        d_inners[c] = (dot_nn(rows, ffn_out_t) * slopes[c].astype(F32)).astype(BF)

    def after_back(c, own, got):
        back = own + got.astype(F32)
        ffn_backs[c] = back
        d_afters[c] = errors[c] + normal_back(back * (1.0 + scale_ffn), unit2[c], scale2[c])
        d_crosses[c] = d_afters[c].astype(BF)

    inner_of(f)
    got_g, acts[f] = tie(got_g, acts[f])
    x_g = ffn_input(g, own_g, got_g)
    acts[f], x_g = tie(acts[f], x_g)
    y_g = swap(x_g)
    branch_f = dot_nt(acts[f], ffn_out_t)
    y_g, branch_f = tie(y_g, branch_f)
    rows2[g] = jnp.concatenate([x_g, y_g], axis=0)
    own_f, got_f = halves(branch_f)
    inner_of(g)
    got_f, acts[g] = tie(got_f, acts[g])
    loss_of(f, own_f, got_f)
    acts[g], d_ffn[f] = tie(acts[g], d_ffn[f])
    d_f = swap(d_ffn[f])
    branch_g = dot_nt(acts[g], ffn_out_t)
    d_f, branch_g = tie(d_f, branch_g)
    own_g, got_g = halves(branch_g)
    d_f = cat([d_ffn[f], d_f])
    inner_back(f, d_f)
    d_inners[f], got_g = tie(d_inners[f], got_g)
    loss_of(g, own_g, got_g)
    d_inners[f], d_ffn[g] = tie(d_inners[f], d_ffn[g])
    d_g = swap(d_ffn[g])
    back_f = dot_nt(d_inners[f], ffn_in_w)
    d_g, back_f = tie(d_g, back_f)
    own_f, got_f = halves(back_f)
    d_g = cat([d_ffn[g], d_g])
    g_out = dot_tn(cat([d_f, d_g]), cat([acts[f], acts[g]])).astype(BF)
    got_f, d_g, g_out = tie(got_f, d_g, g_out)
    s_out = reduce_rows(g_out[None])
    inner_back(g, d_g)
    after_back(f, own_f, got_f)
    d_inners[g], d_crosses[f] = tie(d_inners[g], d_crosses[f])
    c_f = swap(d_crosses[f])
    back_g = dot_nt(d_inners[g], ffn_in_w)
    c_f, d_inners[g], back_g = tie(c_f, d_inners[g], back_g)
    own_g, got_g = halves(back_g)
    g_in = dot_tn(cat([rows2[f], rows2[g]]), cat([d_inners[f], d_inners[g]])).astype(BF)
    got_g, g_in = tie(got_g, g_in)
    after_back(g, own_g, got_g)
    c_f, d_crosses[g] = tie(c_f, d_crosses[g])
    c_g = swap(d_crosses[g])
    d_rows1 = list(none)
    d_rows1[f] = [d_crosses[f], c_f]
    d_rows1[g] = [d_crosses[g], c_g]
    err_sq = sum(squares_of)
    gate_ffn_grad = sum(gate_grads)
    bias3 = sum(colsum(x.astype(F32)) for x in d_ffn)
    bias2 = sum(colsum(x.astype(F32)) for x in d_crosses)
    ffn_b_grad = sum(colsum(x.astype(F32)) for x in d_inners)
    shift2 = sum(colsum(x) for x in ffn_backs)
    scale2_g = sum(colsum(x * z) for x, z in zip(ffn_backs, unit2))

    bias0 = bias1 = norm3_g = gate0_g = cross_qb = cross_qgain = cross_dk = cross_dv = 0.0
    d_qpres, d_rows0, state = [list(none) for _ in range(3)]
    for c in (f, g):
        d_mixed = dot_nn(cat(d_rows1[c]), cross_out_t).astype(BF)
        if c == g:
            d_mixed, q_back = tie(d_mixed, q_back)
            own_q, got_q = halves(q_back)
        dqw, dk, dv, qdot, qgain = attend_back_cross(
            cross_q[c], cross_k, cross_v, d_mixed, cross_lse[c], cross_qp[c], cross_qs[c], qg_full[1, 0]
        )
        if c == f:
            d_rows1[g][1], dqw, qdot = tie(d_rows1[g][1], dqw, qdot)
        else:
            got_q, dqw, qdot = tie(got_q, dqw, qdot)
        cross_dk = cross_dk + dk
        cross_dv = cross_dv + dv
        cross_qgain = cross_qgain + qgain[0]
        r = cross_qs[c]
        dot = row_totals(qdot)
        d_qpres[c] = (dqw * r - cross_qp[c] * (r * r * r * dot / D)).astype(BF)
        cross_qb = cross_qb + colsum(d_qpres[c].astype(F32))
        q_back = dot_nt(d_qpres[c], cross_w[0])
    backs = {f: own_q + got_q.astype(F32), g: spread(q_back)}
    for c in (f, g):
        back = backs[c]
        norm3_g = norm3_g + colsum(back * unit1[c])
        bias0 = bias0 + colsum(back)
        state[c] = d_afters[c] + normal_back(back * norm3_row, unit1[c], scale1[c])
        gate0_g = gate0_g + colsum(branch0[c] * state[c])
        d_self = (gate_attn * state[c]).astype(BF)
        bias1 = bias1 + colsum(d_self.astype(F32))
        d_rows0[c] = [d_self, swap(d_self)]

    cross_dkw = cross_dk * qg_full[1, 1]
    kdot = row_totals(jnp.sum(cross_dkw * cross_kp, axis=-1, keepdims=True))
    cross_kgain = colsum(cross_dk * cross_kp * cross_kr)
    d_kpre = (cross_dkw * cross_kr - cross_kp * (cross_kr**3 * kdot / D)).astype(BF)
    d_v = cross_dv.astype(BF)
    g_cross = head_grads(
        [
            list(zip(rows1, d_qpres)),
            [(text_pieces, d_kpre)],
            [(text_pieces, d_v)],
            list(zip(d_rows1, cross_mixed)),
        ]
    )
    own_text, got_text = halves(dot_nt(d_kpre, cross_w[1]) + dot_nt(d_v, cross_w[2]))
    cross_b = jnp.stack([cross_qb, colsum(d_kpre.astype(F32)), colsum(d_v.astype(F32))])

    g_self_out = head_grads([list(zip(d_rows0, self_mixed))])
    d_mixed = dot_nn(cat([x for pieces in d_rows0 for x in pieces]), self_out_t).astype(BF)
    d_mixed, g_self_out, g_cross, s_out, g_in = tie(d_mixed, g_self_out, g_cross, s_out, g_in)
    s_in = reduce_rows(g_in[None])
    ffn_out_g = s_out[0].astype(F32).T
    ffn_in_g = s_in[0].astype(F32)
    lse = jnp.concatenate(self_lse, axis=2)
    dqw, dkw, dv, qdot, kdot, self_qgain, self_kgain = attend_back_self(
        self_q, self_k, vv, d_mixed, lse, key_mask, qp, kp, qs, ks, qg_full[0, 0], qg_full[0, 1], cos, sin
    )
    dots = []
    for a, b in spans:
        dots.append(row_totals(jnp.concatenate([qdot[a:b], kdot[a:b]], axis=1)))
    dots = cat(dots)
    d_q = (dqw * qs - qp * (qs**3 * dots[:, 0:1] / D)).astype(BF)
    d_k = (dkw * ks - kp * (ks**3 * dots[:, 1:2] / D)).astype(BF)
    d_q, got_text = tie(d_q, got_text)
    text_g = own_text + got_text.astype(F32)
    text_g, d_k = tie(text_g, d_k)
    g_self, part, other = self_back(rows0, spans, heads_w, [d_q, d_k, dv])
    self_b = jnp.stack([colsum(g.astype(F32)) for g in (d_q, d_k, dv)])

    blank = jnp.zeros((D,), F32)
    wide = jnp.stack(
        [blank, blank, gate0_g, shift2, scale2_g, gate_ffn_grad, bias0, bias1, bias2, bias3, norm3_g]
        + [jnp.broadcast_to(err_sq, (D,))]
        + [blank] * 4
    )
    narrow = jnp.concatenate(
        [
            self_b.reshape(-1, HD),
            cross_b.reshape(-1, HD),
            jnp.stack([self_qgain[0], self_kgain[0], cross_qgain, cross_kgain]).reshape(-1, HD),
            ffn_b_grad.reshape(-1, HD),
        ],
        axis=0,
    )
    n_narrow = narrow.shape[0]
    narrow = jnp.pad(narrow.reshape(-1), (0, -narrow.size % (8 * D))).reshape(-1, D)
    sums, hidden_g, small = tail(
        ndp,
        [g_self, g_self_out, g_cross],
        part,
        other,
        state,
        unit0,
        cat(scale0),
        1.0 + scale_attn,
        jnp.concatenate([wide, narrow]),
    )
    self_qkv_g = sums[:3]
    self_out_g = sums[3].T
    cross_qkv_g = sums[4:7]
    cross_out_g = sums[7].T
    wide = small[:16]
    narrow = small[16:].reshape(-1)[: n_narrow * HD].reshape(n_narrow, HD)
    narrow = lax.dynamic_slice_in_dim(narrow, dp * w_low, w_low, 1)
    mine = lax.dynamic_slice_in_dim(wide, (dp * 2 + mp) * w_f32, w_f32, 1)
    mean_loss = wide[11, 0] / (jnp.sum(lengths).astype(F32) * D)
    nh = head_bias.size // head_bias.shape[-1]
    ng = qk_gain.size // qk_gain.shape[-1]
    return (
        cat(results)[None, :own_len],
        mean_loss,
        hidden_g[None, :own_len],
        text_g[None],
        mine[:6],
        mine[6:10],
        mine[10],
        self_qkv_g,
        self_out_g,
        cross_qkv_g,
        cross_out_g,
        ffn_in_g,
        ffn_out_g,
        narrow[:nh].reshape(head_bias.shape),
        narrow[nh : nh + ng].reshape(qk_gain.shape),
        narrow[nh + ng :].reshape(ffn_bias.shape),
    )


def solution(mesh):
    in_specs = (
        P("dp", "mp", None),
        P("dp", "mp", None),
        P("dp", None, None),
        P(),
        P("dp", None, None),
        P("dp", "mp", None),
        P(None, ("dp", "mp")),
        P(None, ("dp", "mp")),
        P(("dp", "mp")),
        P(None, "dp", "mp"),
        P("mp", "dp"),
        P(None, "dp", "mp"),
        P("mp", "dp"),
        P("dp", "mp"),
        P("mp", "dp"),
        P(None, None, "mp", "dp"),
        P(None, None, "mp", "dp"),
        P("mp", "dp"),
    )
    out_specs = (
        P("dp", "mp", None),
        P(),
        P("dp", "mp", None),
        P("dp", "mp", None),
        P(None, ("dp", "mp")),
        P(None, ("dp", "mp")),
        P(("dp", "mp")),
        P(None, "dp", "mp"),
        P("mp", "dp"),
        P(None, "dp", "mp"),
        P("mp", "dp"),
        P("dp", "mp"),
        P("mp", "dp"),
        P(None, None, "mp", "dp"),
        P(None, None, "mp", "dp"),
        P("mp", "dp"),
    )
    return jax.shard_map(local, mesh=mesh, in_specs=in_specs, out_specs=out_specs, check_vma=False)
```
